128 devices in a mesh: comp: 2 (over z_lo), ty: 8 (over y, z_hi), tx: 8 (over x, core).
Axes of the slice: x: 4, y: 4, z: 4 (z_hi: 2, z_lo: 2; z = z_hi * 2 + z_lo), core: 2. Of those that a mesh axis runs over, the one named last changes fastest.
Arguments:
- atm_flux: float32 [8, 2097152], P(None, ('comp', 'ty', 'tx')), may hold values from -6 to 6
- margin_source: int32 [32768, 128], P(('comp', 'ty', 'tx')), may hold values from 0 to 127
- margin_cell: int32 [32768, 128], P(('comp', 'ty', 'tx')), may hold values from 0 to 65535, as said below
- margin_weight: float32 [32768, 128], P(('comp', 'ty', 'tx')), may hold values from 0 to 1
- margin_tile: int32 [32768, 1], P(('comp', 'ty', 'tx')), may hold values from 0 to 127; in each aligned block of 256 rows (0 to 255, 256 to 511, ...) at most 4 rows name the same one
- land_mask: int32 [1024, 8192], P(('comp', 'ty'), 'tx'), may hold values 0 or 1
- sea_depth: float32 [1024, 8192], P(('comp', 'ty'), 'tx'), may hold values from 0.5 to 1.8
- sea_height: float32 [1024, 8192], P(('comp', 'ty'), 'tx'), may hold values from -3 to 3
- transport: float32 [2, 1024, 8192], P(None, ('comp', 'ty'), 'tx'), may hold values from -3 to 3
- tracers: float32 [2, 16, 1024, 8192], P(None, None, ('comp', 'ty'), 'tx'), may hold values from -6 to 6
Outputs:
- new_height: float32 [1024, 8192], P(('comp', 'ty'), 'tx')
- new_transport: float32 [2, 1024, 8192], P(None, ('comp', 'ty'), 'tx')
- new_tracers: float32 [2, 16, 1024, 8192], P(None, None, ('comp', 'ty'), 'tx')
The draws below stay inside these ranges and needn't reach their ends.
Inputs may be any that keep to these rules, and one draw needn't show every extreme that they name: `margin_tile`: among the 256 blocks of one atmosphere owner (an aligned run of 256 rows), no ocean tile is named by more than 4 blocks. All entries of one block lie in one row of its tile: margin_cell[b, j] // 1024 is the same for every j.
All inputs are finite; a program needn't handle non-finite values. No bound on the sum of `land_mask` on one device may be relied on, other than what follows from the above.
Results may differ from the reference program's by a relative error of at most 0.000088.
Values sent between devices are 32-bit elements; how exact they have to be, the bound alone decides.
No kernel may reach another device: no remote copies, remote signals or barrier semaphores. Data moves between devices by JAX's collectives and lax.ppermute only.
A program may use at most 192 MiB of HBM per device.

```python
import math
import jax
import jax.numpy as jnp
import numpy as np
from jax import lax

NFLUX = 8
LEV = 16
SUB = 3
BW = 128
CY = 64
CX = 1024
BLK_DEV = 256
ACOL_DEV = 16384
CAP = 4
TCOLS = 8
NY = 1024
NX = 8192
NBT = 32768
ACOLS = 2097152
DEVICES = 128


def draw_margin_cell(key, part):
    row_key = jax.random.fold_in(key, 11)
    col_key = jax.random.fold_in(key, 12)
    rows = jax.random.randint(row_key, (NBT, 1), 0, CY)
    cols = jax.random.randint(col_key, (NBT, BW), 0, CX)
    return (rows * CX + cols).astype(jnp.int32)


def place_ends(values, own_key, low, largest):
    index_at = [jax.random.randint(jax.random.fold_in(own_key, axis), (), 0, length) for axis, length in enumerate(values.shape)]
    main_axis = values.shape.index(max(values.shape))
    beside = index_at[:main_axis] + [(index_at[main_axis] + 1) % values.shape[main_axis]] + index_at[main_axis + 1:]
    return values.at[tuple(index_at)].set(low).at[tuple(beside)].set(largest)


def block_scale(stream_key, dims, split, least, top_value):
    gain, own = 1.0, jax.random.fold_in(stream_key, 6)
    for dim, parts in split:
        draws = jnp.exp(jax.random.uniform(jax.random.fold_in(own, dim), (parts,), jnp.float32, least / len(split), top_value / len(split)))
        gain = gain * jnp.repeat(draws, dims[dim] // parts).reshape([-1 if axis == dim else 1 for axis in range(len(dims))])
    return gain


def deal_out(rng, own, number, rows, number_of, top, limit, lean):
    ranking = jax.random.permutation(rng, number_of)
    crowded, usual = shares(number_of, rows * top, limit, lean, True), shares(number_of, rows * top, limit, lean, False)
    places = jnp.arange(number_of)

    def named(tallies, offset_by):
        used = int((tallies > 0).sum())
        fixed = max(1, used // 4)
        passed = fixed + (places - fixed + offset_by * (used - fixed)) % max(1, number_of - fixed)
        return jnp.zeros((number_of,), jnp.int32).at[ranking[jnp.where(places < fixed, places, passed)]].set(jnp.asarray(tallies, jnp.int32))

    tallies = jnp.where(number % 4 == 0, named(crowded, number // 4), named(usual, number - number // 4 - 1))
    mixed = jax.random.permutation(jax.random.fold_in(own, 3), number_of)
    donor, taker = mixed[0:number_of // 2 * 2:2], mixed[1:number_of // 2 * 2:2]
    margin = jnp.minimum(tallies[donor] - 1, limit - tallies[taker]) // 2
    margin = jnp.where((donor == ranking[0]) | (taker == ranking[0]) | (tallies[taker] == 0), 0, jnp.maximum(margin, 0))
    passed = jax.random.randint(jax.random.fold_in(own, 4), (number_of // 2,), 0, 1 << 20) % (margin + 1)
    tallies = tallies.at[donor].add(-passed).at[taker].add(passed)
    labels = jnp.searchsorted(jnp.cumsum(tallies), jnp.arange(rows * top), side="right").astype(jnp.int32)
    table = labels.reshape(top, rows).T
    table = table[jax.random.permutation(jax.random.fold_in(own, 1), rows)]
    offset_by = jax.random.randint(jax.random.fold_in(own, 2), (rows, 1), 0, top)
    return jnp.take_along_axis(table, (jnp.arange(top)[None, :] + offset_by) % top, axis=1)


def shares(count, total, bound, slope, full):
    loads = [(1 << 20) // math.isqrt(rank ** slope) + 1 for rank in range(1, count + 1)]
    largest = bound if full else min(bound, max(-(-total // count), total * loads[0] // sum(loads)))
    least = 1 if total - largest >= count - 1 else 0
    holding, rest = [largest] + [least] * (count - 1), total - largest - least * (count - 1)
    while rest > 0:
        candidates = [i for i in range(1, count) if holding[i] < largest] or [i for i in range(1, count) if holding[i] < bound]
        mass, budget = sum([loads[i] for i in candidates]), rest
        for i in candidates:
            more = min(bound - holding[i], max(1, budget * loads[i] // mass), rest)
            holding[i] = holding[i] + more
            rest = rest - more
    return np.array(holding)


def scatter_about(rng, dims, scale, reach, cuts=(), held_as=jnp.bfloat16):
    entries = jax.random.normal(rng, dims, jnp.float32) * scale
    if len(cuts) > 0:
        entries = block_scale(rng, dims, cuts, -0.22, 0.18) * entries
    return jnp.clip(entries, min=-reach, max=reach).astype(held_as)


def setup_inputs(seed: int = 0) -> dict:
    splits = jax.random.split(jax.random.key(seed), 11)
    atm_flux = scatter_about(splits[0], (NFLUX, ACOLS), 1.0, 6.0, ((1, 128),), jnp.float32)
    margin_source = place_ends(jax.random.randint(splits[1], (NBT, BW), 0, BW), jax.random.fold_in(splits[1], 1), 0, BW - 1).astype(jnp.int32)
    margin_cell = draw_margin_cell(jax.random.fold_in(splits[10], 71), 0)
    margin_weight = jnp.clip(1.0 * jax.random.uniform(splits[3], (NBT, BW), jnp.float32) ** block_scale(splits[3], (NBT, BW), ((0, 128),), -0.2, 0.2), 0.0, 1.0)
    margin_tile_keys = jax.random.split(jax.random.fold_in(splits[4], 1), NBT // BLK_DEV)
    margin_tile_turns = jax.random.permutation(jax.random.fold_in(splits[4], 3), NBT // BLK_DEV)
    margin_tile = jax.vmap(lambda own, number: deal_out(jax.random.fold_in(splits[4], 2), own, number, BLK_DEV, DEVICES, 1, CAP, 2))(margin_tile_keys, margin_tile_turns).reshape((NBT, 1))
    land_mask = place_ends((jax.random.randint(splits[5], (NY, NX), 0, 4) < 3).astype(jnp.int32), jax.random.fold_in(splits[5], 1), 0, 1)
    sea_depth = jnp.clip(jnp.exp(math.log(1.8) - 1.2809338 * jax.random.uniform(splits[6], (NY, NX), jnp.float32) ** block_scale(splits[6], (NY, NX), ((0, 16), (1, 8)), -0.2, 0.2)), 0.5, 1.8)
    sea_height = scatter_about(splits[7], (NY, NX), 0.5, 3.0, ((0, 16), (1, 8)), jnp.float32)
    transport = scatter_about(splits[8], (2, NY, NX), 0.5, 3.0, ((1, 16), (2, 8)), jnp.float32)
    tracers = scatter_about(splits[9], (2, LEV, NY, NX), 1.0, 6.0, ((2, 16), (3, 8)), jnp.float32)
    return dict(atm_flux=atm_flux, margin_source=margin_source, margin_cell=margin_cell, margin_weight=margin_weight, margin_tile=margin_tile, land_mask=land_mask, sea_depth=sea_depth, sea_height=sea_height, transport=transport, tracers=tracers)


damping = 0.95
advect = 0.15
diffuse = 0.1


def four_sides(padded):
    eastern = padded[..., 1:-1, 2:]
    western = padded[..., 1:-1, :-2]
    northern = padded[..., 2:, 1:-1]
    southern = padded[..., :-2, 1:-1]
    return eastern, western, northern, southern


def zero_sides(values):
    padding = [(0, 0)] * (values.ndim - 2) + [(1, 1), (1, 1)]
    return four_sides(jnp.pad(values, padding))


def momentum(pressure_sides, along_flow, across, ocean_mask, bottom, wind_x, wind_y):
    eastern, western, northern, southern = pressure_sides
    along_flow = ocean_mask * (damping * along_flow + (-0.5 * bottom * (eastern - western) + wind_x))
    across = ocean_mask * (damping * across + (-0.5 * bottom * (northern - southern) + wind_y))
    return along_flow, across


def continuity(height, along_sides, across_sides, ocean_mask, source):
    divergence = along_sides[0] - along_sides[1] + across_sides[2] - across_sides[3]
    return ocean_mask * (height - 0.5 * divergence + source)


def barotropic(height, along_flow, across, ocean_mask, bottom, pressure_term, wind_x, wind_y, source, count):
    for k in range(count):
        pressure = ocean_mask * (height + pressure_term)
        along_flow, across = momentum(zero_sides(pressure), along_flow, across, ocean_mask, bottom, wind_x, wind_y)
        height = continuity(height, zero_sides(along_flow), zero_sides(across), ocean_mask, source)
    return height, along_flow, across


def horizontal(tracer_sides, mask_sides, tracers, transport, bottom):
    eastern, western, northern, southern = [
        edge_mask * near_value + (1.0 - edge_mask) * tracers
        for near_value, edge_mask in zip(tracer_sides, mask_sides)]
    east_speed = transport[0] / bottom
    north_speed = transport[1] / bottom
    carried = (jnp.maximum(east_speed, 0.0) * (tracers - western)
               + jnp.minimum(east_speed, 0.0) * (eastern - tracers)
               + jnp.maximum(north_speed, 0.0) * (tracers - southern)
               + jnp.minimum(north_speed, 0.0) * (northern - tracers))
    spread = eastern + western + northern + southern - 4.0 * tracers
    return tracers - advect * carried + diffuse * spread


def column_solve(heated, mixing):
    levels = heated.shape[1]
    nothing = jnp.zeros_like(mixing[0])
    ratios = []
    values = []
    last_ratio = nothing
    last_value = heated[:, 0]
    for k in range(levels):
        upper_mix = mixing[k] if k < levels - 1 else nothing
        lower_mix = mixing[k - 1] if k > 0 else nothing
        pivot_term = 1.0 + upper_mix + lower_mix
        right_side = heated[:, k]
        if k > 0:
            pivot_term = pivot_term + lower_mix * last_ratio
            right_side = right_side + lower_mix * last_value
        last_ratio = -upper_mix / pivot_term
        last_value = right_side / pivot_term
        ratios.append(last_ratio)
        values.append(last_value)
    result = [values[levels - 1]]
    for k in range(levels - 2, -1, -1):
        result.append(values[k] - ratios[k] * result[-1])
    return jnp.stack(result[::-1], axis=1)


def surface_and_mixing(moved, forcing):
    levels = moved.shape[1]
    depths = jnp.arange(levels, dtype=jnp.float32)
    absorb = jnp.exp(-depths / 3.0) - jnp.exp(-(depths + 1.0) / 3.0)
    heat = 0.5 * forcing[4][None] * absorb[:, None, None]
    heat = heat.at[0].add(0.5 * forcing[3])
    salt = jnp.zeros_like(heat).at[0].set(0.5 * forcing[5] - 0.3 * forcing[6])
    heated = moved + jnp.stack([heat, salt])
    mixing = 0.2 + 0.5 * (forcing[7] * forcing[7])[None] * jnp.exp(-depths[:-1] / 2.0)[:, None, None]
    return column_solve(heated, mixing)


def remap_fluxes(atm_flux, margin_source, margin_cell, margin_weight, margin_tile):
    block_ids = jnp.arange(margin_source.shape[0], dtype=jnp.int32)
    owner_device = block_ids // BLK_DEV
    window_start = ((block_ids % BLK_DEV) // 2) * BW
    columns = (owner_device * ACOL_DEV + window_start)[:, None] + margin_source
    target_tile = margin_tile[:, 0]
    row_index = (target_tile // TCOLS)[:, None] * CY + margin_cell // CX
    col_index = (target_tile % TCOLS)[:, None] * CX + margin_cell % CX
    places = (row_index * NX + col_index).reshape(-1)

    def spread_field(values):
        weighted = (values[columns] * margin_weight).reshape(-1)
        return jnp.zeros((NY * NX,), jnp.float32).at[places].add(weighted)

    return lax.map(spread_field, atm_flux).reshape(atm_flux.shape[0], NY, NX)


def reference(atm_flux, margin_source, margin_cell, margin_weight, margin_tile, land_mask, sea_depth, sea_height, transport, tracers):
    ocean_mask = land_mask.astype(jnp.float32)
    forcing = remap_fluxes(atm_flux, margin_source, margin_cell, margin_weight, margin_tile)
    pressure_term = 0.5 * forcing[2]
    wind_x = 0.5 * forcing[0]
    wind_y = 0.5 * forcing[1]
    source = 0.1 * (forcing[6] - forcing[5])
    height, along_flow, across = barotropic(sea_height, transport[0], transport[1], ocean_mask, sea_depth,
                                            pressure_term, wind_x, wind_y, source, SUB)
    moved = horizontal(zero_sides(tracers), zero_sides(ocean_mask), tracers, transport, sea_depth)
    solved = surface_and_mixing(moved, forcing)
    new_tracers = ocean_mask * solved + (1.0 - ocean_mask) * tracers
    return height, jnp.stack([along_flow, across]), new_tracers
```

```python
import functools

import jax
import jax.numpy as jnp
import numpy as np
from jax import lax
from jax.experimental import pallas as pl
from jax.experimental.pallas import tpu as pltpu
from jax.sharding import PartitionSpec as P

SUB = 3
EDGE = 8
LANES = 128
EVERY = ("comp", "ty", "tx")
ROWS = ("comp", "ty")
f32 = jnp.float32
i32 = jnp.int32
VM = pl.BlockSpec(memory_space=pltpu.VMEM)
SM = pl.BlockSpec(memory_space=pltpu.SMEM)


def params(mib):
    return pltpu.CompilerParams(vmem_limit_bytes=mib << 20)


def pack_kernel(tile_ref, flux_ref, source_ref, cell_ref, weight_ref, first_ref, second_ref, count_ref):
    blocks = source_ref.shape[0]
    tiles = first_ref.shape[0]
    group = 4
    first_ref[...] = jnp.zeros_like(first_ref)
    second_ref[...] = jnp.zeros_like(second_ref)

    def clear(t, carry):
        count_ref[t] = 0
        return carry

    lax.fori_loop(0, tiles, clear, 0)
    sub = lax.broadcasted_iota(i32, (8, LANES), 0)

    def step(i, carry):
        for g in range(group):
            w = i * group + g
            x = flux_ref[:, pl.ds(pl.multiple_of(w * LANES, LANES), LANES)]
            after = pltpu.roll(x, 1, 0)
            six = pltpu.roll(x, 5, 0)
            five = pltpu.roll(x, 6, 0)
            y = jnp.where((sub == 4) | (sub == 5), after, x)
            y = jnp.where(sub == 6, 0.5 * after - 0.3 * x, y)
            y = jnp.where(sub == 3, 0.1 * (six - five), y)
            for half in range(2):
                b = 2 * w + half
                tile = tile_ref[b]
                slot = count_ref[tile]
                count_ref[tile] = slot + 1
                index = jnp.broadcast_to(source_ref[pl.ds(b, 1), :], (8, LANES))
                picked = jnp.take_along_axis(y, index, axis=1)
                value = picked * jnp.broadcast_to(weight_ref[pl.ds(b, 1), :], (8, LANES))
                first_ref[tile, slot] = value[0:4]
                second_ref[tile, slot] = value[4:8]
                first_ref[tile, 4, pl.ds(slot, 1), :] = cell_ref[pl.ds(b, 1), :].astype(f32)
        return carry

    lax.fori_loop(0, blocks // (2 * group), step, 0)


def pack(tile, flux, source, cell, weight, tiles):
    return pl.pallas_call(
        pack_kernel,
        name="pack_margin",
        in_specs=[SM, VM, VM, VM, VM],
        out_specs=[VM, VM],
        out_shape=[
            jax.ShapeDtypeStruct((tiles, 5, 4, LANES), f32),
            jax.ShapeDtypeStruct((tiles, 4, 4, LANES), f32),
        ],
        scratch_shapes=[pltpu.SMEM((tiles,), i32)],
        compiler_params=params(24),
        cost_estimate=pl.CostEstimate(flops=1 << 22, bytes_accessed=4 << 20, transcendentals=0),
    )(tile, flux, source, cell, weight)


def spread_kernel(cells_ref, value_ref, out_ref, acc_ref, *, group):
    sources = value_ref.shape[0]
    rows = out_ref.shape[1]
    columns = out_ref.shape[2]
    high = columns // LANES
    depth = 4 * high
    acc_ref[...] = jnp.zeros_like(acc_ref)
    sub_high = lax.broadcasted_iota(i32, (high, LANES), 0)
    sub_low = lax.broadcasted_iota(i32, (LANES, LANES), 0)
    blank = jnp.zeros((LANES, LANES), jnp.bfloat16)

    def step(i, carry):
        for g in range(group):
            s = i * group + g
            cells = cells_ref[s, 4].astype(i32)
            highs = (cells & (columns - 1)) >> 7
            lows = cells & (LANES - 1)
            for pair in range(2):
                left = []
                right = []
                for k in (2 * pair, 2 * pair + 1):
                    value = value_ref[s, k]
                    coarse = value.astype(jnp.bfloat16).astype(f32)
                    fine = value - coarse
                    hit = jnp.broadcast_to(highs[k : k + 1], (high, LANES)) == sub_high
                    parts = [
                        jnp.where(hit, jnp.broadcast_to(piece[f : f + 1], (high, LANES)), 0.0)
                        for piece in (coarse, fine)
                        for f in range(4)
                    ]
                    left.append(jnp.concatenate(parts, axis=0).astype(jnp.bfloat16))
                    one = jnp.where(jnp.broadcast_to(lows[k : k + 1], (LANES, LANES)) == sub_low, 1.0, 0.0)
                    right.append(one.astype(jnp.bfloat16))
                lhs = jnp.concatenate(left, axis=1)
                rhs = jnp.concatenate(
                    [
                        jnp.concatenate([right[0], blank], axis=1),
                        jnp.concatenate([blank, right[1]], axis=1),
                    ],
                    axis=0,
                )
                both = lax.dot_general(lhs, rhs, (((1,), (1,)), ((), ())), preferred_element_type=f32)
                both = both[:depth] + both[depth:]
                for n in range(2):
                    k = 2 * pair + n
                    row = cells[k, 0] // columns
                    place = pl.ds(pl.multiple_of(row * depth, depth), depth)
                    acc_ref[place, :] += both[:, n * LANES : (n + 1) * LANES]
        return carry

    lax.fori_loop(0, sources // group, step, 0)
    for f in range(4):
        for h in range(high):
            for r in range(0, rows, 8):
                out_ref[f, r : r + 8, h * LANES : (h + 1) * LANES] = acc_ref[
                    pl.ds(r * depth + f * high + h, 8, stride=depth), :
                ]


def spread(cells, values, rows, columns, name):
    depth = 4 * columns // LANES
    group = 8 if values.shape[0] % 8 == 0 else 1
    return pl.pallas_call(
        functools.partial(spread_kernel, group=group),
        name=name,
        in_specs=[VM, VM],
        out_specs=VM,
        out_shape=jax.ShapeDtypeStruct((4, rows, columns), f32),
        scratch_shapes=[pltpu.VMEM((rows * depth, LANES), f32)],
        compiler_params=params(24),
        cost_estimate=pl.CostEstimate(flops=1 << 30, bytes_accessed=4 << 20, transcendentals=0),
    )(cells, values)


def edges_kernel(low_ref, high_ref, west_ref, east_ref, south_ref, north_ref, columns_ref):
    levels = low_ref.shape[0]
    rows = west_ref.shape[1]
    lane = lax.broadcasted_iota(i32, (rows, LANES), 1)
    lasts = jnp.zeros((rows, LANES), f32)
    firsts = jnp.zeros((rows, LANES), f32)
    for p in range(levels):
        south_ref[p : p + 1, :] = low_ref[p, 0:1, :]
        north_ref[p : p + 1, :] = high_ref[p, EDGE - 1 : EDGE, :]
        firsts = jnp.where(lane == p, west_ref[p, :, 0:1], firsts)
        lasts = jnp.where(lane == p, east_ref[p, :, LANES - 1 : LANES], lasts)
    columns_ref[0] = firsts
    columns_ref[1] = lasts


def edges(planes):
    levels, rows, columns = planes.shape
    last_row = rows // EDGE - 1
    last_lane = columns // LANES - 1
    return pl.pallas_call(
        edges_kernel,
        name="tracer_edges",
        grid=(1,),
        in_specs=[
            pl.BlockSpec((levels, EDGE, columns), lambda i: (0, 0, 0)),
            pl.BlockSpec((levels, EDGE, columns), lambda i: (0, last_row, 0)),
            pl.BlockSpec((levels, rows, LANES), lambda i: (0, 0, 0)),
            pl.BlockSpec((levels, rows, LANES), lambda i: (0, 0, last_lane)),
        ],
        out_specs=[
            pl.BlockSpec((levels, columns), lambda i: (0, 0)),
            pl.BlockSpec((levels, columns), lambda i: (0, 0)),
            pl.BlockSpec((2, rows, LANES), lambda i: (0, 0, 0)),
        ],
        out_shape=[
            jax.ShapeDtypeStruct((levels, columns), f32),
            jax.ShapeDtypeStruct((levels, columns), f32),
            jax.ShapeDtypeStruct((2, rows, LANES), f32),
        ],
        compiler_params=params(24),
        cost_estimate=pl.CostEstimate(flops=1 << 20, bytes_accessed=4 << 20, transcendentals=0),
    )(planes, planes, planes, planes)


def beside(array, amount, axis):
    return pltpu.roll(array, amount % array.shape[axis], axis)


def move_kernel(south_ref, north_ref, sides_ref, fixed_ref, side_fixed_ref, planes_ref, out_ref, coef_ref, *, per):
    step = pl.program_id(0)
    rows = planes_ref.shape[1]
    columns = planes_ref.shape[2]

    @pl.when(step == 0)
    def _():
        middle = slice(EDGE, EDGE + rows)
        mask = fixed_ref[0, middle, :]
        lane = lax.broadcasted_iota(i32, (rows, columns), 1)
        beyond = side_fixed_ref[0, middle, :]
        east = jnp.where(lane == columns - 1, beyond[:, 0:1], beside(mask, -1, 1))
        west = jnp.where(lane == 0, beyond[:, LANES - 1 : LANES], beside(mask, 1, 1))
        tall = fixed_ref[0]
        north = beside(tall, -1, 0)[middle]
        south = beside(tall, 1, 0)[middle]
        depth = fixed_ref[1, middle, :]
        u = fixed_ref[3, middle, :] / depth
        v = fixed_ref[4, middle, :] / depth
        east = mask * east * (0.1 - 0.15 * jnp.minimum(u, 0.0))
        west = mask * west * (0.1 + 0.15 * jnp.maximum(u, 0.0))
        north = mask * north * (0.1 - 0.15 * jnp.minimum(v, 0.0))
        south = mask * south * (0.1 + 0.15 * jnp.maximum(v, 0.0))
        coef_ref[0] = 1.0 - (east + west + north + south)
        coef_ref[1] = east
        coef_ref[2] = west
        coef_ref[3] = north
        coef_ref[4] = south

    lane_side = lax.broadcasted_iota(i32, (rows, LANES), 1)
    for n in range(per):
        p = step * per + n
        chosen = lane_side == p
        first = jnp.sum(jnp.where(chosen, sides_ref[0], 0.0), axis=1, keepdims=True)
        last = jnp.sum(jnp.where(chosen, sides_ref[1], 0.0), axis=1, keepdims=True)
        south_row = south_ref[pl.ds(p, 1), :]
        north_row = north_ref[pl.ds(p, 1), :]
        for r in range(0, rows, 8):
            span = slice(r, r + 8)
            q = planes_ref[n, span, :]
            lane = lax.broadcasted_iota(i32, (8, columns), 1)
            sub = lax.broadcasted_iota(i32, (8, columns), 0)
            east = jnp.where(lane == columns - 1, first[span], beside(q, -1, 1))
            west = jnp.where(lane == 0, last[span], beside(q, 1, 1))
            below = south_row if r == 0 else planes_ref[n, r - 1 : r, :]
            above = north_row if r + 8 == rows else planes_ref[n, r + 8 : r + 9, :]
            north = jnp.where(sub == 7, above, beside(q, -1, 0))
            south = jnp.where(sub == 0, below, beside(q, 1, 0))
            out_ref[n, span, :] = (
                coef_ref[0, span, :] * q
                + coef_ref[1, span, :] * east
                + coef_ref[2, span, :] * west
                + coef_ref[3, span, :] * north
                + coef_ref[4, span, :] * south
            )


def move(south, north, sides, fixed, side_fixed, planes):
    levels, rows, columns = planes.shape
    per = 4
    whole = lambda a: pl.BlockSpec(a.shape, lambda i: (0,) * a.ndim)
    return pl.pallas_call(
        functools.partial(move_kernel, per=per),
        name="tracer_move",
        grid=(levels // per,),
        in_specs=[
            whole(south),
            whole(north),
            whole(sides),
            whole(fixed),
            whole(side_fixed),
            pl.BlockSpec((per, rows, columns), lambda i: (i, 0, 0)),
        ],
        out_specs=pl.BlockSpec((per, rows, columns), lambda i: (i, 0, 0)),
        out_shape=jax.ShapeDtypeStruct(planes.shape, f32),
        scratch_shapes=[pltpu.VMEM((5, rows, columns), f32)],
        compiler_params=params(32),
        cost_estimate=pl.CostEstimate(flops=1 << 25, bytes_accessed=18 << 20, transcendentals=0),
    )(south, north, sides, fixed, side_fixed, planes)


def solve_kernel(flux_ref, mask_ref, moved_ref, out_ref, ratio_ref, *, absorb, decay):
    levels = moved_ref.shape[1]
    mask = mask_ref[...]
    heat_top = 0.5 * mask * flux_ref[0]
    sun = 0.5 * mask * flux_ref[1]
    salt_top = mask * flux_ref[2]
    stir = flux_ref[3]
    base = 0.2 * mask
    stir = 0.5 * mask * (stir * stir)
    above = jnp.zeros_like(mask)
    link = jnp.zeros_like(mask)
    heat_last = None
    salt_last = None
    for k in range(levels):
        heat = moved_ref[0, k] + absorb[k] * sun
        salt = moved_ref[1, k]
        if k == 0:
            heat = heat + heat_top
            salt = salt + salt_top
        below = base + decay[k] * stir if k < levels - 1 else jnp.zeros_like(mask)
        pivot = 1.0 + below + above
        if k > 0:
            pivot = pivot + above * link
            heat = heat + above * heat_last
            salt = salt + above * salt_last
        inverse = 1.0 / pivot
        link = -below * inverse
        heat_last = heat * inverse
        salt_last = salt * inverse
        above = below
        if k < levels - 1:
            ratio_ref[k] = link
        out_ref[0, k] = heat_last
        out_ref[1, k] = salt_last
    for k in range(levels - 2, -1, -1):
        link = ratio_ref[k]
        heat_last = out_ref[0, k] - link * heat_last
        salt_last = out_ref[1, k] - link * salt_last
        out_ref[0, k] = heat_last
        out_ref[1, k] = salt_last


def solve(flux, mask, moved):
    count, levels, rows, columns = moved.shape
    depths = np.arange(levels, dtype=np.float64)
    absorb = tuple(float(a) for a in np.exp(-depths / 3.0) - np.exp(-(depths + 1.0) / 3.0))
    decay = tuple(float(a) for a in np.exp(-depths / 2.0))
    return pl.pallas_call(
        functools.partial(solve_kernel, absorb=absorb, decay=decay),
        name="column_solve",
        grid=(rows // 8,),
        in_specs=[
            pl.BlockSpec((4, 8, columns), lambda i: (0, i, 0)),
            pl.BlockSpec((8, columns), lambda i: (i, 0)),
            pl.BlockSpec((count, levels, 8, columns), lambda i: (0, 0, i, 0)),
        ],
        out_specs=pl.BlockSpec((count, levels, 8, columns), lambda i: (0, 0, i, 0)),
        out_shape=jax.ShapeDtypeStruct(moved.shape, f32),
        scratch_shapes=[pltpu.VMEM((levels, 8, columns), f32)],
        compiler_params=params(16),
        cost_estimate=pl.CostEstimate(flops=1 << 25, bytes_accessed=18 << 20, transcendentals=0),
    )(flux, mask, moved)


def barotropic_kernel(fixed_ref, fixed_side_ref, flux_ref, flux_side_ref, height_ref, flow_ref, wide_ref):
    rows = height_ref.shape[0]
    columns = height_ref.shape[1]
    wide_ref[0:5, :, :columns] = fixed_ref[...]
    wide_ref[0:5, :, columns:] = fixed_side_ref[...]
    wide_ref[5:9, :, :columns] = flux_ref[...]
    wide_ref[5:9, :, columns:] = flux_side_ref[...]
    mask = wide_ref[0]
    drag = -0.5 * wide_ref[1]
    height = wide_ref[2]
    along = wide_ref[3]
    across = wide_ref[4]
    wind_x = 0.5 * wide_ref[5]
    wind_y = 0.5 * wide_ref[6]
    push = 0.5 * wide_ref[7]
    source = wide_ref[8]
    for k in range(SUB):
        level = mask * (height + push)
        along = mask * (0.95 * along + drag * (beside(level, -1, 1) - beside(level, 1, 1)) + wind_x)
        across = mask * (0.95 * across + drag * (beside(level, -1, 0) - beside(level, 1, 0)) + wind_y)
        spread_out = beside(along, -1, 1) - beside(along, 1, 1) + beside(across, -1, 0) - beside(across, 1, 0)
        height = mask * (height - 0.5 * spread_out + source)
    middle = slice(EDGE, EDGE + rows)
    height_ref[...] = height[middle, :columns]
    flow_ref[0] = along[middle, :columns]
    flow_ref[1] = across[middle, :columns]


def barotropic(fixed, fixed_side, flux, flux_side):
    _, tall, columns = fixed.shape
    rows = tall - 2 * EDGE
    return pl.pallas_call(
        barotropic_kernel,
        name="barotropic",
        in_specs=[VM] * 4,
        out_specs=[VM, VM],
        out_shape=[
            jax.ShapeDtypeStruct((rows, columns), f32),
            jax.ShapeDtypeStruct((2, rows, columns), f32),
        ],
        scratch_shapes=[pltpu.VMEM((9, tall, columns + LANES), f32)],
        compiler_params=params(24),
        cost_estimate=pl.CostEstimate(flops=1 << 24, bytes_accessed=6 << 20, transcendentals=0),
    )(fixed, fixed_side, flux, flux_side)


def to_next(array, axes):
    ends = lax.axis_size(axes) - 1
    return lax.ppermute(array, axes, [(i, i + 1) for i in range(ends)])


def to_previous(array, axes):
    ends = lax.axis_size(axes) - 1
    return lax.ppermute(array, axes, [(i + 1, i) for i in range(ends)])


def merge_sides(from_west, from_east):
    lane = lax.broadcasted_iota(i32, from_west.shape, from_west.ndim - 1)
    return jnp.where(lane < LANES // 2, from_east, from_west)


def all_to_all(array):
    return lax.all_to_all(array, EVERY, split_axis=0, concat_axis=0, tiled=True)


def local(
    atm_flux,
    margin_source,
    margin_cell,
    margin_weight,
    margin_tile,
    land_mask,
    sea_depth,
    sea_height,
    transport,
    tracers,
):
    tiles = lax.axis_size(EVERY)
    count, levels, rows, columns = tracers.shape
    first, second = pack(margin_tile.reshape(-1), atm_flux, margin_source, margin_cell, margin_weight, tiles)
    first = all_to_all(first)
    second = all_to_all(second)

    mask = land_mask.astype(f32)
    planes = tracers.reshape(count * levels, rows, columns)
    tracer_south, tracer_north, tracer_sides = edges(planes)
    fixed = jnp.concatenate([jnp.stack([mask, sea_depth, sea_height]), transport], axis=0)
    tops = fixed[:, rows - EDGE :].reshape(5 * EDGE, columns)
    bottoms = fixed[:, :EDGE].reshape(5 * EDGE, columns)
    from_south = to_next(jnp.concatenate([tracer_north, tops], axis=0), ROWS)
    from_north = to_previous(jnp.concatenate([tracer_south, bottoms], axis=0), ROWS)
    wide = count * levels
    fixed = jnp.concatenate(
        [
            from_south[wide:].reshape(5, EDGE, columns),
            fixed,
            from_north[wide:].reshape(5, EDGE, columns),
        ],
        axis=1,
    )
    tall = rows + 2 * EDGE
    east_edge = jnp.concatenate([fixed[:, :, -LANES:].reshape(5 * tall, LANES), tracer_sides[1]], axis=0)
    west_edge = jnp.concatenate([fixed[:, :, :LANES].reshape(5 * tall, LANES), tracer_sides[0]], axis=0)
    from_west = to_next(east_edge, "tx")
    from_east = to_previous(west_edge, "tx")
    fixed_side = merge_sides(from_west[: 5 * tall], from_east[: 5 * tall]).reshape(5, tall, LANES)
    sides = jnp.stack([from_east[5 * tall :], from_west[5 * tall :]])
    moved = move(from_south[:wide], from_north[:wide], sides, fixed, fixed_side, planes)

    winds = spread(first, first, rows, columns, "spread_first")
    flux_south = to_next(winds[:, rows - EDGE :], ROWS)
    flux_north = to_previous(winds[:, :EDGE], ROWS)
    winds = jnp.concatenate([flux_south, winds, flux_north], axis=1)
    flux_west = to_next(winds[:, :, -LANES:], "tx")
    flux_east = to_previous(winds[:, :, :LANES], "tx")
    winds_side = merge_sides(flux_west, flux_east)

    heats = spread(first, second, rows, columns, "spread_second")
    solved = solve(heats, mask, moved.reshape(tracers.shape))
    new_height, new_transport = barotropic(fixed, fixed_side, winds, winds_side)
    return new_height, new_transport, solved


def solution(mesh):
    in_specs = (
        P(None, EVERY),
        P(EVERY, None),
        P(EVERY, None),
        P(EVERY, None),
        P(EVERY, None),
        P(ROWS, "tx"),
        P(ROWS, "tx"),
        P(ROWS, "tx"),
        P(None, ROWS, "tx"),
        P(None, None, ROWS, "tx"),
    )
    out_specs = (P(ROWS, "tx"), P(None, ROWS, "tx"), P(None, None, ROWS, "tx"))
    return jax.shard_map(local, mesh=mesh, in_specs=in_specs, out_specs=out_specs, check_vma=False)
```

```python
import functools

import jax
import jax.numpy as jnp
import numpy as np
from jax import lax
from jax.experimental import pallas as pl
from jax.experimental.pallas import tpu as pltpu
from jax.sharding import PartitionSpec as P

SUB = 3
EDGE = 8
LANES = 128
EVERY = ("comp", "ty", "tx")
ROWS = ("comp", "ty")
f32 = jnp.float32
i32 = jnp.int32
VM = pl.BlockSpec(memory_space=pltpu.VMEM)
SM = pl.BlockSpec(memory_space=pltpu.SMEM)


def params(mib):
    return pltpu.CompilerParams(vmem_limit_bytes=mib << 20)


def whole(array):
    return pl.BlockSpec(array.shape, lambda i: (0,) * array.ndim)


def pack_kernel(tile_ref, flux_ref, source_ref, cell_ref, weight_ref, out_ref, count_ref, *, beyond):
    blocks = source_ref.shape[0]
    tiles = out_ref.shape[0]
    group = 4
    nowhere = jnp.full((4, LANES), beyond, f32)

    def clear(t, carry):
        count_ref[t] = 0
        out_ref[t, 8] = nowhere
        return carry

    lax.fori_loop(0, tiles, clear, 0, unroll=True)
    sub = lax.broadcasted_iota(i32, (8, LANES), 0)

    def step(i, carry):
        for g in range(group):
            w = i * group + g
            x = flux_ref[:, pl.ds(pl.multiple_of(w * LANES, LANES), LANES)]
            after = pltpu.roll(x, 1, 0)
            six = pltpu.roll(x, 5, 0)
            five = pltpu.roll(x, 6, 0)
            y = jnp.where((sub == 4) | (sub == 5), after, x)
            y = jnp.where(sub == 6, 0.5 * after - 0.3 * x, y)
            y = jnp.where(sub == 3, 0.1 * (six - five), y)
            for half in range(2):
                b = 2 * w + half
                tile = tile_ref[b]
                slot = count_ref[tile]
                count_ref[tile] = slot + 1
                index = jnp.broadcast_to(source_ref[pl.ds(b, 1), :], (8, LANES))
                picked = jnp.take_along_axis(y, index, axis=1)
                value = picked * jnp.broadcast_to(weight_ref[pl.ds(b, 1), :], (8, LANES))
                out_ref[tile, slot] = value[0:4]
                out_ref[tile, 4 + slot] = value[4:8]
                out_ref[tile, 8, pl.ds(slot, 1), :] = cell_ref[pl.ds(b, 1), :].astype(f32)
        return carry

    lax.fori_loop(0, blocks // (2 * group), step, 0)


def pack(tile, flux, source, cell, weight, tiles, beyond):
    return pl.pallas_call(
        functools.partial(pack_kernel, beyond=beyond),
        name="pack_margin",
        in_specs=[SM, VM, VM, VM, VM],
        out_specs=VM,
        out_shape=jax.ShapeDtypeStruct((tiles, 9, 4, LANES), f32),
        scratch_shapes=[pltpu.SMEM((tiles,), i32)],
        compiler_params=params(24),
        cost_estimate=pl.CostEstimate(flops=1 << 22, bytes_accessed=4 << 20, transcendentals=0),
    )(tile, flux, source, cell, weight)


def spread_kernel(load_ref, winds_ref, heats_ref, south_ref, north_ref, acc_ref, *, group):
    sources = load_ref.shape[0]
    _, rows, columns = winds_ref.shape
    fields = 8
    high = columns // LANES
    depth = fields * high
    def clear(i, c):
        acc_ref[pl.ds(pl.multiple_of(i * 256, 256), 256),:] = jnp.zeros((256, LANES), f32)
        return c
    lax.fori_loop(0, rows * depth // 256, clear, 0)
    low_iota = lax.broadcasted_iota(i32, (LANES, LANES), 0).astype(f32).astype(jnp.bfloat16)
    pattern = [
        (2 * i + (lax.broadcasted_iota(i32, (16, LANES), 0) >> 3)).astype(f32).astype(jnp.bfloat16) for i in range(high // 2)
    ]
    zero16 = jnp.zeros((16, LANES), jnp.bfloat16)
    one = jnp.ones((LANES, LANES), jnp.bfloat16)
    zero = jnp.zeros((LANES, LANES), jnp.bfloat16)

    def step(i, carry):
        for g in range(group):
            s = i * group + g
            cells = load_ref[s, 8].astype(i32)
            highs = ((cells & (columns - 1)) >> 7).astype(f32)
            lows = (cells & (LANES - 1)).astype(f32)
            for k in range(4):
                value = jnp.concatenate([load_ref[s, k], load_ref[s, 4 + k]], axis=0)
                coarse = value.astype(jnp.bfloat16).astype(f32)
                fine = value - coarse
                coarse = jnp.concatenate([coarse, coarse], axis=0).astype(jnp.bfloat16)
                fine = jnp.concatenate([fine, fine], axis=0).astype(jnp.bfloat16)
                hk = jnp.broadcast_to(highs[k : k + 1], (16, LANES)).astype(jnp.bfloat16)
                lk = jnp.broadcast_to(lows[k : k + 1], (16, LANES)).astype(jnp.bfloat16)
                lk = jnp.concatenate([lk] * (LANES // 16), axis=0)
                left = []
                right = []
                for p in pattern:
                    hit = hk == p
                    left.append(jnp.where(hit, coarse, zero16))
                    right.append(jnp.where(hit, fine, zero16))
                lhs = jnp.concatenate([jnp.concatenate(left, axis=0), jnp.concatenate(right, axis=0)], axis=1)
                onehot = jnp.where(lk == low_iota, one, zero)
                rhs = jnp.concatenate([onehot, onehot], axis=1)
                both = lax.dot_general(lhs, rhs, (((1,), (1,)), ((), ())), preferred_element_type=f32)
                row = cells[k, 0] >> (columns.bit_length() - 1)
                place = pl.ds(pl.multiple_of(row * depth, depth), depth)
                acc_ref[place, :] += both
        return carry

    lax.fori_loop(0, sources // group, step, 0)

    def turn(i, carry):
        r = pl.multiple_of(i * 8, 8)
        block = acc_ref[pl.ds(pl.multiple_of(r * depth, 8 * depth), 8 * depth), :].reshape(8, depth, LANES)
        for h in range(high):
            piece = jnp.swapaxes(block[:, h * 8 : h * 8 + 8, :], 0, 1)
            for f in range(fields):
                ref = winds_ref if f < 4 else heats_ref
                ref[f % 4, pl.ds(r, 8), h * LANES : (h + 1) * LANES] = piece[f]
        return carry

    lax.fori_loop(0, rows // 8, turn, 0)
    south_ref[...] = winds_ref[:, 0:EDGE, :]
    north_ref[...] = winds_ref[:, rows - EDGE : rows, :]

def spread(load, rows, columns):
    depth = 8 * columns // LANES
    group = 8 if load.shape[0] % 8 == 0 else 1
    return pl.pallas_call(
        functools.partial(spread_kernel, group=group),
        name="spread_all",
        in_specs=[VM],
        out_specs=[VM] * 4,
        out_shape=[
            jax.ShapeDtypeStruct((4, rows, columns), f32),
            jax.ShapeDtypeStruct((4, rows, columns), f32),
            jax.ShapeDtypeStruct((4, EDGE, columns), f32),
            jax.ShapeDtypeStruct((4, EDGE, columns), f32),
        ],
        scratch_shapes=[pltpu.VMEM(((rows + 1) * depth, LANES), f32)],
        compiler_params=params(24),
        cost_estimate=pl.CostEstimate(flops=1 << 30, bytes_accessed=4 << 20, transcendentals=0),
    )(load)


def edges_kernel(low_ref, high_ref, west_ref, east_ref, south_ref, north_ref, columns_ref):
    levels = low_ref.shape[0]
    rows = west_ref.shape[1]
    lane = lax.broadcasted_iota(i32, (rows, LANES), 1)
    lasts = jnp.zeros((rows, LANES), f32)
    firsts = jnp.zeros((rows, LANES), f32)
    for p in range(levels):
        south_ref[p : p + 1, :] = low_ref[p, 0:1, :]
        north_ref[p : p + 1, :] = high_ref[p, EDGE - 1 : EDGE, :]
        firsts = jnp.where(lane == p, west_ref[p, :, 0:1], firsts)
        lasts = jnp.where(lane == p, east_ref[p, :, LANES - 1 : LANES], lasts)
    columns_ref[0] = firsts
    columns_ref[1] = lasts


def edges(planes):
    levels, rows, columns = planes.shape
    last_row = rows // EDGE - 1
    last_lane = columns // LANES - 1
    return pl.pallas_call(
        edges_kernel,
        name="tracer_edges",
        grid=(1,),
        in_specs=[
            pl.BlockSpec((levels, EDGE, columns), lambda i: (0, 0, 0)),
            pl.BlockSpec((levels, EDGE, columns), lambda i: (0, last_row, 0)),
            pl.BlockSpec((levels, rows, LANES), lambda i: (0, 0, 0)),
            pl.BlockSpec((levels, rows, LANES), lambda i: (0, 0, last_lane)),
        ],
        out_specs=[
            pl.BlockSpec((levels, columns), lambda i: (0, 0)),
            pl.BlockSpec((levels, columns), lambda i: (0, 0)),
            pl.BlockSpec((2, rows, LANES), lambda i: (0, 0, 0)),
        ],
        out_shape=[
            jax.ShapeDtypeStruct((levels, columns), f32),
            jax.ShapeDtypeStruct((levels, columns), f32),
            jax.ShapeDtypeStruct((2, rows, LANES), f32),
        ],
        compiler_params=params(56),
        cost_estimate=pl.CostEstimate(flops=1 << 20, bytes_accessed=4 << 20, transcendentals=0),
    )(planes, planes, planes, planes)


def beside(array, amount, axis):
    return pltpu.roll(array, amount % array.shape[axis], axis)


def move_kernel(south_ref, north_ref, sides_ref, fixed_ref, side_fixed_ref, planes_ref, out_ref, coef_ref, *, per):
    step = pl.program_id(0)
    rows = planes_ref.shape[1]
    columns = planes_ref.shape[2]

    @pl.when(step == 0)
    def _():
        middle = slice(EDGE, EDGE + rows)
        mask = fixed_ref[0, middle, :]
        lane = lax.broadcasted_iota(i32, (rows, columns), 1)
        beyond = side_fixed_ref[0, middle, :]
        east = jnp.where(lane == columns - 1, beyond[:, 0:1], beside(mask, -1, 1))
        west = jnp.where(lane == 0, beyond[:, LANES - 1 : LANES], beside(mask, 1, 1))
        tall = fixed_ref[0]
        north = beside(tall, -1, 0)[middle]
        south = beside(tall, 1, 0)[middle]
        depth = fixed_ref[1, middle, :]
        u = fixed_ref[3, middle, :] / depth
        v = fixed_ref[4, middle, :] / depth
        east = mask * east * (0.1 - 0.15 * jnp.minimum(u, 0.0))
        west = mask * west * (0.1 + 0.15 * jnp.maximum(u, 0.0))
        north = mask * north * (0.1 - 0.15 * jnp.minimum(v, 0.0))
        south = mask * south * (0.1 + 0.15 * jnp.maximum(v, 0.0))
        coef_ref[0] = 1.0 - (east + west + north + south)
        coef_ref[1] = east
        coef_ref[2] = west
        coef_ref[3] = north
        coef_ref[4] = south

    lane_side = lax.broadcasted_iota(i32, (rows, LANES), 1)
    for n in range(per):
        p = step * per + n
        chosen = lane_side == p
        first = jnp.sum(jnp.where(chosen, sides_ref[0], 0.0), axis=1, keepdims=True)
        last = jnp.sum(jnp.where(chosen, sides_ref[1], 0.0), axis=1, keepdims=True)
        south_row = south_ref[pl.ds(p, 1), :]
        north_row = north_ref[pl.ds(p, 1), :]
        for r in range(0, rows, 8):
            span = slice(r, r + 8)
            q = planes_ref[n, span, :]
            lane = lax.broadcasted_iota(i32, (8, columns), 1)
            sub = lax.broadcasted_iota(i32, (8, columns), 0)
            east = jnp.where(lane == columns - 1, first[span], beside(q, -1, 1))
            west = jnp.where(lane == 0, last[span], beside(q, 1, 1))
            below = south_row if r == 0 else planes_ref[n, r - 1 : r, :]
            above = north_row if r + 8 == rows else planes_ref[n, r + 8 : r + 9, :]
            north = jnp.where(sub == 7, above, beside(q, -1, 0))
            south = jnp.where(sub == 0, below, beside(q, 1, 0))
            out_ref[n, span, :] = (
                coef_ref[0, span, :] * q
                + coef_ref[1, span, :] * east
                + coef_ref[2, span, :] * west
                + coef_ref[3, span, :] * north
                + coef_ref[4, span, :] * south
            )


def move(south, north, sides, fixed, side_fixed, planes):
    levels, rows, columns = planes.shape
    per = 4
    return pl.pallas_call(
        functools.partial(move_kernel, per=per),
        name="tracer_move",
        grid=(levels // per,),
        in_specs=[
            whole(south),
            whole(north),
            whole(sides),
            whole(fixed),
            whole(side_fixed),
            pl.BlockSpec((per, rows, columns), lambda i: (i, 0, 0)),
        ],
        out_specs=pl.BlockSpec((per, rows, columns), lambda i: (i, 0, 0)),
        out_shape=jax.ShapeDtypeStruct(planes.shape, f32),
        scratch_shapes=[pltpu.VMEM((5, rows, columns), f32)],
        compiler_params=params(56),
        cost_estimate=pl.CostEstimate(flops=1 << 25, bytes_accessed=18 << 20, transcendentals=0),
    )(south, north, sides, fixed, side_fixed, planes)


def solve_kernel(flux_ref, mask_ref, moved_ref, out_ref, ratio_ref, *, absorb, decay):
    levels = moved_ref.shape[1]
    mask = mask_ref[...]
    heat_top = 0.5 * mask * flux_ref[0]
    sun = 0.5 * mask * flux_ref[1]
    salt_top = mask * flux_ref[2]
    stir = flux_ref[3]
    base = 0.2 * mask
    stir = 0.5 * mask * (stir * stir)
    above = jnp.zeros_like(mask)
    link = jnp.zeros_like(mask)
    heat_last = None
    salt_last = None
    for k in range(levels):
        heat = moved_ref[0, k] + absorb[k] * sun
        salt = moved_ref[1, k]
        if k == 0:
            heat = heat + heat_top
            salt = salt + salt_top
        below = base + decay[k] * stir if k < levels - 1 else jnp.zeros_like(mask)
        pivot = 1.0 + below + above
        if k > 0:
            pivot = pivot + above * link
            heat = heat + above * heat_last
            salt = salt + above * salt_last
        inverse = 1.0 / pivot
        link = -below * inverse
        heat_last = heat * inverse
        salt_last = salt * inverse
        above = below
        if k < levels - 1:
            ratio_ref[k] = link
        out_ref[0, k] = heat_last
        out_ref[1, k] = salt_last
    for k in range(levels - 2, -1, -1):
        link = ratio_ref[k]
        heat_last = out_ref[0, k] - link * heat_last
        salt_last = out_ref[1, k] - link * salt_last
        out_ref[0, k] = heat_last
        out_ref[1, k] = salt_last


def solve(flux, mask, moved, part, parts):
    count, levels, rows, columns = moved.shape
    depths = np.arange(levels, dtype=np.float64)
    absorb = tuple(float(a) for a in np.exp(-depths / 3.0) - np.exp(-(depths + 1.0) / 3.0))
    decay = tuple(float(a) for a in np.exp(-depths / 2.0))
    steps = rows // 8 // parts
    first = part * steps
    return pl.pallas_call(
        functools.partial(solve_kernel, absorb=absorb, decay=decay),
        name=f"column_solve_{part}",
        grid=(steps,),
        in_specs=[
            pl.BlockSpec((4, 8, columns), lambda i: (0, first + i, 0)),
            pl.BlockSpec((8, columns), lambda i: (first + i, 0)),
            pl.BlockSpec((count, levels, 8, columns), lambda i: (0, 0, first + i, 0)),
        ],
        out_specs=pl.BlockSpec((count, levels, 8, columns), lambda i: (0, 0, first + i, 0)),
        out_shape=jax.ShapeDtypeStruct(moved.shape, f32),
        scratch_shapes=[pltpu.VMEM((levels, 8, columns), f32)],
        input_output_aliases={2: 0},
        compiler_params=params(56),
        cost_estimate=pl.CostEstimate(flops=1 << 24, bytes_accessed=(18 << 20) // parts, transcendentals=0),
    )(flux, mask, moved)


def barotropic_kernel(
    fixed_ref, fixed_side_ref, flux_ref, south_ref, north_ref, west_ref, east_ref, height_ref, flow_ref, wide_ref
):
    rows = height_ref.shape[0]
    columns = height_ref.shape[1]
    wide_ref[0:5, :, :columns] = fixed_ref[...]
    wide_ref[0:5, :, columns:] = fixed_side_ref[...]
    middle = slice(EDGE, EDGE + rows)
    wide_ref[5:9, :EDGE, :columns] = south_ref[...]
    wide_ref[5:9, middle, :columns] = flux_ref[...]
    wide_ref[5:9, EDGE + rows :, :columns] = north_ref[...]
    lane = lax.broadcasted_iota(i32, west_ref.shape, 2)
    wide_ref[5:9, :, columns:] = jnp.where(lane < LANES // 2, east_ref[...], west_ref[...])
    mask = wide_ref[0]
    drag = -0.5 * wide_ref[1]
    height = wide_ref[2]
    along = wide_ref[3]
    across = wide_ref[4]
    wind_x = 0.5 * wide_ref[5]
    wind_y = 0.5 * wide_ref[6]
    push = 0.5 * wide_ref[7]
    source = wide_ref[8]
    for k in range(SUB):
        level = mask * (height + push)
        along = mask * (0.95 * along + drag * (beside(level, -1, 1) - beside(level, 1, 1)) + wind_x)
        across = mask * (0.95 * across + drag * (beside(level, -1, 0) - beside(level, 1, 0)) + wind_y)
        spread_out = beside(along, -1, 1) - beside(along, 1, 1) + beside(across, -1, 0) - beside(across, 1, 0)
        height = mask * (height - 0.5 * spread_out + source)
    height_ref[...] = height[middle, :columns]
    flow_ref[0] = along[middle, :columns]
    flow_ref[1] = across[middle, :columns]


def barotropic(fixed, fixed_side, flux, south, north, west, east):
    _, tall, columns = fixed.shape
    rows = tall - 2 * EDGE
    return pl.pallas_call(
        barotropic_kernel,
        name="barotropic",
        grid=(1,),
        in_specs=[
            whole(fixed),
            whole(fixed_side),
            pl.BlockSpec((4, rows, columns), lambda i: (0, 0, 0)),
            whole(south),
            whole(north),
            whole(west),
            whole(east),
        ],
        out_specs=[
            pl.BlockSpec((rows, columns), lambda i: (0, 0)),
            pl.BlockSpec((2, rows, columns), lambda i: (0, 0, 0)),
        ],
        out_shape=[
            jax.ShapeDtypeStruct((rows, columns), f32),
            jax.ShapeDtypeStruct((2, rows, columns), f32),
        ],
        scratch_shapes=[pltpu.VMEM((9, tall, columns + LANES), f32)],
        compiler_params=params(24),
        cost_estimate=pl.CostEstimate(flops=1 << 24, bytes_accessed=6 << 20, transcendentals=0),
    )(fixed, fixed_side, flux, south, north, west, east)


def to_next(array, axes):
    ends = lax.axis_size(axes) - 1
    return lax.ppermute(array, axes, [(i, i + 1) for i in range(ends)])


def to_previous(array, axes):
    ends = lax.axis_size(axes) - 1
    return lax.ppermute(array, axes, [(i + 1, i) for i in range(ends)])


def merge_sides(from_west, from_east):
    lane = lax.broadcasted_iota(i32, from_west.shape, from_west.ndim - 1)
    return jnp.where(lane < LANES // 2, from_east, from_west)


def all_to_all(array):
    return lax.all_to_all(array, EVERY, split_axis=0, concat_axis=0, tiled=True)


def local(
    atm_flux,
    margin_source,
    margin_cell,
    margin_weight,
    margin_tile,
    land_mask,
    sea_depth,
    sea_height,
    transport,
    tracers,
):
    tiles = lax.axis_size(EVERY)
    count, levels, rows, columns = tracers.shape
    packed = pack(
        margin_tile.reshape(-1), atm_flux, margin_source, margin_cell, margin_weight, tiles, rows * columns
    )
    packed, land_mask, sea_depth, sea_height, transport, tracers = lax.optimization_barrier(
        (packed, land_mask, sea_depth, sea_height, transport, tracers)
    )
    arrived = all_to_all(packed)

    mask = land_mask.astype(f32)
    planes = tracers.reshape(count * levels, rows, columns)
    tracer_south, tracer_north, tracer_sides = edges(planes)
    fixed = jnp.concatenate([jnp.stack([mask, sea_depth, sea_height]), transport], axis=0)
    tops = fixed[:, rows - EDGE :].reshape(5 * EDGE, columns)
    bottoms = fixed[:, :EDGE].reshape(5 * EDGE, columns)
    from_south = to_next(jnp.concatenate([tracer_north, tops], axis=0), ROWS)
    from_north = to_previous(jnp.concatenate([tracer_south, bottoms], axis=0), ROWS)
    wide = count * levels
    fixed = jnp.concatenate(
        [
            from_south[wide:].reshape(5, EDGE, columns),
            fixed,
            from_north[wide:].reshape(5, EDGE, columns),
        ],
        axis=1,
    )
    tall = rows + 2 * EDGE
    east_edge = jnp.concatenate([fixed[:, :, -LANES:].reshape(5 * tall, LANES), tracer_sides[1]], axis=0)
    west_edge = jnp.concatenate([fixed[:, :, :LANES].reshape(5 * tall, LANES), tracer_sides[0]], axis=0)
    from_west = to_next(east_edge, "tx")
    from_east = to_previous(west_edge, "tx")
    fixed_side = merge_sides(from_west[: 5 * tall], from_east[: 5 * tall]).reshape(5, tall, LANES)
    sides = jnp.stack([from_east[5 * tall :], from_west[5 * tall :]])
    moved = move(from_south[:wide], from_north[:wide], sides, fixed, fixed_side, planes)

    arrived, moved = lax.optimization_barrier((arrived, moved))
    winds, heats, flux_low, flux_high = spread(arrived, rows, columns)
    flux_south = to_next(flux_high, ROWS)
    flux_north = to_previous(flux_low, ROWS)
    moved = solve(heats, mask, moved.reshape(tracers.shape), 0, 2)
    flux_south, flux_north, moved = lax.optimization_barrier((flux_south, flux_north, moved))
    east_edge = jnp.concatenate(
        [flux_south[:, :, -LANES:], winds[:, :, -LANES:], flux_north[:, :, -LANES:]], axis=1
    )
    west_edge = jnp.concatenate(
        [flux_south[:, :, :LANES], winds[:, :, :LANES], flux_north[:, :, :LANES]], axis=1
    )
    flux_west = to_next(east_edge, "tx")
    flux_east = to_previous(west_edge, "tx")
    solved = solve(heats, mask, moved, 1, 2)
    flux_west, flux_east, solved = lax.optimization_barrier((flux_west, flux_east, solved))
    new_height, new_transport = barotropic(
        fixed, fixed_side, winds, flux_south, flux_north, flux_west, flux_east
    )
    return new_height, new_transport, solved


def solution(mesh):
    in_specs = (
        P(None, EVERY),
        P(EVERY, None),
        P(EVERY, None),
        P(EVERY, None),
        P(EVERY, None),
        P(ROWS, "tx"),
        P(ROWS, "tx"),
        P(ROWS, "tx"),
        P(None, ROWS, "tx"),
        P(None, None, ROWS, "tx"),
    )
    out_specs = (P(ROWS, "tx"), P(None, ROWS, "tx"), P(None, None, ROWS, "tx"))
    return jax.shard_map(local, mesh=mesh, in_specs=in_specs, out_specs=out_specs, check_vma=False)
```

```python
import functools

import jax
import jax.numpy as jnp
import numpy as np
from jax import lax
from jax.experimental import pallas as pl
from jax.experimental.pallas import tpu as pltpu
from jax.sharding import PartitionSpec as P

SUB = 3
EDGE = 8
LANES = 128
EVERY = ("comp", "ty", "tx")
ROWS = ("comp", "ty")
f32 = jnp.float32
i32 = jnp.int32
VM = pl.BlockSpec(memory_space=pltpu.VMEM)
SM = pl.BlockSpec(memory_space=pltpu.SMEM)


def params(mib):
    return pltpu.CompilerParams(vmem_limit_bytes=mib << 20)


def whole(array):
    return pl.BlockSpec(array.shape, lambda i: (0,) * array.ndim)


def pack_kernel(tile_ref, flux_ref, source_ref, cell_ref, weight_ref, first_ref, second_ref, count_ref, *, beyond):
    blocks = source_ref.shape[0]
    tiles = first_ref.shape[0]
    group = 4
    nowhere = jnp.full((4, LANES), beyond, f32)

    def clear(t, carry):
        count_ref[t] = 0
        first_ref[t, 4] = nowhere
        return carry

    lax.fori_loop(0, tiles, clear, 0, unroll=True)
    sub = lax.broadcasted_iota(i32, (8, LANES), 0)

    def step(i, carry):
        for g in range(group):
            w = i * group + g
            x = flux_ref[:, pl.ds(pl.multiple_of(w * LANES, LANES), LANES)]
            after = pltpu.roll(x, 1, 0)
            six = pltpu.roll(x, 5, 0)
            five = pltpu.roll(x, 6, 0)
            y = jnp.where((sub == 4) | (sub == 5), after, x)
            y = jnp.where(sub == 6, 0.5 * after - 0.3 * x, y)
            y = jnp.where(sub == 3, 0.1 * (six - five), y)
            for half in range(2):
                b = 2 * w + half
                tile = tile_ref[b]
                slot = count_ref[tile]
                count_ref[tile] = slot + 1
                index = jnp.broadcast_to(source_ref[pl.ds(b, 1), :], (8, LANES))
                picked = jnp.take_along_axis(y, index, axis=1)
                value = picked * jnp.broadcast_to(weight_ref[pl.ds(b, 1), :], (8, LANES))
                first_ref[tile, slot] = value[0:4]
                second_ref[tile, slot] = value[4:8]
                first_ref[tile, 4, pl.ds(slot, 1), :] = cell_ref[pl.ds(b, 1), :].astype(f32)
        return carry

    lax.fori_loop(0, blocks // (2 * group), step, 0)


def pack(tile, flux, source, cell, weight, tiles, beyond):
    return pl.pallas_call(
        functools.partial(pack_kernel, beyond=beyond),
        name="pack_margin",
        grid=(1,),
        in_specs=[SM, whole(flux), whole(source), whole(cell), whole(weight)],
        out_specs=[
            pl.BlockSpec((tiles, 5, 4, LANES), lambda i: (0, 0, 0, 0)),
            pl.BlockSpec((tiles, 4, 4, LANES), lambda i: (0, 0, 0, 0)),
        ],
        out_shape=[
            jax.ShapeDtypeStruct((tiles, 5, 4, LANES), f32),
            jax.ShapeDtypeStruct((tiles, 4, 4, LANES), f32),
        ],
        scratch_shapes=[pltpu.SMEM((tiles,), i32)],
        compiler_params=params(56),
        cost_estimate=pl.CostEstimate(flops=1 << 22, bytes_accessed=4 << 20, transcendentals=0),
    )(tile, flux, source, cell, weight)


def spread_kernel(cells_ref, value_ref, out_ref, acc_ref, *, group):
    sources = value_ref.shape[0]
    fields, rows, columns = out_ref.shape
    high = columns // LANES
    depth = fields * high

    def clear(i, c):
        acc_ref[pl.ds(pl.multiple_of(i * 256, 256), 256), :] = jnp.zeros((256, LANES), f32)
        return c

    lax.fori_loop(0, rows * depth // 256, clear, 0)
    lane = lax.broadcasted_iota(i32, (LANES, LANES), 0).astype(f32).astype(jnp.bfloat16)
    sub = lax.broadcasted_iota(i32, (16, LANES), 0) >> 2
    pattern = [(4 * i + sub).astype(f32).astype(jnp.bfloat16) for i in range(high // 4)]
    zero16 = jnp.zeros((16, LANES), jnp.bfloat16)
    one = jnp.ones((LANES, LANES), jnp.bfloat16)
    zero = jnp.zeros((LANES, LANES), jnp.bfloat16)

    def step(i, carry):
        for g in range(group):
            s = i * group + g
            cells = cells_ref[s, 4].astype(i32)
            highs = ((cells & (columns - 1)) >> 7).astype(f32)
            lows = (cells & (LANES - 1)).astype(f32)
            for k in range(4):
                value = value_ref[s, k]
                coarse = value.astype(jnp.bfloat16).astype(f32)
                fine = value - coarse
                coarse = jnp.concatenate([coarse] * 4, axis=0).astype(jnp.bfloat16)
                fine = jnp.concatenate([fine] * 4, axis=0).astype(jnp.bfloat16)
                hk = jnp.broadcast_to(highs[k : k + 1], (16, LANES)).astype(jnp.bfloat16)
                left = []
                right = []
                for p in pattern:
                    hit = hk == p
                    left.append(jnp.where(hit, coarse, zero16))
                    right.append(jnp.where(hit, fine, zero16))
                lhs = jnp.concatenate([jnp.concatenate(left, axis=0), jnp.concatenate(right, axis=0)], axis=1)
                low = jnp.concatenate([jnp.broadcast_to(lows[k : k + 1], (16, LANES)).astype(jnp.bfloat16)] * (LANES // 16), axis=0)
                onehot = jnp.where(low == lane, one, zero)
                rhs = jnp.concatenate([onehot, onehot], axis=1)
                both = lax.dot_general(lhs, rhs, (((1,), (1,)), ((), ())), preferred_element_type=f32)
                row = cells[k, 0] >> (columns.bit_length() - 1)
                place = pl.ds(pl.multiple_of(row * depth, depth), depth)
                acc_ref[place, :] += both
        return carry

    lax.fori_loop(0, sources // group, step, 0)

    def turn(i, carry):
        r = pl.multiple_of(i * 8, 8)
        block = acc_ref[pl.ds(pl.multiple_of(r * depth, 8 * depth), 8 * depth), :].reshape(8, depth, LANES)
        for n in range(depth // 8):
            piece = jnp.swapaxes(block[:, n * 8 : n * 8 + 8, :], 0, 1)
            for e in range(8):
                h = 2 * n + e // 4
                out_ref[e % 4, pl.ds(r, 8), h * LANES : (h + 1) * LANES] = piece[e]
        return carry

    lax.fori_loop(0, rows // 8, turn, 0)

def spread(cells, load, rows, columns, name):
    depth = 4 * columns // LANES
    group = 8
    return pl.pallas_call(
        functools.partial(spread_kernel, group=group),
        name=name,
        in_specs=[VM, VM],
        out_specs=VM,
        out_shape=jax.ShapeDtypeStruct((4, rows, columns), f32),
        scratch_shapes=[pltpu.VMEM(((rows + 1) * depth, LANES), f32)],
        compiler_params=params(24),
        cost_estimate=pl.CostEstimate(flops=1 << 30, bytes_accessed=4 << 20, transcendentals=0),
    )(cells, load)


def edges_kernel(low_ref, high_ref, west_ref, east_ref, south_ref, north_ref, columns_ref):
    levels = low_ref.shape[0]
    rows = west_ref.shape[1]
    lane = lax.broadcasted_iota(i32, (rows, LANES), 1)
    lasts = jnp.zeros((rows, LANES), f32)
    firsts = jnp.zeros((rows, LANES), f32)
    for p in range(levels):
        south_ref[p : p + 1, :] = low_ref[p, 0:1, :]
        north_ref[p : p + 1, :] = high_ref[p, EDGE - 1 : EDGE, :]
        firsts = jnp.where(lane == p, west_ref[p, :, 0:1], firsts)
        lasts = jnp.where(lane == p, east_ref[p, :, LANES - 1 : LANES], lasts)
    columns_ref[0] = firsts
    columns_ref[1] = lasts


def edges(planes):
    levels, rows, columns = planes.shape
    last_row = rows // EDGE - 1
    last_lane = columns // LANES - 1
    return pl.pallas_call(
        edges_kernel,
        name="tracer_edges",
        grid=(1,),
        in_specs=[
            pl.BlockSpec((levels, EDGE, columns), lambda i: (0, 0, 0)),
            pl.BlockSpec((levels, EDGE, columns), lambda i: (0, last_row, 0)),
            pl.BlockSpec((levels, rows, LANES), lambda i: (0, 0, 0)),
            pl.BlockSpec((levels, rows, LANES), lambda i: (0, 0, last_lane)),
        ],
        out_specs=[
            pl.BlockSpec((levels, columns), lambda i: (0, 0)),
            pl.BlockSpec((levels, columns), lambda i: (0, 0)),
            pl.BlockSpec((2, rows, LANES), lambda i: (0, 0, 0)),
        ],
        out_shape=[
            jax.ShapeDtypeStruct((levels, columns), f32),
            jax.ShapeDtypeStruct((levels, columns), f32),
            jax.ShapeDtypeStruct((2, rows, LANES), f32),
        ],
        compiler_params=params(56),
        cost_estimate=pl.CostEstimate(flops=1 << 20, bytes_accessed=4 << 20, transcendentals=0),
    )(planes, planes, planes, planes)


def beside(array, amount, axis):
    return pltpu.roll(array, amount % array.shape[axis], axis)


def drift(speed, toward):
    return 0.1 + 0.15 * jnp.maximum(-toward * speed, 0.0)


def move_kernel(mask_ref, depth_ref, flow_ref, planes_ref, out_ref, coef_ref, *, per):
    step = pl.program_id(0)
    rows = planes_ref.shape[1]
    columns = planes_ref.shape[2]

    @pl.when(step == 0)
    def _():
        mask = mask_ref[...].astype(f32)
        lane = lax.broadcasted_iota(i32, (rows, columns), 1)
        sub = lax.broadcasted_iota(i32, (rows, columns), 0)
        u = flow_ref[0] / depth_ref[...]
        v = flow_ref[1] / depth_ref[...]
        east = mask * jnp.where(lane == columns - 1, 0.0, beside(mask, -1, 1)) * drift(u, 1.0)
        west = mask * jnp.where(lane == 0, 0.0, beside(mask, 1, 1)) * drift(u, -1.0)
        north = mask * jnp.where(sub == rows - 1, 0.0, beside(mask, -1, 0)) * drift(v, 1.0)
        south = mask * jnp.where(sub == 0, 0.0, beside(mask, 1, 0)) * drift(v, -1.0)
        coef_ref[0] = 1.0 - (east + west + north + south)
        coef_ref[1] = east
        coef_ref[2] = west
        coef_ref[3] = north
        coef_ref[4] = south

    for n in range(per):
        for r in range(0, rows, 8):
            span = slice(r, r + 8)
            q = planes_ref[n, span, :]
            sub = lax.broadcasted_iota(i32, (8, columns), 0)
            east = beside(q, -1, 1)
            west = beside(q, 1, 1)
            below = planes_ref[n, max(r - 1, 0) : max(r - 1, 0) + 1, :]
            above = planes_ref[n, min(r + 8, rows - 1) : min(r + 8, rows - 1) + 1, :]
            north = jnp.where(sub == 7, above, beside(q, -1, 0))
            south = jnp.where(sub == 0, below, beside(q, 1, 0))
            out_ref[n, span, :] = (
                coef_ref[0, span, :] * q
                + coef_ref[1, span, :] * east
                + coef_ref[2, span, :] * west
                + coef_ref[3, span, :] * north
                + coef_ref[4, span, :] * south
            )


def move(mask, depth, flow, planes):
    levels, rows, columns = planes.shape
    per = 4
    return pl.pallas_call(
        functools.partial(move_kernel, per=per),
        name="tracer_move",
        grid=(levels // per,),
        in_specs=[
            whole(mask),
            whole(depth),
            whole(flow),
            pl.BlockSpec((per, rows, columns), lambda i: (i, 0, 0)),
        ],
        out_specs=pl.BlockSpec((per, rows, columns), lambda i: (i, 0, 0)),
        out_shape=jax.ShapeDtypeStruct(planes.shape, f32),
        scratch_shapes=[pltpu.VMEM((5, rows, columns), f32)],
        compiler_params=params(56),
        cost_estimate=pl.CostEstimate(flops=1 << 25, bytes_accessed=18 << 20, transcendentals=0),
    )(mask, depth, flow, planes)


def patch_rows_kernel(south_ref, north_ref, low_ref, high_ref, fixed_ref, moved_ref, out_ref):
    step = pl.program_id(0)
    levels = moved_ref.shape[0]
    columns = moved_ref.shape[2]
    upper = step == 1
    row = jnp.where(upper, fixed_ref.shape[1] - EDGE - 1, EDGE)
    other = jnp.where(upper, row + 1, row - 1)
    toward = jnp.where(upper, 1.0, -1.0)
    mask = fixed_ref[0, pl.ds(row, 1), :]
    beyond = fixed_ref[0, pl.ds(other, 1), :]
    v = fixed_ref[4, pl.ds(row, 1), :] / fixed_ref[1, pl.ds(row, 1), :]
    coef = mask * beyond * drift(v, toward)
    near = jnp.where(upper, north_ref[0:levels, :], south_ref[0:levels, :])
    own = jnp.where(upper, high_ref[...], low_ref[...])
    extra = coef * (near - own)
    hit = lax.broadcasted_iota(i32, (EDGE, columns), 0) == jnp.where(upper, EDGE - 1, 0)
    for p in range(levels):
        out_ref[p] = moved_ref[p] + jnp.where(hit, extra[p : p + 1, :], 0.0)


def patch_rows(south, north, low, high, fixed, moved):
    levels, rows, columns = moved.shape
    last = rows // EDGE - 1
    block = pl.BlockSpec((levels, EDGE, columns), lambda i: (0, i * last, 0))
    return pl.pallas_call(
        patch_rows_kernel,
        name="patch_rows",
        grid=(2,),
        in_specs=[whole(south), whole(north), whole(low), whole(high), whole(fixed), block],
        out_specs=block,
        out_shape=jax.ShapeDtypeStruct(moved.shape, f32),
        input_output_aliases={5: 0},
        compiler_params=params(56),
        cost_estimate=pl.CostEstimate(flops=1 << 20, bytes_accessed=4 << 20, transcendentals=0),
    )(south, north, low, high, fixed, moved)


def patch_columns_kernel(near_ref, own_ref, side_ref, fixed_ref, moved_ref, out_ref):
    step = pl.program_id(0)
    levels, rows, _ = moved_ref.shape
    upper = step == 1
    edge = jnp.where(upper, LANES - 1, 0)
    toward = jnp.where(upper, 1.0, -1.0)
    lane = lax.broadcasted_iota(i32, (rows, LANES), 1)
    hit = lane == edge
    middle = slice(EDGE, EDGE + rows)

    def column(value, chosen):
        return jnp.sum(jnp.where(chosen, value, 0.0), axis=1, keepdims=True)

    mask = column(fixed_ref[0, middle, :], hit)
    depth = column(fixed_ref[1, middle, :], hit)
    flow = column(fixed_ref[3, middle, :], hit)
    beyond = column(side_ref[0, middle, :], lane == LANES - 1 - edge)
    coef = mask * beyond * drift(flow / depth, toward)
    extra = coef * (near_ref[0] - own_ref[0])
    for p in range(levels):
        out_ref[p] = moved_ref[p] + jnp.where(hit, extra[:, p : p + 1], 0.0)


def patch_columns(near, own, side, fixed, moved):
    levels, rows, columns = moved.shape
    last = columns // LANES - 1
    block = pl.BlockSpec((levels, rows, LANES), lambda i: (0, 0, i * last))
    one = pl.BlockSpec((1, rows, LANES), lambda i: (i, 0, 0))
    return pl.pallas_call(
        patch_columns_kernel,
        name="patch_columns",
        grid=(2,),
        in_specs=[
            one,
            one,
            whole(side),
            pl.BlockSpec((5, fixed.shape[1], LANES), lambda i: (0, 0, i * last)),
            block,
        ],
        out_specs=block,
        out_shape=jax.ShapeDtypeStruct(moved.shape, f32),
        input_output_aliases={4: 0},
        compiler_params=params(56),
        cost_estimate=pl.CostEstimate(flops=1 << 20, bytes_accessed=4 << 20, transcendentals=0),
    )(near, own, side, fixed, moved)


def solve_kernel(flux_ref, mask_ref, moved_ref, out_ref, ratio_ref, *, absorb, decay):
    levels = moved_ref.shape[1]
    mask = mask_ref[...]
    heat_top = 0.5 * mask * flux_ref[0]
    sun = 0.5 * mask * flux_ref[1]
    salt_top = mask * flux_ref[2]
    stir = flux_ref[3]
    base = 0.2 * mask
    stir = 0.5 * mask * (stir * stir)
    above = jnp.zeros_like(mask)
    link = jnp.zeros_like(mask)
    heat_last = None
    salt_last = None
    for k in range(levels):
        heat = moved_ref[0, k] + absorb[k] * sun
        salt = moved_ref[1, k]
        if k == 0:
            heat = heat + heat_top
            salt = salt + salt_top
        below = base + decay[k] * stir if k < levels - 1 else jnp.zeros_like(mask)
        pivot = 1.0 + below + above
        if k > 0:
            pivot = pivot + above * link
            heat = heat + above * heat_last
            salt = salt + above * salt_last
        inverse = 1.0 / pivot
        link = -below * inverse
        heat_last = heat * inverse
        salt_last = salt * inverse
        above = below
        if k < levels - 1:
            ratio_ref[k] = link
        out_ref[0, k] = heat_last
        out_ref[1, k] = salt_last
    for k in range(levels - 2, -1, -1):
        link = ratio_ref[k]
        heat_last = out_ref[0, k] - link * heat_last
        salt_last = out_ref[1, k] - link * salt_last
        out_ref[0, k] = heat_last
        out_ref[1, k] = salt_last


def solve(flux, mask, moved):
    count, levels, rows, columns = moved.shape
    depths = np.arange(levels, dtype=np.float64)
    absorb = tuple(float(a) for a in np.exp(-depths / 3.0) - np.exp(-(depths + 1.0) / 3.0))
    decay = tuple(float(a) for a in np.exp(-depths / 2.0))
    return pl.pallas_call(
        functools.partial(solve_kernel, absorb=absorb, decay=decay),
        name="column_solve",
        grid=(rows // 8,),
        in_specs=[
            pl.BlockSpec((4, 8, columns), lambda i: (0, i, 0)),
            pl.BlockSpec((8, columns), lambda i: (i, 0)),
            pl.BlockSpec((count, levels, 8, columns), lambda i: (0, 0, i, 0)),
        ],
        out_specs=pl.BlockSpec((count, levels, 8, columns), lambda i: (0, 0, i, 0)),
        out_shape=jax.ShapeDtypeStruct(moved.shape, f32),
        scratch_shapes=[pltpu.VMEM((levels, 8, columns), f32)],
        input_output_aliases={2: 0},
        compiler_params=params(56),
        cost_estimate=pl.CostEstimate(flops=1 << 25, bytes_accessed=18 << 20, transcendentals=0),
    )(flux, mask, moved)


def barotropic_kernel(
    fixed_ref, fixed_side_ref, flux_ref, south_ref, north_ref, west_ref, east_ref, height_ref, flow_ref, wide_ref
):
    rows = height_ref.shape[0]
    columns = height_ref.shape[1]
    wide_ref[0:5, :, :columns] = fixed_ref[...]
    wide_ref[0:5, :, columns:] = fixed_side_ref[...]
    middle = slice(EDGE, EDGE + rows)
    wide_ref[5:9, :EDGE, :columns] = south_ref[...]
    wide_ref[5:9, middle, :columns] = flux_ref[...]
    wide_ref[5:9, EDGE + rows :, :columns] = north_ref[...]
    lane = lax.broadcasted_iota(i32, west_ref.shape, 2)
    wide_ref[5:9, :, columns:] = jnp.where(lane < LANES // 2, east_ref[...], west_ref[...])
    mask = wide_ref[0]
    drag = -0.5 * wide_ref[1]
    height = wide_ref[2]
    along = wide_ref[3]
    across = wide_ref[4]
    wind_x = 0.5 * wide_ref[5]
    wind_y = 0.5 * wide_ref[6]
    push = 0.5 * wide_ref[7]
    source = wide_ref[8]
    for k in range(SUB):
        level = mask * (height + push)
        along = mask * (0.95 * along + drag * (beside(level, -1, 1) - beside(level, 1, 1)) + wind_x)
        across = mask * (0.95 * across + drag * (beside(level, -1, 0) - beside(level, 1, 0)) + wind_y)
        spread_out = beside(along, -1, 1) - beside(along, 1, 1) + beside(across, -1, 0) - beside(across, 1, 0)
        height = mask * (height - 0.5 * spread_out + source)
    height_ref[...] = height[middle, :columns]
    flow_ref[0] = along[middle, :columns]
    flow_ref[1] = across[middle, :columns]


def barotropic(fixed, fixed_side, flux, south, north, west, east):
    _, tall, columns = fixed.shape
    rows = tall - 2 * EDGE
    return pl.pallas_call(
        barotropic_kernel,
        name="barotropic",
        grid=(1,),
        in_specs=[
            whole(fixed),
            whole(fixed_side),
            pl.BlockSpec((4, rows, columns), lambda i: (0, 0, 0)),
            whole(south),
            whole(north),
            whole(west),
            whole(east),
        ],
        out_specs=[
            pl.BlockSpec((rows, columns), lambda i: (0, 0)),
            pl.BlockSpec((2, rows, columns), lambda i: (0, 0, 0)),
        ],
        out_shape=[
            jax.ShapeDtypeStruct((rows, columns), f32),
            jax.ShapeDtypeStruct((2, rows, columns), f32),
        ],
        scratch_shapes=[pltpu.VMEM((9, tall, columns + LANES), f32)],
        compiler_params=params(24),
        cost_estimate=pl.CostEstimate(flops=1 << 24, bytes_accessed=6 << 20, transcendentals=0),
    )(fixed, fixed_side, flux, south, north, west, east)


def to_next(array, axes):
    ends = lax.axis_size(axes) - 1
    return lax.ppermute(array, axes, [(i, i + 1) for i in range(ends)])


def to_previous(array, axes):
    ends = lax.axis_size(axes) - 1
    return lax.ppermute(array, axes, [(i + 1, i) for i in range(ends)])


def merge_sides(from_west, from_east):
    lane = lax.broadcasted_iota(i32, from_west.shape, from_west.ndim - 1)
    return jnp.where(lane < LANES // 2, from_east, from_west)


def all_to_all(array):
    return lax.all_to_all(array, EVERY, split_axis=0, concat_axis=0, tiled=True)


def local(
    atm_flux,
    margin_source,
    margin_cell,
    margin_weight,
    margin_tile,
    land_mask,
    sea_depth,
    sea_height,
    transport,
    tracers,
):
    tiles = lax.axis_size(EVERY)
    count, levels, rows, columns = tracers.shape
    first, second = pack(
        margin_tile.reshape(-1), atm_flux, margin_source, margin_cell, margin_weight, tiles, rows * columns
    )
    first, second, land_mask, sea_depth, sea_height, transport, tracers = lax.optimization_barrier(
        (first, second, land_mask, sea_depth, sea_height, transport, tracers)
    )
    arrived = all_to_all(first)

    planes = tracers.reshape(count * levels, rows, columns)
    wide = count * levels
    low, high, own_sides = edges(planes)
    mask = land_mask.astype(f32)
    fixed = jnp.concatenate([jnp.stack([mask, sea_depth, sea_height]), transport], axis=0)
    tops = fixed[:, rows - EDGE :].reshape(5 * EDGE, columns)
    bottoms = fixed[:, :EDGE].reshape(5 * EDGE, columns)
    from_south = to_next(jnp.concatenate([high, tops], axis=0), ROWS)
    from_north = to_previous(jnp.concatenate([low, bottoms], axis=0), ROWS)
    moved = move(land_mask, sea_depth, transport, planes)
    arrived, second, moved = lax.optimization_barrier((arrived, second, moved))
    arrived_second = all_to_all(second)

    from_south, from_north, arrived = lax.optimization_barrier((from_south, from_north, arrived))
    fixed = jnp.concatenate(
        [
            from_south[wide:].reshape(5, EDGE, columns),
            fixed,
            from_north[wide:].reshape(5, EDGE, columns),
        ],
        axis=1,
    )
    tall = rows + 2 * EDGE
    east_edge = jnp.concatenate([fixed[:, :, -LANES:].reshape(5 * tall, LANES), own_sides[1]], axis=0)
    west_edge = jnp.concatenate([fixed[:, :, :LANES].reshape(5 * tall, LANES), own_sides[0]], axis=0)
    from_west = to_next(east_edge, "tx")
    from_east = to_previous(west_edge, "tx")
    moved = patch_rows(from_south, from_north, low, high, fixed, moved)
    winds = spread(arrived, arrived, rows, columns, "spread_winds")
    from_west, from_east, winds, moved = lax.optimization_barrier((from_west, from_east, winds, moved))
    flux_south = to_next(winds[:, rows - EDGE :], ROWS)
    flux_north = to_previous(winds[:, :EDGE], ROWS)
    fixed_side = merge_sides(from_west[: 5 * tall], from_east[: 5 * tall]).reshape(5, tall, LANES)
    near_sides = jnp.stack([from_west[5 * tall :], from_east[5 * tall :]])
    moved = patch_columns(near_sides, own_sides, fixed_side, fixed, moved)
    flux_south, flux_north, moved = lax.optimization_barrier((flux_south, flux_north, moved))
    east_edge = jnp.concatenate(
        [flux_south[:, :, -LANES:], winds[:, :, -LANES:], flux_north[:, :, -LANES:]], axis=1
    )
    west_edge = jnp.concatenate(
        [flux_south[:, :, :LANES], winds[:, :, :LANES], flux_north[:, :, :LANES]], axis=1
    )
    flux_west = to_next(east_edge, "tx")
    flux_east = to_previous(west_edge, "tx")
    heats = spread(arrived, arrived_second, rows, columns, "spread_heats")
    solved = solve(heats, mask, moved.reshape(tracers.shape))
    new_height, new_transport = barotropic(
        fixed, fixed_side, winds, flux_south, flux_north, flux_west, flux_east
    )
    return new_height, new_transport, solved


def solution(mesh):
    in_specs = (
        P(None, EVERY),
        P(EVERY, None),
        P(EVERY, None),
        P(EVERY, None),
        P(EVERY, None),
        P(ROWS, "tx"),
        P(ROWS, "tx"),
        P(ROWS, "tx"),
        P(None, ROWS, "tx"),
        P(None, None, ROWS, "tx"),
    )
    out_specs = (P(ROWS, "tx"), P(None, ROWS, "tx"), P(None, None, ROWS, "tx"))
    return jax.shard_map(local, mesh=mesh, in_specs=in_specs, out_specs=out_specs, check_vma=False)
```

```python
import functools

import jax
import jax.numpy as jnp
import numpy as np
from jax import lax
from jax.experimental import pallas as pl
from jax.experimental.pallas import tpu as pltpu
from jax.sharding import PartitionSpec as P

SUB = 3
EDGE = 8
LANES = 128
EVERY = ("comp", "ty", "tx")
ROWS = ("comp", "ty")
f32 = jnp.float32
i32 = jnp.int32
VM = pl.BlockSpec(memory_space=pltpu.VMEM)
SM = pl.BlockSpec(memory_space=pltpu.SMEM)


def params(mib):
    return pltpu.CompilerParams(vmem_limit_bytes=mib << 20)


def whole(array):
    return pl.BlockSpec(array.shape, lambda i: (0,) * array.ndim)


def pack_kernel(tile_ref, flux_ref, source_ref, cell_ref, weight_ref, out_ref, count_ref, *, beyond):
    blocks = source_ref.shape[0]
    tiles = out_ref.shape[0]
    group = 4
    nowhere = jnp.full((4, LANES), beyond, f32)

    def clear(t, carry):
        count_ref[t] = 0
        out_ref[t, 8] = nowhere
        return carry

    lax.fori_loop(0, tiles, clear, 0, unroll=True)
    sub = lax.broadcasted_iota(i32, (8, LANES), 0)

    def step(i, carry):
        for g in range(group):
            w = i * group + g
            x = flux_ref[:, pl.ds(pl.multiple_of(w * LANES, LANES), LANES)]
            after = pltpu.roll(x, 1, 0)
            six = pltpu.roll(x, 5, 0)
            five = pltpu.roll(x, 6, 0)
            y = jnp.where((sub == 4) | (sub == 5), after, x)
            y = jnp.where(sub == 6, 0.5 * after - 0.3 * x, y)
            y = jnp.where(sub == 3, 0.1 * (six - five), y)
            for half in range(2):
                b = 2 * w + half
                tile = tile_ref[b]
                slot = count_ref[tile]
                count_ref[tile] = slot + 1
                index = jnp.broadcast_to(source_ref[pl.ds(b, 1), :], (8, LANES))
                picked = jnp.take_along_axis(y, index, axis=1)
                value = picked * jnp.broadcast_to(weight_ref[pl.ds(b, 1), :], (8, LANES))
                out_ref[tile, slot] = value[0:4]
                out_ref[tile, 4 + slot] = value[4:8]
                out_ref[tile, 8, pl.ds(slot, 1), :] = cell_ref[pl.ds(b, 1), :].astype(f32)
        return carry

    lax.fori_loop(0, blocks // (2 * group), step, 0)


def pack(tile, flux, source, cell, weight, tiles, beyond):
    return pl.pallas_call(
        functools.partial(pack_kernel, beyond=beyond),
        name="pack_margin",
        grid=(1,),
        in_specs=[SM, whole(flux), whole(source), whole(cell), whole(weight)],
        out_specs=pl.BlockSpec((tiles, 9, 4, LANES), lambda i: (0, 0, 0, 0)),
        out_shape=jax.ShapeDtypeStruct((tiles, 9, 4, LANES), f32),
        scratch_shapes=[pltpu.SMEM((tiles,), i32)],
        compiler_params=params(56),
        cost_estimate=pl.CostEstimate(flops=1 << 22, bytes_accessed=4 << 20, transcendentals=0),
    )(tile, flux, source, cell, weight)


def spread_kernel(load_ref, winds_ref, heats_ref, south_ref, north_ref, acc_ref, *, group):
    sources = load_ref.shape[0]
    _, rows, columns = winds_ref.shape
    fields = 8
    high = columns // LANES
    depth = fields * high
    def clear(i, c):
        acc_ref[pl.ds(pl.multiple_of(i * 256, 256), 256),:] = jnp.zeros((256, LANES), f32)
        return c
    lax.fori_loop(0, rows * depth // 256, clear, 0)
    low_iota = lax.broadcasted_iota(i32, (LANES, LANES), 0).astype(f32).astype(jnp.bfloat16)
    pattern = [
        (2 * i + (lax.broadcasted_iota(i32, (16, LANES), 0) >> 3)).astype(f32).astype(jnp.bfloat16) for i in range(high // 2)
    ]
    zero16 = jnp.zeros((16, LANES), jnp.bfloat16)
    one = jnp.ones((LANES, LANES), jnp.bfloat16)
    zero = jnp.zeros((LANES, LANES), jnp.bfloat16)

    def step(i, carry):
        for g in range(group):
            s = i * group + g
            cells = load_ref[s, 8].astype(i32)
            highs = ((cells & (columns - 1)) >> 7).astype(f32)
            lows = (cells & (LANES - 1)).astype(f32)
            for k in range(4):
                value = jnp.concatenate([load_ref[s, k], load_ref[s, 4 + k]], axis=0)
                coarse = value.astype(jnp.bfloat16).astype(f32)
                fine = value - coarse
                coarse = jnp.concatenate([coarse, coarse], axis=0).astype(jnp.bfloat16)
                fine = jnp.concatenate([fine, fine], axis=0).astype(jnp.bfloat16)
                hk = jnp.broadcast_to(highs[k : k + 1], (16, LANES)).astype(jnp.bfloat16)
                lk = jnp.broadcast_to(lows[k : k + 1], (16, LANES)).astype(jnp.bfloat16)
                lk = jnp.concatenate([lk] * (LANES // 16), axis=0)
                left = []
                right = []
                for p in pattern:
                    hit = hk == p
                    left.append(jnp.where(hit, coarse, zero16))
                    right.append(jnp.where(hit, fine, zero16))
                lhs = jnp.concatenate([jnp.concatenate(left, axis=0), jnp.concatenate(right, axis=0)], axis=1)
                onehot = jnp.where(lk == low_iota, one, zero)
                rhs = jnp.concatenate([onehot, onehot], axis=1)
                both = lax.dot_general(lhs, rhs, (((1,), (1,)), ((), ())), preferred_element_type=f32)
                row = cells[k, 0] >> (columns.bit_length() - 1)
                place = pl.ds(pl.multiple_of(row * depth, depth), depth)
                acc_ref[place, :] += both
        return carry

    lax.fori_loop(0, sources // group, step, 0)

    def turn(i, carry):
        r = pl.multiple_of(i * 8, 8)
        block = acc_ref[pl.ds(pl.multiple_of(r * depth, 8 * depth), 8 * depth), :].reshape(8, depth, LANES)
        for h in range(high):
            piece = jnp.swapaxes(block[:, h * 8 : h * 8 + 8, :], 0, 1)
            for f in range(fields):
                ref = winds_ref if f < 4 else heats_ref
                ref[f % 4, pl.ds(r, 8), h * LANES : (h + 1) * LANES] = piece[f]
        return carry

    lax.fori_loop(0, rows // 8, turn, 0)
    south_ref[...] = winds_ref[:, 0:EDGE, :]
    north_ref[...] = winds_ref[:, rows - EDGE : rows, :]

def spread(load, rows, columns):
    depth = 8 * columns // LANES
    group = 8 if load.shape[0] % 8 == 0 else 1
    return pl.pallas_call(
        functools.partial(spread_kernel, group=group),
        name="spread_all",
        in_specs=[VM],
        out_specs=[VM] * 4,
        out_shape=[
            jax.ShapeDtypeStruct((4, rows, columns), f32),
            jax.ShapeDtypeStruct((4, rows, columns), f32),
            jax.ShapeDtypeStruct((4, EDGE, columns), f32),
            jax.ShapeDtypeStruct((4, EDGE, columns), f32),
        ],
        scratch_shapes=[pltpu.VMEM(((rows + 1) * depth, LANES), f32)],
        compiler_params=params(24),
        cost_estimate=pl.CostEstimate(flops=1 << 30, bytes_accessed=4 << 20, transcendentals=0),
    )(load)


def edges_kernel(
    low_ref, high_ref, left_ref, right_ref, mask_ref, depth_ref, height_ref, flow_ref, south_ref, north_ref, west_ref, east_ref
):
    levels = low_ref.shape[0]
    rows, columns = mask_ref.shape
    lane = lax.broadcasted_iota(i32, (rows, LANES), 1)
    lasts = jnp.zeros((rows, LANES), f32)
    firsts = jnp.zeros((rows, LANES), f32)
    for p in range(levels):
        south_ref[p : p + 1, :] = low_ref[p, 0:1, :]
        north_ref[p : p + 1, :] = high_ref[p, EDGE - 1 : EDGE, :]
        firsts = jnp.where(lane == p, left_ref[p, :, 0:1], firsts)
        lasts = jnp.where(lane == p, right_ref[p, :, LANES - 1 : LANES], lasts)
    fields = [mask_ref, depth_ref, height_ref, flow_ref.at[0], flow_ref.at[1]]
    for f, ref in enumerate(fields):
        place = slice(levels + f * EDGE, levels + (f + 1) * EDGE)
        south_ref[place, :] = ref[0:EDGE, :].astype(f32)
        north_ref[place, :] = ref[rows - EDGE : rows, :].astype(f32)
        place = slice(f * rows, (f + 1) * rows)
        west_ref[place, :] = ref[:, 0:LANES].astype(f32)
        east_ref[place, :] = ref[:, columns - LANES : columns].astype(f32)
    west_ref[5 * rows : 6 * rows, :] = firsts
    east_ref[5 * rows : 6 * rows, :] = lasts


def edges(planes, mask, depth, height, flow):
    levels, rows, columns = planes.shape
    last_row = rows // EDGE - 1
    last_lane = columns // LANES - 1
    tall = jax.ShapeDtypeStruct((levels + 5 * EDGE, columns), f32)
    thin = jax.ShapeDtypeStruct((6 * rows, LANES), f32)
    return pl.pallas_call(
        edges_kernel,
        name="tile_edges",
        grid=(1,),
        in_specs=[
            pl.BlockSpec((levels, EDGE, columns), lambda i: (0, 0, 0)),
            pl.BlockSpec((levels, EDGE, columns), lambda i: (0, last_row, 0)),
            pl.BlockSpec((levels, rows, LANES), lambda i: (0, 0, 0)),
            pl.BlockSpec((levels, rows, LANES), lambda i: (0, 0, last_lane)),
            whole(mask),
            whole(depth),
            whole(height),
            whole(flow),
        ],
        out_specs=[whole(tall), whole(tall), whole(thin), whole(thin)],
        out_shape=[tall, tall, thin, thin],
        compiler_params=params(56),
        cost_estimate=pl.CostEstimate(flops=1 << 20, bytes_accessed=6 << 20, transcendentals=0),
    )(planes, planes, planes, planes, mask, depth, height, flow)


def beside(array, amount, axis):
    return pltpu.roll(array, amount % array.shape[axis], axis)


def drift(speed, toward):
    return 0.1 + 0.15 * jnp.maximum(-toward * speed, 0.0)


def move_kernel(mask_ref, depth_ref, flow_ref, planes_ref, out_ref, coef_ref, *, per):
    step = pl.program_id(0)
    rows = planes_ref.shape[1]
    columns = planes_ref.shape[2]

    @pl.when(step == 0)
    def _():
        mask = mask_ref[...].astype(f32)
        lane = lax.broadcasted_iota(i32, (rows, columns), 1)
        sub = lax.broadcasted_iota(i32, (rows, columns), 0)
        u = flow_ref[0] / depth_ref[...]
        v = flow_ref[1] / depth_ref[...]
        east = mask * jnp.where(lane == columns - 1, 0.0, beside(mask, -1, 1)) * drift(u, 1.0)
        west = mask * jnp.where(lane == 0, 0.0, beside(mask, 1, 1)) * drift(u, -1.0)
        north = mask * jnp.where(sub == rows - 1, 0.0, beside(mask, -1, 0)) * drift(v, 1.0)
        south = mask * jnp.where(sub == 0, 0.0, beside(mask, 1, 0)) * drift(v, -1.0)
        coef_ref[0] = 1.0 - (east + west + north + south)
        coef_ref[1] = east
        coef_ref[2] = west
        coef_ref[3] = north
        coef_ref[4] = south

    for n in range(per):
        for r in range(0, rows, 8):
            span = slice(r, r + 8)
            q = planes_ref[n, span, :]
            sub = lax.broadcasted_iota(i32, (8, columns), 0)
            east = beside(q, -1, 1)
            west = beside(q, 1, 1)
            below = planes_ref[n, max(r - 1, 0) : max(r - 1, 0) + 1, :]
            above = planes_ref[n, min(r + 8, rows - 1) : min(r + 8, rows - 1) + 1, :]
            north = jnp.where(sub == 7, above, beside(q, -1, 0))
            south = jnp.where(sub == 0, below, beside(q, 1, 0))
            out_ref[n, span, :] = (
                coef_ref[0, span, :] * q
                + coef_ref[1, span, :] * east
                + coef_ref[2, span, :] * west
                + coef_ref[3, span, :] * north
                + coef_ref[4, span, :] * south
            )


def move(mask, depth, flow, planes):
    levels, rows, columns = planes.shape
    per = 4
    return pl.pallas_call(
        functools.partial(move_kernel, per=per),
        name="tracer_move",
        grid=(levels // per,),
        in_specs=[
            whole(mask),
            whole(depth),
            whole(flow),
            pl.BlockSpec((per, rows, columns), lambda i: (i, 0, 0)),
        ],
        out_specs=pl.BlockSpec((per, rows, columns), lambda i: (i, 0, 0)),
        out_shape=jax.ShapeDtypeStruct(planes.shape, f32),
        scratch_shapes=[pltpu.VMEM((5, rows, columns), f32)],
        compiler_params=params(56),
        cost_estimate=pl.CostEstimate(flops=1 << 25, bytes_accessed=18 << 20, transcendentals=0),
    )(mask, depth, flow, planes)


def patch_columns_kernel(west_ref, east_ref, own_west_ref, own_east_ref, moved_ref, out_ref):
    upper = pl.program_id(0) == 1
    levels, rows, _ = moved_ref.shape
    edge = jnp.where(upper, LANES - 1, 0)
    toward = jnp.where(upper, 1.0, -1.0)
    lane = lax.broadcasted_iota(i32, (rows, LANES), 1)
    hit = lane == edge

    def column(field, chosen, low_ref, high_ref):
        place = slice(field * rows, (field + 1) * rows)
        value = jnp.where(upper, high_ref[place, :], low_ref[place, :])
        return jnp.sum(jnp.where(chosen, value, 0.0), axis=1, keepdims=True)

    mask = column(0, hit, own_west_ref, own_east_ref)
    depth = column(1, hit, own_west_ref, own_east_ref)
    flow = column(3, hit, own_west_ref, own_east_ref)
    beyond = column(0, lane == LANES - 1 - edge, west_ref, east_ref)
    coef = mask * beyond * drift(flow / depth, toward)
    place = slice(5 * rows, 6 * rows)
    near = jnp.where(upper, east_ref[place, :], west_ref[place, :])
    own = jnp.where(upper, own_east_ref[place, :], own_west_ref[place, :])
    extra = coef * (near - own)
    for p in range(levels):
        out_ref[p] = moved_ref[p] + jnp.where(hit, extra[:, p : p + 1], 0.0)


def patch_columns(west, east, own_west, own_east, moved):
    levels, rows, columns = moved.shape
    last = columns // LANES - 1
    block = pl.BlockSpec((levels, rows, LANES), lambda i: (0, 0, i * last))
    return pl.pallas_call(
        patch_columns_kernel,
        name="patch_columns",
        grid=(2,),
        in_specs=[whole(west), whole(east), whole(own_west), whole(own_east), block],
        out_specs=block,
        out_shape=jax.ShapeDtypeStruct(moved.shape, f32),
        input_output_aliases={4: 0},
        compiler_params=params(56),
        cost_estimate=pl.CostEstimate(flops=1 << 20, bytes_accessed=4 << 20, transcendentals=0),
    )(west, east, own_west, own_east, moved)


def solve_kernel(
    flux_ref, mask_ref, depth_ref, flow_ref, near_ref, own_ref, moved_ref, out_ref, ratio_ref, *, part, parts, absorb, decay
):
    step = pl.program_id(0)
    at_edge = step == (0 if part == 0 else pl.num_programs(0) - 1)
    run = functools.partial(
        solve_rows, flux_ref, mask_ref, depth_ref, flow_ref, near_ref, own_ref, moved_ref, out_ref, ratio_ref, absorb, decay
    )
    toward = -1.0 if part == 0 else 1.0

    @pl.when(at_edge)
    def _():
        run(toward)

    @pl.when(jnp.logical_not(at_edge))
    def _():
        run(None)


def solve_rows(
    flux_ref, mask_ref, depth_ref, flow_ref, near_ref, own_ref, moved_ref, out_ref, ratio_ref, absorb, decay, toward
):
    levels = moved_ref.shape[1]
    columns = mask_ref.shape[1]
    planes = 2 * levels
    mask = mask_ref[...].astype(f32)
    if toward is not None:
        row = 0 if toward < 0 else EDGE - 1
        other = planes + (EDGE - 1 if toward < 0 else 0)
        line = slice(row, row + 1)
        coef = mask[line] * near_ref[other : other + 1, :] * drift(flow_ref[0, line, :] / depth_ref[line, :], toward)
        hit = lax.broadcasted_iota(i32, (EDGE, columns), 0) == row

    def moved(tracer, k):
        value = moved_ref[tracer, k]
        if toward is not None:
            p = tracer * levels + k
            extra = coef * (near_ref[p : p + 1, :] - own_ref[p : p + 1, :])
            value = value + jnp.where(hit, extra, 0.0)
        return value

    heat_top = 0.5 * mask * flux_ref[0]
    sun = 0.5 * mask * flux_ref[1]
    salt_top = mask * flux_ref[2]
    stir = flux_ref[3]
    base = 0.2 * mask
    stir = 0.5 * mask * (stir * stir)
    above = jnp.zeros_like(mask)
    link = jnp.zeros_like(mask)
    heat_last = None
    salt_last = None
    for k in range(levels):
        heat = moved(0, k) + absorb[k] * sun
        salt = moved(1, k)
        if k == 0:
            heat = heat + heat_top
            salt = salt + salt_top
        below = base + decay[k] * stir if k < levels - 1 else jnp.zeros_like(mask)
        pivot = 1.0 + below + above
        if k > 0:
            pivot = pivot + above * link
            heat = heat + above * heat_last
            salt = salt + above * salt_last
        inverse = 1.0 / pivot
        link = -below * inverse
        heat_last = heat * inverse
        salt_last = salt * inverse
        above = below
        if k < levels - 1:
            ratio_ref[k] = link
        out_ref[0, k] = heat_last
        out_ref[1, k] = salt_last
    for k in range(levels - 2, -1, -1):
        link = ratio_ref[k]
        heat_last = out_ref[0, k] - link * heat_last
        salt_last = out_ref[1, k] - link * salt_last
        out_ref[0, k] = heat_last
        out_ref[1, k] = salt_last


def solve(flux, mask, depth, flow, near, own, moved, part, parts):
    count, levels, rows, columns = moved.shape
    depths = np.arange(levels, dtype=np.float64)
    absorb = tuple(float(a) for a in np.exp(-depths / 3.0) - np.exp(-(depths + 1.0) / 3.0))
    decay = tuple(float(a) for a in np.exp(-depths / 2.0))
    steps = rows // EDGE // parts
    first = part * steps
    line = pl.BlockSpec((EDGE, columns), lambda i: (first + i, 0))
    return pl.pallas_call(
        functools.partial(solve_kernel, part=part, parts=parts, absorb=absorb, decay=decay),
        name=f"column_solve_{part}",
        grid=(steps,),
        in_specs=[
            pl.BlockSpec((4, EDGE, columns), lambda i: (0, first + i, 0)),
            line,
            line,
            pl.BlockSpec((1, EDGE, columns), lambda i: (1, first + i, 0)),
            whole(near),
            whole(own),
            pl.BlockSpec((count, levels, EDGE, columns), lambda i: (0, 0, first + i, 0)),
        ],
        out_specs=pl.BlockSpec((count, levels, EDGE, columns), lambda i: (0, 0, first + i, 0)),
        out_shape=jax.ShapeDtypeStruct(moved.shape, f32),
        scratch_shapes=[pltpu.VMEM((levels, EDGE, columns), f32)],
        input_output_aliases={6: 0},
        compiler_params=params(56),
        cost_estimate=pl.CostEstimate(flops=1 << 24, bytes_accessed=9 << 20, transcendentals=0),
    )(flux, mask, depth, flow, near, own, moved)


def sides_kernel(left_ref, right_ref, south_ref, north_ref, low_ref, high_ref, west_ref, east_ref):
    rows = left_ref.shape[1]
    columns = south_ref.shape[2]
    levels = low_ref.shape[0] - 5 * EDGE
    tall = rows + 2 * EDGE
    for ref, part_ref, lanes in (
        (west_ref, left_ref, slice(0, LANES)),
        (east_ref, right_ref, slice(columns - LANES, columns)),
    ):
        for f in range(4):
            start = f * tall
            ref[start : start + EDGE, :] = south_ref[f, :, lanes]
            ref[start + EDGE : start + EDGE + rows, :] = part_ref[f]
            ref[start + EDGE + rows : start + tall, :] = north_ref[f, :, lanes]
        for f in range(5):
            start = 4 * tall + 2 * EDGE * f
            place = slice(levels + f * EDGE, levels + (f + 1) * EDGE)
            ref[start : start + EDGE, :] = low_ref[place, lanes]
            ref[start + EDGE : start + 2 * EDGE, :] = high_ref[place, lanes]


def sides(winds, south, north, low, high):
    _, rows, columns = winds.shape
    last = columns // LANES - 1
    shape = jax.ShapeDtypeStruct((4 * (rows + 2 * EDGE) + 10 * EDGE, LANES), f32)
    return pl.pallas_call(
        sides_kernel,
        name="tile_sides",
        grid=(1,),
        in_specs=[
            pl.BlockSpec((4, rows, LANES), lambda i: (0, 0, 0)),
            pl.BlockSpec((4, rows, LANES), lambda i: (0, 0, last)),
            whole(south),
            whole(north),
            whole(low),
            whole(high),
        ],
        out_specs=[whole(shape), whole(shape)],
        out_shape=[shape, shape],
        compiler_params=params(16),
        cost_estimate=pl.CostEstimate(flops=1 << 16, bytes_accessed=2 << 20, transcendentals=0),
    )(winds, winds, south, north, low, high)


def barotropic_kernel(
    mask_ref, depth_ref, begin_ref, stream_ref, low_ref, high_ref, left_ref, right_ref,
    flux_ref, south_ref, north_ref, west_ref, east_ref, height_ref, flow_ref, wide_ref,
):
    rows, columns = begin_ref.shape
    levels = low_ref.shape[0] - 5 * EDGE
    tall = rows + 2 * EDGE
    middle = slice(EDGE, EDGE + rows)

    def merge(low, high):
        lane = lax.broadcasted_iota(i32, low.shape, 1)
        return jnp.where(lane < LANES // 2, high, low)

    for f, ref in enumerate([mask_ref, depth_ref, begin_ref, stream_ref.at[0], stream_ref.at[1]]):
        place = slice(levels + f * EDGE, levels + (f + 1) * EDGE)
        wide_ref[f, 0:EDGE, 0:columns] = low_ref[place, :]
        wide_ref[f, middle, 0:columns] = ref[...].astype(f32)
        wide_ref[f, EDGE + rows : tall, 0:columns] = high_ref[place, :]
        place = slice(f * rows, (f + 1) * rows)
        wide_ref[f, middle, columns : columns + LANES] = merge(left_ref[place, :], right_ref[place, :])
        start = 4 * tall + 2 * EDGE * f
        corner = merge(west_ref[start : start + 2 * EDGE, :], east_ref[start : start + 2 * EDGE, :])
        wide_ref[f, 0:EDGE, columns : columns + LANES] = corner[0:EDGE]
        wide_ref[f, EDGE + rows : tall, columns : columns + LANES] = corner[EDGE : 2 * EDGE]
    for f in range(4):
        wide_ref[5 + f, 0:EDGE, 0:columns] = south_ref[f]
        wide_ref[5 + f, middle, 0:columns] = flux_ref[f]
        wide_ref[5 + f, EDGE + rows : tall, 0:columns] = north_ref[f]
        place = slice(f * tall, (f + 1) * tall)
        wide_ref[5 + f, :, columns : columns + LANES] = merge(west_ref[place, :], east_ref[place, :])
    mask = wide_ref[0]
    drag = -0.5 * wide_ref[1]
    height = wide_ref[2]
    along = wide_ref[3]
    across = wide_ref[4]
    wind_x = 0.5 * wide_ref[5]
    wind_y = 0.5 * wide_ref[6]
    push = 0.5 * wide_ref[7]
    source = wide_ref[8]
    for k in range(SUB):
        level = mask * (height + push)
        along = mask * (0.95 * along + drag * (beside(level, -1, 1) - beside(level, 1, 1)) + wind_x)
        across = mask * (0.95 * across + drag * (beside(level, -1, 0) - beside(level, 1, 0)) + wind_y)
        spread_out = beside(along, -1, 1) - beside(along, 1, 1) + beside(across, -1, 0) - beside(across, 1, 0)
        height = mask * (height - 0.5 * spread_out + source)
    height_ref[...] = height[middle, :columns]
    flow_ref[0] = along[middle, :columns]
    flow_ref[1] = across[middle, :columns]


def barotropic(*arrays):
    rows, columns = arrays[2].shape
    outs = [jax.ShapeDtypeStruct((rows, columns), f32), jax.ShapeDtypeStruct((2, rows, columns), f32)]
    return pl.pallas_call(
        barotropic_kernel,
        name="barotropic",
        grid=(1,),
        in_specs=[whole(array) for array in arrays],
        out_specs=[whole(out) for out in outs],
        out_shape=outs,
        scratch_shapes=[pltpu.VMEM((9, rows + 2 * EDGE, columns + LANES), f32)],
        compiler_params=params(32),
        cost_estimate=pl.CostEstimate(flops=1 << 24, bytes_accessed=6 << 20, transcendentals=0),
    )(*arrays)


def to_next(array, axes):
    ends = lax.axis_size(axes) - 1
    return lax.ppermute(array, axes, [(i, i + 1) for i in range(ends)])


def to_previous(array, axes):
    ends = lax.axis_size(axes) - 1
    return lax.ppermute(array, axes, [(i + 1, i) for i in range(ends)])


def all_to_all(array):
    return lax.all_to_all(array, EVERY, split_axis=0, concat_axis=0, tiled=True)


def local(
    atm_flux,
    margin_source,
    margin_cell,
    margin_weight,
    margin_tile,
    land_mask,
    sea_depth,
    sea_height,
    transport,
    tracers,
):
    tiles = lax.axis_size(EVERY)
    count, levels, rows, columns = tracers.shape
    packed = pack(
        margin_tile.reshape(-1), atm_flux, margin_source, margin_cell, margin_weight, tiles, rows * columns
    )
    packed, land_mask, sea_depth, sea_height, transport, tracers = lax.optimization_barrier(
        (packed, land_mask, sea_depth, sea_height, transport, tracers)
    )
    arrived = all_to_all(packed)

    planes = tracers.reshape(count * levels, rows, columns)
    own_south, own_north, own_west, own_east = edges(planes, land_mask, sea_depth, sea_height, transport)
    from_west = to_next(own_east, "tx")
    from_east = to_previous(own_west, "tx")
    from_south = to_next(own_north, ROWS)
    from_north = to_previous(own_south, ROWS)
    moved = move(land_mask, sea_depth, transport, planes)
    moved = patch_columns(from_west, from_east, own_west, own_east, moved).reshape(tracers.shape)
    arrived, moved = lax.optimization_barrier((arrived, moved))

    winds, heats, flux_low, flux_high = spread(arrived, rows, columns)
    flux_south = to_next(flux_high, ROWS)
    flux_north = to_previous(flux_low, ROWS)
    moved = solve(heats, land_mask, sea_depth, transport, from_south, own_south, moved, 0, 2)
    flux_south, flux_north, moved = lax.optimization_barrier((flux_south, flux_north, moved))
    side_west, side_east = sides(winds, flux_south, flux_north, from_south, from_north)
    flux_west = to_next(side_east, "tx")
    flux_east = to_previous(side_west, "tx")
    solved = solve(heats, land_mask, sea_depth, transport, from_north, own_north, moved, 1, 2)
    flux_west, flux_east, solved = lax.optimization_barrier((flux_west, flux_east, solved))
    new_height, new_transport = barotropic(
        land_mask, sea_depth, sea_height, transport, from_south, from_north, from_west, from_east,
        winds, flux_south, flux_north, flux_west, flux_east,
    )
    return new_height, new_transport, solved


def solution(mesh):
    in_specs = (
        P(None, EVERY),
        P(EVERY, None),
        P(EVERY, None),
        P(EVERY, None),
        P(EVERY, None),
        P(ROWS, "tx"),
        P(ROWS, "tx"),
        P(ROWS, "tx"),
        P(None, ROWS, "tx"),
        P(None, None, ROWS, "tx"),
    )
    out_specs = (P(ROWS, "tx"), P(None, ROWS, "tx"), P(None, None, ROWS, "tx"))
    return jax.shard_map(local, mesh=mesh, in_specs=in_specs, out_specs=out_specs, check_vma=False)
```

```python
import functools

import jax
import jax.numpy as jnp
import numpy as np
from jax import lax
from jax.experimental import pallas as pl
from jax.experimental.pallas import tpu as pltpu
from jax.sharding import PartitionSpec as P

SUB = 3
EDGE = 8
LANES = 128
EVERY = ("comp", "ty", "tx")
ROWS = ("comp", "ty")
f32 = jnp.float32
i32 = jnp.int32
VM = pl.BlockSpec(memory_space=pltpu.VMEM)
SM = pl.BlockSpec(memory_space=pltpu.SMEM)


def params(mib):
    return pltpu.CompilerParams(vmem_limit_bytes=mib << 20)


def whole(array):
    return pl.BlockSpec(array.shape, lambda i: (0,) * array.ndim)


def pack_kernel(tile_ref, flux_ref, source_ref, cell_ref, weight_ref, out_ref, count_ref, *, beyond):
    blocks = source_ref.shape[0]
    tiles = out_ref.shape[0]
    group = 4
    nowhere = jnp.full((4, LANES), beyond, f32)

    def clear(t, carry):
        count_ref[t] = 0
        out_ref[t, 8] = nowhere
        return carry

    lax.fori_loop(0, tiles, clear, 0, unroll=True)
    sub = lax.broadcasted_iota(i32, (8, LANES), 0)

    def step(i, carry):
        for g in range(group):
            w = i * group + g
            x = flux_ref[:, pl.ds(pl.multiple_of(w * LANES, LANES), LANES)]
            after = pltpu.roll(x, 1, 0)
            six = pltpu.roll(x, 5, 0)
            five = pltpu.roll(x, 6, 0)
            y = jnp.where((sub == 4) | (sub == 5), after, x)
            y = jnp.where(sub == 6, 0.5 * after - 0.3 * x, y)
            y = jnp.where(sub == 3, 0.1 * (six - five), y)
            for half in range(2):
                b = 2 * w + half
                tile = tile_ref[b]
                slot = count_ref[tile]
                count_ref[tile] = slot + 1
                index = jnp.broadcast_to(source_ref[pl.ds(b, 1), :], (8, LANES))
                picked = jnp.take_along_axis(y, index, axis=1)
                value = picked * jnp.broadcast_to(weight_ref[pl.ds(b, 1), :], (8, LANES))
                out_ref[tile, slot] = value[0:4]
                out_ref[tile, 4 + slot] = value[4:8]
                out_ref[tile, 8, pl.ds(slot, 1), :] = cell_ref[pl.ds(b, 1), :].astype(f32)
        return carry

    lax.fori_loop(0, blocks // (2 * group), step, 0)


def pack(tile, flux, source, cell, weight, tiles, beyond):
    return pl.pallas_call(
        functools.partial(pack_kernel, beyond=beyond),
        name="pack_margin",
        grid=(1,),
        in_specs=[SM, whole(flux), whole(source), whole(cell), whole(weight)],
        out_specs=pl.BlockSpec((tiles, 9, 4, LANES), lambda i: (0, 0, 0, 0)),
        out_shape=jax.ShapeDtypeStruct((tiles, 9, 4, LANES), f32),
        scratch_shapes=[pltpu.SMEM((tiles,), i32)],
        compiler_params=params(56),
        cost_estimate=pl.CostEstimate(flops=1 << 22, bytes_accessed=4 << 20, transcendentals=0),
    )(tile, flux, source, cell, weight)


def spread_kernel(load_ref, winds_ref, heats_ref, south_ref, north_ref, acc_ref, *, group):
    _, rows, columns = winds_ref.shape
    fields = 8
    high = columns // LANES
    depth = fields * high
    def clear(i, c):
        acc_ref[pl.ds(pl.multiple_of(i * 256, 256), 256),:] = jnp.zeros((256, LANES), f32)
        return c
    @pl.when(pl.program_id(0) == 0)
    def _():
        lax.fori_loop(0, rows * depth // 256, clear, 0)

    low_iota = lax.broadcasted_iota(i32, (LANES, LANES), 0).astype(f32).astype(jnp.bfloat16)
    pattern = [
        (2 * i + (lax.broadcasted_iota(i32, (16, LANES), 0) >> 3)).astype(f32).astype(jnp.bfloat16) for i in range(high // 2)
    ]
    zero16 = jnp.zeros((16, LANES), jnp.bfloat16)
    one = jnp.ones((LANES, LANES), jnp.bfloat16)
    zero = jnp.zeros((LANES, LANES), jnp.bfloat16)

    for s in range(group):
        cells = load_ref[s, 8].astype(i32)
        highs = ((cells & (columns - 1)) >> 7).astype(f32)
        lows = (cells & (LANES - 1)).astype(f32)
        for k in range(4):
            value = jnp.concatenate([load_ref[s, k], load_ref[s, 4 + k]], axis=0)
            coarse = value.astype(jnp.bfloat16).astype(f32)
            fine = value - coarse
            coarse = jnp.concatenate([coarse, coarse], axis=0).astype(jnp.bfloat16)
            fine = jnp.concatenate([fine, fine], axis=0).astype(jnp.bfloat16)
            hk = jnp.broadcast_to(highs[k : k + 1], (16, LANES)).astype(jnp.bfloat16)
            lk = jnp.broadcast_to(lows[k : k + 1], (16, LANES)).astype(jnp.bfloat16)
            lk = jnp.concatenate([lk] * (LANES // 16), axis=0)
            left = []
            right = []
            for p in pattern:
                hit = hk == p
                left.append(jnp.where(hit, coarse, zero16))
                right.append(jnp.where(hit, fine, zero16))
            lhs = jnp.concatenate([jnp.concatenate(left, axis=0), jnp.concatenate(right, axis=0)], axis=1)
            onehot = jnp.where(lk == low_iota, one, zero)
            rhs = jnp.concatenate([onehot, onehot], axis=1)
            both = lax.dot_general(lhs, rhs, (((1,), (1,)), ((), ())), preferred_element_type=f32)
            row = cells[k, 0] >> (columns.bit_length() - 1)
            place = pl.ds(pl.multiple_of(row * depth, depth), depth)
            acc_ref[place, :] += both

    def turn(i, carry):
        r = pl.multiple_of(i * 8, 8)
        block = acc_ref[pl.ds(pl.multiple_of(r * depth, 8 * depth), 8 * depth), :].reshape(8, depth, LANES)
        for h in range(high):
            piece = jnp.swapaxes(block[:, h * 8 : h * 8 + 8, :], 0, 1)
            for f in range(fields):
                ref = winds_ref if f < 4 else heats_ref
                ref[f % 4, pl.ds(r, 8), h * LANES : (h + 1) * LANES] = piece[f]
        return carry

    @pl.when(pl.program_id(0) == pl.num_programs(0) - 1)
    def _():
        lax.fori_loop(0, rows // 8, turn, 0)
        south_ref[...] = winds_ref[:, 0:EDGE, :]
        north_ref[...] = winds_ref[:, rows - EDGE : rows, :]


def spread(load, rows, columns):
    depth = 8 * columns // LANES
    sources = load.shape[0]
    group = 16 if sources % 16 == 0 else 1
    outs = [
        jax.ShapeDtypeStruct((4, rows, columns), f32),
        jax.ShapeDtypeStruct((4, rows, columns), f32),
        jax.ShapeDtypeStruct((4, EDGE, columns), f32),
        jax.ShapeDtypeStruct((4, EDGE, columns), f32),
    ]
    return pl.pallas_call(
        functools.partial(spread_kernel, group=group),
        name="spread_all",
        grid=(sources // group,),
        in_specs=[pl.BlockSpec((group, *load.shape[1:]), lambda i: (i, 0, 0, 0))],
        out_specs=[whole(out) for out in outs],
        out_shape=outs,
        scratch_shapes=[pltpu.VMEM(((rows + 1) * depth, LANES), f32)],
        compiler_params=params(24),
        cost_estimate=pl.CostEstimate(flops=1 << 30, bytes_accessed=4 << 20, transcendentals=0),
    )(load)


def edges_kernel(
    low_ref, high_ref, left_ref, right_ref, mask_ref, depth_ref, height_ref, flow_ref, south_ref, north_ref, west_ref, east_ref
):
    levels = low_ref.shape[0]
    rows, columns = mask_ref.shape
    lane = lax.broadcasted_iota(i32, (rows, LANES), 1)
    lasts = jnp.zeros((rows, LANES), f32)
    firsts = jnp.zeros((rows, LANES), f32)
    for p in range(levels):
        south_ref[p : p + 1, :] = low_ref[p, 0:1, :]
        north_ref[p : p + 1, :] = high_ref[p, EDGE - 1 : EDGE, :]
        firsts = jnp.where(lane == p, left_ref[p, :, 0:1], firsts)
        lasts = jnp.where(lane == p, right_ref[p, :, LANES - 1 : LANES], lasts)
    fields = [mask_ref, depth_ref, height_ref, flow_ref.at[0], flow_ref.at[1]]
    for f, ref in enumerate(fields):
        place = slice(levels + f * EDGE, levels + (f + 1) * EDGE)
        south_ref[place, :] = ref[0:EDGE, :].astype(f32)
        north_ref[place, :] = ref[rows - EDGE : rows, :].astype(f32)
        place = slice(f * rows, (f + 1) * rows)
        west_ref[place, :] = ref[:, 0:LANES].astype(f32)
        east_ref[place, :] = ref[:, columns - LANES : columns].astype(f32)
    west_ref[5 * rows : 6 * rows, :] = firsts
    east_ref[5 * rows : 6 * rows, :] = lasts


def edges(planes, mask, depth, height, flow):
    levels, rows, columns = planes.shape
    last_row = rows // EDGE - 1
    last_lane = columns // LANES - 1
    tall = jax.ShapeDtypeStruct((levels + 5 * EDGE, columns), f32)
    thin = jax.ShapeDtypeStruct((6 * rows, LANES), f32)
    return pl.pallas_call(
        edges_kernel,
        name="tile_edges",
        grid=(1,),
        in_specs=[
            pl.BlockSpec((levels, EDGE, columns), lambda i: (0, 0, 0)),
            pl.BlockSpec((levels, EDGE, columns), lambda i: (0, last_row, 0)),
            pl.BlockSpec((levels, rows, LANES), lambda i: (0, 0, 0)),
            pl.BlockSpec((levels, rows, LANES), lambda i: (0, 0, last_lane)),
            whole(mask),
            whole(depth),
            whole(height),
            whole(flow),
        ],
        out_specs=[whole(tall), whole(tall), whole(thin), whole(thin)],
        out_shape=[tall, tall, thin, thin],
        compiler_params=params(56),
        cost_estimate=pl.CostEstimate(flops=1 << 20, bytes_accessed=6 << 20, transcendentals=0),
    )(planes, planes, planes, planes, mask, depth, height, flow)


def beside(array, amount, axis):
    return pltpu.roll(array, amount % array.shape[axis], axis)


def drift(speed, toward):
    return 0.1 + 0.15 * jnp.maximum(-toward * speed, 0.0)


def move_kernel(mask_ref, depth_ref, flow_ref, planes_ref, out_ref, coef_ref, *, per):
    step = pl.program_id(0)
    rows = planes_ref.shape[1]
    columns = planes_ref.shape[2]

    @pl.when(step == 0)
    def _():
        mask = mask_ref[...].astype(f32)
        lane = lax.broadcasted_iota(i32, (rows, columns), 1)
        sub = lax.broadcasted_iota(i32, (rows, columns), 0)
        u = flow_ref[0] / depth_ref[...]
        v = flow_ref[1] / depth_ref[...]
        east = mask * jnp.where(lane == columns - 1, 0.0, beside(mask, -1, 1)) * drift(u, 1.0)
        west = mask * jnp.where(lane == 0, 0.0, beside(mask, 1, 1)) * drift(u, -1.0)
        north = mask * jnp.where(sub == rows - 1, 0.0, beside(mask, -1, 0)) * drift(v, 1.0)
        south = mask * jnp.where(sub == 0, 0.0, beside(mask, 1, 0)) * drift(v, -1.0)
        coef_ref[0] = 1.0 - (east + west + north + south)
        coef_ref[1] = east
        coef_ref[2] = west
        coef_ref[3] = north
        coef_ref[4] = south

    for n in range(per):
        for r in range(0, rows, 8):
            span = slice(r, r + 8)
            q = planes_ref[n, span, :]
            sub = lax.broadcasted_iota(i32, (8, columns), 0)
            east = beside(q, -1, 1)
            west = beside(q, 1, 1)
            below = planes_ref[n, max(r - 1, 0) : max(r - 1, 0) + 1, :]
            above = planes_ref[n, min(r + 8, rows - 1) : min(r + 8, rows - 1) + 1, :]
            north = jnp.where(sub == 7, above, beside(q, -1, 0))
            south = jnp.where(sub == 0, below, beside(q, 1, 0))
            out_ref[n, span, :] = (
                coef_ref[0, span, :] * q
                + coef_ref[1, span, :] * east
                + coef_ref[2, span, :] * west
                + coef_ref[3, span, :] * north
                + coef_ref[4, span, :] * south
            )


def move(mask, depth, flow, planes):
    levels, rows, columns = planes.shape
    per = 4
    return pl.pallas_call(
        functools.partial(move_kernel, per=per),
        name="tracer_move",
        grid=(levels // per,),
        in_specs=[
            whole(mask),
            whole(depth),
            whole(flow),
            pl.BlockSpec((per, rows, columns), lambda i: (i, 0, 0)),
        ],
        out_specs=pl.BlockSpec((per, rows, columns), lambda i: (i, 0, 0)),
        out_shape=jax.ShapeDtypeStruct(planes.shape, f32),
        scratch_shapes=[pltpu.VMEM((5, rows, columns), f32)],
        compiler_params=params(56),
        cost_estimate=pl.CostEstimate(flops=1 << 25, bytes_accessed=18 << 20, transcendentals=0),
    )(mask, depth, flow, planes)


def patch_columns_kernel(west_ref, east_ref, own_west_ref, own_east_ref, moved_ref, out_ref):
    upper = pl.program_id(0) == 1
    levels, rows, _ = moved_ref.shape
    edge = jnp.where(upper, LANES - 1, 0)
    toward = jnp.where(upper, 1.0, -1.0)
    lane = lax.broadcasted_iota(i32, (rows, LANES), 1)
    hit = lane == edge

    def column(field, chosen, low_ref, high_ref):
        place = slice(field * rows, (field + 1) * rows)
        value = jnp.where(upper, high_ref[place, :], low_ref[place, :])
        return jnp.sum(jnp.where(chosen, value, 0.0), axis=1, keepdims=True)

    mask = column(0, hit, own_west_ref, own_east_ref)
    depth = column(1, hit, own_west_ref, own_east_ref)
    flow = column(3, hit, own_west_ref, own_east_ref)
    beyond = column(0, lane == LANES - 1 - edge, west_ref, east_ref)
    coef = mask * beyond * drift(flow / depth, toward)
    place = slice(5 * rows, 6 * rows)
    near = jnp.where(upper, east_ref[place, :], west_ref[place, :])
    own = jnp.where(upper, own_east_ref[place, :], own_west_ref[place, :])
    extra = coef * (near - own)
    for p in range(levels):
        out_ref[p] = moved_ref[p] + jnp.where(hit, extra[:, p : p + 1], 0.0)


def patch_columns(west, east, own_west, own_east, moved):
    levels, rows, columns = moved.shape
    last = columns // LANES - 1
    block = pl.BlockSpec((levels, rows, LANES), lambda i: (0, 0, i * last))
    return pl.pallas_call(
        patch_columns_kernel,
        name="patch_columns",
        grid=(2,),
        in_specs=[whole(west), whole(east), whole(own_west), whole(own_east), block],
        out_specs=block,
        out_shape=jax.ShapeDtypeStruct(moved.shape, f32),
        input_output_aliases={4: 0},
        compiler_params=params(40),
        cost_estimate=pl.CostEstimate(flops=1 << 20, bytes_accessed=4 << 20, transcendentals=0),
    )(west, east, own_west, own_east, moved)


def solve_kernel(
    flux_ref, mask_ref, depth_ref, flow_ref, near_ref, own_ref, moved_ref, out_ref, ratio_ref, *, part, parts, absorb, decay
):
    step = pl.program_id(0)
    at_edge = step == (0 if part == 0 else pl.num_programs(0) - 1)
    run = functools.partial(
        solve_rows, flux_ref, mask_ref, depth_ref, flow_ref, near_ref, own_ref, moved_ref, out_ref, ratio_ref, absorb, decay
    )
    toward = -1.0 if part == 0 else 1.0

    @pl.when(at_edge)
    def _():
        run(toward)

    @pl.when(jnp.logical_not(at_edge))
    def _():
        run(None)


def solve_rows(
    flux_ref, mask_ref, depth_ref, flow_ref, near_ref, own_ref, moved_ref, out_ref, ratio_ref, absorb, decay, toward
):
    levels = moved_ref.shape[1]
    columns = mask_ref.shape[1]
    planes = 2 * levels
    mask = mask_ref[...].astype(f32)
    if toward is not None:
        row = 0 if toward < 0 else EDGE - 1
        other = planes + (EDGE - 1 if toward < 0 else 0)
        line = slice(row, row + 1)
        coef = mask[line] * near_ref[other : other + 1, :] * drift(flow_ref[0, line, :] / depth_ref[line, :], toward)
        hit = lax.broadcasted_iota(i32, (EDGE, columns), 0) == row

    def moved(tracer, k):
        value = moved_ref[tracer, k]
        if toward is not None:
            p = tracer * levels + k
            extra = coef * (near_ref[p : p + 1, :] - own_ref[p : p + 1, :])
            value = value + jnp.where(hit, extra, 0.0)
        return value

    heat_top = 0.5 * mask * flux_ref[0]
    sun = 0.5 * mask * flux_ref[1]
    salt_top = mask * flux_ref[2]
    stir = flux_ref[3]
    base = 0.2 * mask
    stir = 0.5 * mask * (stir * stir)
    above = jnp.zeros_like(mask)
    link = jnp.zeros_like(mask)
    heat_last = None
    salt_last = None
    for k in range(levels):
        heat = moved(0, k) + absorb[k] * sun
        salt = moved(1, k)
        if k == 0:
            heat = heat + heat_top
            salt = salt + salt_top
        below = base + decay[k] * stir if k < levels - 1 else jnp.zeros_like(mask)
        pivot = 1.0 + below + above
        if k > 0:
            pivot = pivot + above * link
            heat = heat + above * heat_last
            salt = salt + above * salt_last
        inverse = 1.0 / pivot
        link = -below * inverse
        heat_last = heat * inverse
        salt_last = salt * inverse
        above = below
        if k < levels - 1:
            ratio_ref[k] = link
        out_ref[0, k] = heat_last
        out_ref[1, k] = salt_last
    for k in range(levels - 2, -1, -1):
        link = ratio_ref[k]
        heat_last = out_ref[0, k] - link * heat_last
        salt_last = out_ref[1, k] - link * salt_last
        out_ref[0, k] = heat_last
        out_ref[1, k] = salt_last


def solve(flux, mask, depth, flow, near, own, moved, part, parts):
    count, levels, rows, columns = moved.shape
    depths = np.arange(levels, dtype=np.float64)
    absorb = tuple(float(a) for a in np.exp(-depths / 3.0) - np.exp(-(depths + 1.0) / 3.0))
    decay = tuple(float(a) for a in np.exp(-depths / 2.0))
    steps = rows // EDGE // parts
    first = part * steps
    line = pl.BlockSpec((EDGE, columns), lambda i: (first + i, 0))
    return pl.pallas_call(
        functools.partial(solve_kernel, part=part, parts=parts, absorb=absorb, decay=decay),
        name=f"column_solve_{part}",
        grid=(steps,),
        in_specs=[
            pl.BlockSpec((4, EDGE, columns), lambda i: (0, first + i, 0)),
            line,
            line,
            pl.BlockSpec((1, EDGE, columns), lambda i: (1, first + i, 0)),
            whole(near),
            whole(own),
            pl.BlockSpec((count, levels, EDGE, columns), lambda i: (0, 0, first + i, 0)),
        ],
        out_specs=pl.BlockSpec((count, levels, EDGE, columns), lambda i: (0, 0, first + i, 0)),
        out_shape=jax.ShapeDtypeStruct(moved.shape, f32),
        scratch_shapes=[pltpu.VMEM((levels, EDGE, columns), f32)],
        input_output_aliases={6: 0},
        compiler_params=params(48),
        cost_estimate=pl.CostEstimate(flops=1 << 24, bytes_accessed=9 << 20, transcendentals=0),
    )(flux, mask, depth, flow, near, own, moved)


def sides_kernel(left_ref, right_ref, south_ref, north_ref, low_ref, high_ref, west_ref, east_ref):
    rows = left_ref.shape[1]
    columns = south_ref.shape[2]
    levels = low_ref.shape[0] - 5 * EDGE
    tall = rows + 2 * EDGE
    for ref, part_ref, lanes in (
        (west_ref, left_ref, slice(0, LANES)),
        (east_ref, right_ref, slice(columns - LANES, columns)),
    ):
        for f in range(4):
            start = f * tall
            ref[start : start + EDGE, :] = south_ref[f, :, lanes]
            ref[start + EDGE : start + EDGE + rows, :] = part_ref[f]
            ref[start + EDGE + rows : start + tall, :] = north_ref[f, :, lanes]
        for f in range(5):
            start = 4 * tall + 2 * EDGE * f
            place = slice(levels + f * EDGE, levels + (f + 1) * EDGE)
            ref[start : start + EDGE, :] = low_ref[place, lanes]
            ref[start + EDGE : start + 2 * EDGE, :] = high_ref[place, lanes]


def sides(winds, south, north, low, high):
    _, rows, columns = winds.shape
    last = columns // LANES - 1
    shape = jax.ShapeDtypeStruct((4 * (rows + 2 * EDGE) + 10 * EDGE, LANES), f32)
    return pl.pallas_call(
        sides_kernel,
        name="tile_sides",
        grid=(1,),
        in_specs=[
            pl.BlockSpec((4, rows, LANES), lambda i: (0, 0, 0)),
            pl.BlockSpec((4, rows, LANES), lambda i: (0, 0, last)),
            whole(south),
            whole(north),
            whole(low),
            whole(high),
        ],
        out_specs=[whole(shape), whole(shape)],
        out_shape=[shape, shape],
        compiler_params=params(16),
        cost_estimate=pl.CostEstimate(flops=1 << 16, bytes_accessed=2 << 20, transcendentals=0),
    )(winds, winds, south, north, low, high)


def barotropic_kernel(
    mask_ref, depth_ref, begin_ref, stream_ref, low_ref, high_ref, left_ref, right_ref,
    flux_ref, south_ref, north_ref, west_ref, east_ref, height_ref, flow_ref, wide_ref,
):
    rows, columns = begin_ref.shape
    levels = low_ref.shape[0] - 5 * EDGE
    tall = rows + 2 * EDGE
    middle = slice(EDGE, EDGE + rows)

    def merge(low, high):
        lane = lax.broadcasted_iota(i32, low.shape, 1)
        return jnp.where(lane < LANES // 2, high, low)

    for f, ref in enumerate([mask_ref, depth_ref, begin_ref, stream_ref.at[0], stream_ref.at[1]]):
        place = slice(levels + f * EDGE, levels + (f + 1) * EDGE)
        wide_ref[f, 0:EDGE, 0:columns] = low_ref[place, :]
        wide_ref[f, middle, 0:columns] = ref[...].astype(f32)
        wide_ref[f, EDGE + rows : tall, 0:columns] = high_ref[place, :]
        place = slice(f * rows, (f + 1) * rows)
        wide_ref[f, middle, columns : columns + LANES] = merge(left_ref[place, :], right_ref[place, :])
        start = 4 * tall + 2 * EDGE * f
        corner = merge(west_ref[start : start + 2 * EDGE, :], east_ref[start : start + 2 * EDGE, :])
        wide_ref[f, 0:EDGE, columns : columns + LANES] = corner[0:EDGE]
        wide_ref[f, EDGE + rows : tall, columns : columns + LANES] = corner[EDGE : 2 * EDGE]
    for f in range(4):
        wide_ref[5 + f, 0:EDGE, 0:columns] = south_ref[f]
        wide_ref[5 + f, middle, 0:columns] = flux_ref[f]
        wide_ref[5 + f, EDGE + rows : tall, 0:columns] = north_ref[f]
        place = slice(f * tall, (f + 1) * tall)
        wide_ref[5 + f, :, columns : columns + LANES] = merge(west_ref[place, :], east_ref[place, :])
    mask = wide_ref[0]
    drag = -0.5 * wide_ref[1]
    height = wide_ref[2]
    along = wide_ref[3]
    across = wide_ref[4]
    wind_x = 0.5 * wide_ref[5]
    wind_y = 0.5 * wide_ref[6]
    push = 0.5 * wide_ref[7]
    source = wide_ref[8]
    for k in range(SUB):
        level = mask * (height + push)
        along = mask * (0.95 * along + drag * (beside(level, -1, 1) - beside(level, 1, 1)) + wind_x)
        across = mask * (0.95 * across + drag * (beside(level, -1, 0) - beside(level, 1, 0)) + wind_y)
        spread_out = beside(along, -1, 1) - beside(along, 1, 1) + beside(across, -1, 0) - beside(across, 1, 0)
        height = mask * (height - 0.5 * spread_out + source)
    height_ref[...] = height[middle, :columns]
    flow_ref[0] = along[middle, :columns]
    flow_ref[1] = across[middle, :columns]


def barotropic(*arrays):
    rows, columns = arrays[2].shape
    outs = [jax.ShapeDtypeStruct((rows, columns), f32), jax.ShapeDtypeStruct((2, rows, columns), f32)]
    return pl.pallas_call(
        barotropic_kernel,
        name="barotropic",
        grid=(1,),
        in_specs=[whole(array) for array in arrays],
        out_specs=[whole(out) for out in outs],
        out_shape=outs,
        scratch_shapes=[pltpu.VMEM((9, rows + 2 * EDGE, columns + LANES), f32)],
        compiler_params=params(32),
        cost_estimate=pl.CostEstimate(flops=1 << 24, bytes_accessed=6 << 20, transcendentals=0),
    )(*arrays)


def to_next(array, axes):
    ends = lax.axis_size(axes) - 1
    return lax.ppermute(array, axes, [(i, i + 1) for i in range(ends)])


def to_previous(array, axes):
    ends = lax.axis_size(axes) - 1
    return lax.ppermute(array, axes, [(i + 1, i) for i in range(ends)])


def all_to_all(array):
    return lax.all_to_all(array, EVERY, split_axis=0, concat_axis=0, tiled=True)


def local(
    atm_flux,
    margin_source,
    margin_cell,
    margin_weight,
    margin_tile,
    land_mask,
    sea_depth,
    sea_height,
    transport,
    tracers,
):
    tiles = lax.axis_size(EVERY)
    count, levels, rows, columns = tracers.shape
    packed = pack(
        margin_tile.reshape(-1), atm_flux, margin_source, margin_cell, margin_weight, tiles, rows * columns
    )
    packed, land_mask, sea_depth, sea_height, transport, tracers = lax.optimization_barrier(
        (packed, land_mask, sea_depth, sea_height, transport, tracers)
    )
    arrived = all_to_all(packed)

    planes = tracers.reshape(count * levels, rows, columns)
    own_south, own_north, own_west, own_east = edges(planes, land_mask, sea_depth, sea_height, transport)
    from_west = to_next(own_east, "tx")
    from_east = to_previous(own_west, "tx")
    moved = move(land_mask, sea_depth, transport, planes)
    moved = patch_columns(from_west, from_east, own_west, own_east, moved).reshape(tracers.shape)
    own_south, own_north, moved = lax.optimization_barrier((own_south, own_north, moved))
    from_south = to_next(own_north, ROWS)
    from_north = to_previous(own_south, ROWS)
    arrived, moved = lax.optimization_barrier((arrived, moved))

    winds, heats, flux_low, flux_high = spread(arrived, rows, columns)
    flux_south = to_next(flux_high, ROWS)
    flux_north = to_previous(flux_low, ROWS)
    moved = solve(heats, land_mask, sea_depth, transport, from_south, own_south, moved, 0, 2)
    flux_south, flux_north, moved = lax.optimization_barrier((flux_south, flux_north, moved))
    side_west, side_east = sides(winds, flux_south, flux_north, from_south, from_north)
    flux_west = to_next(side_east, "tx")
    flux_east = to_previous(side_west, "tx")
    solved = solve(heats, land_mask, sea_depth, transport, from_north, own_north, moved, 1, 2)
    flux_west, flux_east, solved = lax.optimization_barrier((flux_west, flux_east, solved))
    new_height, new_transport = barotropic(
        land_mask, sea_depth, sea_height, transport, from_south, from_north, from_west, from_east,
        winds, flux_south, flux_north, flux_west, flux_east,
    )
    return new_height, new_transport, solved


def solution(mesh):
    in_specs = (
        P(None, EVERY),
        P(EVERY, None),
        P(EVERY, None),
        P(EVERY, None),
        P(EVERY, None),
        P(ROWS, "tx"),
        P(ROWS, "tx"),
        P(ROWS, "tx"),
        P(None, ROWS, "tx"),
        P(None, None, ROWS, "tx"),
    )
    out_specs = (P(ROWS, "tx"), P(None, ROWS, "tx"), P(None, None, ROWS, "tx"))
    return jax.shard_map(local, mesh=mesh, in_specs=in_specs, out_specs=out_specs, check_vma=False)
```

```python
import functools

import jax
import jax.numpy as jnp
import numpy as np
from jax import lax
from jax.experimental import pallas as pl
from jax.experimental.pallas import tpu as pltpu
from jax.sharding import PartitionSpec as P

SUB = 3
EDGE = 8
LANES = 128
EVERY = ("comp", "ty", "tx")
ROWS = ("comp", "ty")
f32 = jnp.float32
i32 = jnp.int32
VM = pl.BlockSpec(memory_space=pltpu.VMEM)
SM = pl.BlockSpec(memory_space=pltpu.SMEM)


def params(mib):
    return pltpu.CompilerParams(vmem_limit_bytes=mib << 20)


def whole(array):
    return pl.BlockSpec(array.shape, lambda i: (0,) * array.ndim)


def pack_kernel(tile_ref, flux_ref, source_ref, cell_ref, weight_ref, out_ref, count_ref, *, beyond):
    blocks = source_ref.shape[0]
    tiles = out_ref.shape[0]
    group = 4
    nowhere = jnp.full((4, LANES), beyond, f32)

    def clear(t, carry):
        count_ref[t] = 0
        out_ref[t, 8] = nowhere
        return carry

    lax.fori_loop(0, tiles, clear, 0, unroll=True)
    sub = lax.broadcasted_iota(i32, (8, LANES), 0)

    def step(i, carry):
        for g in range(group):
            w = i * group + g
            x = flux_ref[:, pl.ds(pl.multiple_of(w * LANES, LANES), LANES)]
            after = pltpu.roll(x, 1, 0)
            six = pltpu.roll(x, 5, 0)
            five = pltpu.roll(x, 6, 0)
            y = jnp.where((sub == 4) | (sub == 5), after, x)
            y = jnp.where(sub == 6, 0.5 * after - 0.3 * x, y)
            y = jnp.where(sub == 3, 0.1 * (six - five), y)
            for half in range(2):
                b = 2 * w + half
                tile = tile_ref[b]
                slot = count_ref[tile]
                count_ref[tile] = slot + 1
                index = jnp.broadcast_to(source_ref[pl.ds(b, 1), :], (8, LANES))
                picked = jnp.take_along_axis(y, index, axis=1)
                value = picked * jnp.broadcast_to(weight_ref[pl.ds(b, 1), :], (8, LANES))
                out_ref[tile, slot] = value[0:4]
                out_ref[tile, 4 + slot] = value[4:8]
                out_ref[tile, 8, pl.ds(slot, 1), :] = cell_ref[pl.ds(b, 1), :].astype(f32)
        return carry

    lax.fori_loop(0, blocks // (2 * group), step, 0)


def pack(tile, flux, source, cell, weight, tiles, beyond):
    return pl.pallas_call(
        functools.partial(pack_kernel, beyond=beyond),
        name="pack_margin",
        grid=(1,),
        in_specs=[SM, whole(flux), whole(source), whole(cell), whole(weight)],
        out_specs=pl.BlockSpec((tiles, 9, 4, LANES), lambda i: (0, 0, 0, 0)),
        out_shape=jax.ShapeDtypeStruct((tiles, 9, 4, LANES), f32),
        scratch_shapes=[pltpu.SMEM((tiles,), i32)],
        compiler_params=params(56),
        cost_estimate=pl.CostEstimate(flops=1 << 22, bytes_accessed=4 << 20, transcendentals=0),
    )(tile, flux, source, cell, weight)


def spread_kernel(load_ref, winds_ref, heats_ref, south_ref, north_ref, acc_ref, *, group):
    _, rows, columns = winds_ref.shape
    fields = 8
    high = columns // LANES
    depth = fields * high
    def clear(i, c):
        acc_ref[pl.ds(pl.multiple_of(i * 256, 256), 256),:] = jnp.zeros((256, LANES), f32)
        return c
    @pl.when(pl.program_id(0) == 0)
    def _():
        lax.fori_loop(0, rows * depth // 256, clear, 0)

    low_iota = lax.broadcasted_iota(i32, (LANES, LANES), 0).astype(f32).astype(jnp.bfloat16)
    pattern = [
        (2 * i + (lax.broadcasted_iota(i32, (16, LANES), 0) >> 3)).astype(f32).astype(jnp.bfloat16) for i in range(high // 2)
    ]
    zero16 = jnp.zeros((16, LANES), jnp.bfloat16)
    one = jnp.ones((LANES, LANES), jnp.bfloat16)
    zero = jnp.zeros((LANES, LANES), jnp.bfloat16)

    for s in range(group):
        cells = load_ref[s, 8].astype(i32)
        highs = ((cells & (columns - 1)) >> 7).astype(f32)
        lows = (cells & (LANES - 1)).astype(f32)
        for k in range(4):
            value = jnp.concatenate([load_ref[s, k], load_ref[s, 4 + k]], axis=0)
            coarse = value.astype(jnp.bfloat16).astype(f32)
            fine = value - coarse
            coarse = jnp.concatenate([coarse, coarse], axis=0).astype(jnp.bfloat16)
            fine = jnp.concatenate([fine, fine], axis=0).astype(jnp.bfloat16)
            hk = jnp.broadcast_to(highs[k : k + 1], (16, LANES)).astype(jnp.bfloat16)
            lk = jnp.broadcast_to(lows[k : k + 1], (16, LANES)).astype(jnp.bfloat16)
            lk = jnp.concatenate([lk] * (LANES // 16), axis=0)
            left = []
            right = []
            for p in pattern:
                hit = hk == p
                left.append(jnp.where(hit, coarse, zero16))
                right.append(jnp.where(hit, fine, zero16))
            lhs = jnp.concatenate([jnp.concatenate(left, axis=0), jnp.concatenate(right, axis=0)], axis=1)
            onehot = jnp.where(lk == low_iota, one, zero)
            rhs = jnp.concatenate([onehot, onehot], axis=1)
            both = lax.dot_general(lhs, rhs, (((1,), (1,)), ((), ())), preferred_element_type=f32)
            row = cells[k, 0] >> (columns.bit_length() - 1)
            place = pl.ds(pl.multiple_of(row * depth, depth), depth)
            acc_ref[place, :] += both

    def turn(i, carry):
        r = pl.multiple_of(i * 8, 8)
        block = acc_ref[pl.ds(pl.multiple_of(r * depth, 8 * depth), 8 * depth), :].reshape(8, depth, LANES)
        for h in range(high):
            piece = jnp.swapaxes(block[:, h * 8 : h * 8 + 8, :], 0, 1)
            for f in range(fields):
                ref = winds_ref if f < 4 else heats_ref
                ref[f % 4, pl.ds(r, 8), h * LANES : (h + 1) * LANES] = piece[f]
        return carry

    @pl.when(pl.program_id(0) == pl.num_programs(0) - 1)
    def _():
        lax.fori_loop(0, rows // 8, turn, 0)
        south_ref[...] = winds_ref[:, 0:EDGE, :]
        north_ref[...] = winds_ref[:, rows - EDGE : rows, :]


def spread(load, rows, columns):
    depth = 8 * columns // LANES
    sources = load.shape[0]
    group = 16 if sources % 16 == 0 else 1
    outs = [
        jax.ShapeDtypeStruct((4, rows, columns), f32),
        jax.ShapeDtypeStruct((4, rows, columns), f32),
        jax.ShapeDtypeStruct((4, EDGE, columns), f32),
        jax.ShapeDtypeStruct((4, EDGE, columns), f32),
    ]
    return pl.pallas_call(
        functools.partial(spread_kernel, group=group),
        name="spread_all",
        grid=(sources // group,),
        in_specs=[pl.BlockSpec((group, *load.shape[1:]), lambda i: (i, 0, 0, 0))],
        out_specs=[whole(out) for out in outs],
        out_shape=outs,
        scratch_shapes=[pltpu.VMEM(((rows + 1) * depth, LANES), f32)],
        compiler_params=params(24),
        cost_estimate=pl.CostEstimate(flops=1 << 30, bytes_accessed=4 << 20, transcendentals=0),
    )(load)


def edges_kernel(
    low_ref, high_ref, left_ref, right_ref, mask_ref, depth_ref, height_ref, flow_ref, south_ref, north_ref, west_ref, east_ref
):
    levels = low_ref.shape[0]
    rows, columns = mask_ref.shape
    lane = lax.broadcasted_iota(i32, (rows, LANES), 1)
    lasts = jnp.zeros((rows, LANES), f32)
    firsts = jnp.zeros((rows, LANES), f32)
    for p in range(levels):
        south_ref[p : p + 1, :] = low_ref[p, 0:1, :]
        north_ref[p : p + 1, :] = high_ref[p, EDGE - 1 : EDGE, :]
        firsts = jnp.where(lane == p, left_ref[p, :, 0:1], firsts)
        lasts = jnp.where(lane == p, right_ref[p, :, LANES - 1 : LANES], lasts)
    fields = [mask_ref, depth_ref, height_ref, flow_ref.at[0], flow_ref.at[1]]
    for f, ref in enumerate(fields):
        place = slice(levels + f * EDGE, levels + (f + 1) * EDGE)
        south_ref[place, :] = ref[0:EDGE, :].astype(f32)
        north_ref[place, :] = ref[rows - EDGE : rows, :].astype(f32)
        place = slice(f * rows, (f + 1) * rows)
        west_ref[place, :] = ref[:, 0:LANES].astype(f32)
        east_ref[place, :] = ref[:, columns - LANES : columns].astype(f32)
    west_ref[5 * rows : 6 * rows, :] = firsts
    east_ref[5 * rows : 6 * rows, :] = lasts


def edges(planes, mask, depth, height, flow):
    levels, rows, columns = planes.shape
    last_row = rows // EDGE - 1
    last_lane = columns // LANES - 1
    tall = jax.ShapeDtypeStruct((levels + 5 * EDGE, columns), f32)
    thin = jax.ShapeDtypeStruct((6 * rows, LANES), f32)
    return pl.pallas_call(
        edges_kernel,
        name="tile_edges",
        grid=(1,),
        in_specs=[
            pl.BlockSpec((levels, EDGE, columns), lambda i: (0, 0, 0)),
            pl.BlockSpec((levels, EDGE, columns), lambda i: (0, last_row, 0)),
            pl.BlockSpec((levels, rows, LANES), lambda i: (0, 0, 0)),
            pl.BlockSpec((levels, rows, LANES), lambda i: (0, 0, last_lane)),
            whole(mask),
            whole(depth),
            whole(height),
            whole(flow),
        ],
        out_specs=[whole(tall), whole(tall), whole(thin), whole(thin)],
        out_shape=[tall, tall, thin, thin],
        compiler_params=params(56),
        cost_estimate=pl.CostEstimate(flops=1 << 20, bytes_accessed=6 << 20, transcendentals=0),
    )(planes, planes, planes, planes, mask, depth, height, flow)


def beside(array, amount, axis):
    return pltpu.roll(array, amount % array.shape[axis], axis)


def drift(speed, toward):
    return 0.1 + 0.15 * jnp.maximum(-toward * speed, 0.0)


def move_kernel(mask_ref, depth_ref, flow_ref, planes_ref, out_ref, coef_ref, *, per):
    step = pl.program_id(0)
    rows = planes_ref.shape[1]
    columns = planes_ref.shape[2]

    @pl.when(step == 0)
    def _():
        mask = mask_ref[...].astype(f32)
        lane = lax.broadcasted_iota(i32, (rows, columns), 1)
        sub = lax.broadcasted_iota(i32, (rows, columns), 0)
        u = flow_ref[0] / depth_ref[...]
        v = flow_ref[1] / depth_ref[...]
        east = mask * jnp.where(lane == columns - 1, 0.0, beside(mask, -1, 1)) * drift(u, 1.0)
        west = mask * jnp.where(lane == 0, 0.0, beside(mask, 1, 1)) * drift(u, -1.0)
        north = mask * jnp.where(sub == rows - 1, 0.0, beside(mask, -1, 0)) * drift(v, 1.0)
        south = mask * jnp.where(sub == 0, 0.0, beside(mask, 1, 0)) * drift(v, -1.0)
        coef_ref[0] = 1.0 - (east + west + north + south)
        coef_ref[1] = east
        coef_ref[2] = west
        coef_ref[3] = north
        coef_ref[4] = south

    for n in range(per):
        for r in range(0, rows, 8):
            span = slice(r, r + 8)
            q = planes_ref[n, span, :]
            sub = lax.broadcasted_iota(i32, (8, columns), 0)
            east = beside(q, -1, 1)
            west = beside(q, 1, 1)
            below = planes_ref[n, max(r - 1, 0) : max(r - 1, 0) + 1, :]
            above = planes_ref[n, min(r + 8, rows - 1) : min(r + 8, rows - 1) + 1, :]
            north = jnp.where(sub == 7, above, beside(q, -1, 0))
            south = jnp.where(sub == 0, below, beside(q, 1, 0))
            out_ref[n, span, :] = (
                coef_ref[0, span, :] * q
                + coef_ref[1, span, :] * east
                + coef_ref[2, span, :] * west
                + coef_ref[3, span, :] * north
                + coef_ref[4, span, :] * south
            )


def move(mask, depth, flow, planes):
    levels, rows, columns = planes.shape
    per = 4
    return pl.pallas_call(
        functools.partial(move_kernel, per=per),
        name="tracer_move",
        grid=(levels // per,),
        in_specs=[
            whole(mask),
            whole(depth),
            whole(flow),
            pl.BlockSpec((per, rows, columns), lambda i: (i, 0, 0)),
        ],
        out_specs=pl.BlockSpec((per, rows, columns), lambda i: (i, 0, 0)),
        out_shape=jax.ShapeDtypeStruct(planes.shape, f32),
        scratch_shapes=[pltpu.VMEM((5, rows, columns), f32)],
        compiler_params=params(56),
        cost_estimate=pl.CostEstimate(flops=1 << 25, bytes_accessed=18 << 20, transcendentals=0),
    )(mask, depth, flow, planes)


def solve_kernel(
    flux_ref, mask_ref, depth_ref, flow_ref, near_ref, own_ref, west_ref, east_ref, own_west_ref, own_east_ref, *refs,
    part, parts, absorb, decay,
):
    moved_ref, out_ref, ratio_ref = refs[0], refs[-2], refs[-1]
    step = pl.program_id(0)
    levels = moved_ref.shape[1]
    rows = west_ref.shape[0] // 6
    columns = mask_ref.shape[1]
    start = (part * (rows // EDGE // parts) + step) * EDGE
    lane = lax.broadcasted_iota(i32, (EDGE, LANES), 1)
    sides = (
        (west_ref, own_west_ref, 0, -1.0, slice(0, LANES)),
        (east_ref, own_east_ref, LANES - 1, 1.0, slice(columns - LANES, columns)),
    )
    for beyond_ref, inside_ref, edge, toward, lanes in sides:

        def take(ref, field):
            return ref[pl.ds(pl.multiple_of(field * rows + start, EDGE), EDGE), :]

        there = LANES - 1 - edge
        land = take(inside_ref, 0)[:, edge : edge + 1] * take(beyond_ref, 0)[:, there : there + 1]
        speed = take(inside_ref, 3)[:, edge : edge + 1] / take(inside_ref, 1)[:, edge : edge + 1]
        extra = land * drift(speed, toward) * (take(beyond_ref, 5) - take(inside_ref, 5))
        for tracer in range(2):
            for k in range(levels):
                p = tracer * levels + k
                moved_ref[tracer, k, :, lanes] = moved_ref[tracer, k, :, lanes] + jnp.where(
                    lane == edge, extra[:, p : p + 1], 0.0
                )

    at_edge = step == (0 if part == 0 else pl.num_programs(0) - 1)
    run = functools.partial(
        solve_rows, flux_ref, mask_ref, depth_ref, flow_ref, near_ref, own_ref, moved_ref, out_ref, ratio_ref, absorb, decay
    )
    toward = -1.0 if part == 0 else 1.0

    @pl.when(at_edge)
    def _():
        run(toward)

    @pl.when(jnp.logical_not(at_edge))
    def _():
        run(None)


def solve_rows(
    flux_ref, mask_ref, depth_ref, flow_ref, near_ref, own_ref, moved_ref, out_ref, ratio_ref, absorb, decay, toward
):
    levels = moved_ref.shape[1]
    columns = mask_ref.shape[1]
    planes = 2 * levels
    mask = mask_ref[...].astype(f32)
    if toward is not None:
        row = 0 if toward < 0 else EDGE - 1
        other = planes + (EDGE - 1 if toward < 0 else 0)
        line = slice(row, row + 1)
        coef = mask[line] * near_ref[other : other + 1, :] * drift(flow_ref[0, line, :] / depth_ref[line, :], toward)
        hit = lax.broadcasted_iota(i32, (EDGE, columns), 0) == row

    def moved(tracer, k):
        value = moved_ref[tracer, k]
        if toward is not None:
            p = tracer * levels + k
            extra = coef * (near_ref[p : p + 1, :] - own_ref[p : p + 1, :])
            value = value + jnp.where(hit, extra, 0.0)
        return value

    heat_top = 0.5 * mask * flux_ref[0]
    sun = 0.5 * mask * flux_ref[1]
    salt_top = mask * flux_ref[2]
    stir = flux_ref[3]
    base = 0.2 * mask
    stir = 0.5 * mask * (stir * stir)
    above = jnp.zeros_like(mask)
    link = jnp.zeros_like(mask)
    heat_last = None
    salt_last = None
    for k in range(levels):
        heat = moved(0, k) + absorb[k] * sun
        salt = moved(1, k)
        if k == 0:
            heat = heat + heat_top
            salt = salt + salt_top
        below = base + decay[k] * stir if k < levels - 1 else jnp.zeros_like(mask)
        pivot = 1.0 + below + above
        if k > 0:
            pivot = pivot + above * link
            heat = heat + above * heat_last
            salt = salt + above * salt_last
        inverse = 1.0 / pivot
        link = -below * inverse
        heat_last = heat * inverse
        salt_last = salt * inverse
        above = below
        if k < levels - 1:
            ratio_ref[k] = link
        out_ref[0, k] = heat_last
        out_ref[1, k] = salt_last
    for k in range(levels - 2, -1, -1):
        link = ratio_ref[k]
        heat_last = out_ref[0, k] - link * heat_last
        salt_last = out_ref[1, k] - link * salt_last
        out_ref[0, k] = heat_last
        out_ref[1, k] = salt_last


def solve(flux, mask, depth, flow, near, own, margins, moved, done, part, parts):
    count, levels, rows, columns = moved.shape
    depths = np.arange(levels, dtype=np.float64)
    absorb = tuple(float(a) for a in np.exp(-depths / 3.0) - np.exp(-(depths + 1.0) / 3.0))
    decay = tuple(float(a) for a in np.exp(-depths / 2.0))
    steps = rows // EDGE // parts
    first = part * steps
    line = pl.BlockSpec((EDGE, columns), lambda i: (first + i, 0))
    block = pl.BlockSpec((count, levels, EDGE, columns), lambda i: (0, 0, first + i, 0))
    return pl.pallas_call(
        functools.partial(solve_kernel, part=part, parts=parts, absorb=absorb, decay=decay),
        name=f"column_solve_{part}",
        grid=(steps,),
        in_specs=[
            pl.BlockSpec((4, EDGE, columns), lambda i: (0, first + i, 0)),
            line,
            line,
            pl.BlockSpec((1, EDGE, columns), lambda i: (1, first + i, 0)),
            whole(near),
            whole(own),
            *[whole(margin) for margin in margins],
            block,
            *[pl.BlockSpec(memory_space=pl.ANY) for _ in done],
        ],
        out_specs=block,
        out_shape=jax.ShapeDtypeStruct(moved.shape, f32),
        scratch_shapes=[pltpu.VMEM((levels, EDGE, columns), f32)],
        input_output_aliases={11: 0} if done else {},
        compiler_params=params(24),
        cost_estimate=pl.CostEstimate(flops=1 << 24, bytes_accessed=9 << 20, transcendentals=0),
    )(flux, mask, depth, flow, near, own, *margins, moved, *done)


def sides_kernel(left_ref, right_ref, south_ref, north_ref, low_ref, high_ref, west_ref, east_ref):
    rows = left_ref.shape[1]
    columns = south_ref.shape[2]
    levels = low_ref.shape[0] - 5 * EDGE
    tall = rows + 2 * EDGE
    for ref, part_ref, lanes in (
        (west_ref, left_ref, slice(0, LANES)),
        (east_ref, right_ref, slice(columns - LANES, columns)),
    ):
        for f in range(4):
            start = f * tall
            ref[start : start + EDGE, :] = south_ref[f, :, lanes]
            ref[start + EDGE : start + EDGE + rows, :] = part_ref[f]
            ref[start + EDGE + rows : start + tall, :] = north_ref[f, :, lanes]
        for f in range(5):
            start = 4 * tall + 2 * EDGE * f
            place = slice(levels + f * EDGE, levels + (f + 1) * EDGE)
            ref[start : start + EDGE, :] = low_ref[place, lanes]
            ref[start + EDGE : start + 2 * EDGE, :] = high_ref[place, lanes]


def sides(winds, south, north, low, high):
    _, rows, columns = winds.shape
    last = columns // LANES - 1
    shape = jax.ShapeDtypeStruct((4 * (rows + 2 * EDGE) + 10 * EDGE, LANES), f32)
    return pl.pallas_call(
        sides_kernel,
        name="tile_sides",
        grid=(1,),
        in_specs=[
            pl.BlockSpec((4, rows, LANES), lambda i: (0, 0, 0)),
            pl.BlockSpec((4, rows, LANES), lambda i: (0, 0, last)),
            whole(south),
            whole(north),
            whole(low),
            whole(high),
        ],
        out_specs=[whole(shape), whole(shape)],
        out_shape=[shape, shape],
        compiler_params=params(16),
        cost_estimate=pl.CostEstimate(flops=1 << 16, bytes_accessed=2 << 20, transcendentals=0),
    )(winds, winds, south, north, low, high)


def barotropic_kernel(
    mask_ref, depth_ref, begin_ref, stream_ref, low_ref, high_ref, left_ref, right_ref,
    flux_ref, south_ref, north_ref, west_ref, east_ref, height_ref, flow_ref, wide_ref,
):
    rows, columns = begin_ref.shape
    levels = low_ref.shape[0] - 5 * EDGE
    tall = rows + 2 * EDGE
    middle = slice(EDGE, EDGE + rows)

    def merge(low, high):
        lane = lax.broadcasted_iota(i32, low.shape, 1)
        return jnp.where(lane < LANES // 2, high, low)

    for f, ref in enumerate([mask_ref, depth_ref, begin_ref, stream_ref.at[0], stream_ref.at[1]]):
        place = slice(levels + f * EDGE, levels + (f + 1) * EDGE)
        wide_ref[f, 0:EDGE, 0:columns] = low_ref[place, :]
        wide_ref[f, middle, 0:columns] = ref[...].astype(f32)
        wide_ref[f, EDGE + rows : tall, 0:columns] = high_ref[place, :]
        place = slice(f * rows, (f + 1) * rows)
        wide_ref[f, middle, columns : columns + LANES] = merge(left_ref[place, :], right_ref[place, :])
        start = 4 * tall + 2 * EDGE * f
        corner = merge(west_ref[start : start + 2 * EDGE, :], east_ref[start : start + 2 * EDGE, :])
        wide_ref[f, 0:EDGE, columns : columns + LANES] = corner[0:EDGE]
        wide_ref[f, EDGE + rows : tall, columns : columns + LANES] = corner[EDGE : 2 * EDGE]
    for f in range(4):
        wide_ref[5 + f, 0:EDGE, 0:columns] = south_ref[f]
        wide_ref[5 + f, middle, 0:columns] = flux_ref[f]
        wide_ref[5 + f, EDGE + rows : tall, 0:columns] = north_ref[f]
        place = slice(f * tall, (f + 1) * tall)
        wide_ref[5 + f, :, columns : columns + LANES] = merge(west_ref[place, :], east_ref[place, :])
    mask = wide_ref[0]
    drag = -0.5 * wide_ref[1]
    height = wide_ref[2]
    along = wide_ref[3]
    across = wide_ref[4]
    wind_x = 0.5 * wide_ref[5]
    wind_y = 0.5 * wide_ref[6]
    push = 0.5 * wide_ref[7]
    source = wide_ref[8]
    for k in range(SUB):
        level = mask * (height + push)
        along = mask * (0.95 * along + drag * (beside(level, -1, 1) - beside(level, 1, 1)) + wind_x)
        across = mask * (0.95 * across + drag * (beside(level, -1, 0) - beside(level, 1, 0)) + wind_y)
        spread_out = beside(along, -1, 1) - beside(along, 1, 1) + beside(across, -1, 0) - beside(across, 1, 0)
        height = mask * (height - 0.5 * spread_out + source)
    height_ref[...] = height[middle, :columns]
    flow_ref[0] = along[middle, :columns]
    flow_ref[1] = across[middle, :columns]


def barotropic(*arrays):
    rows, columns = arrays[2].shape
    outs = [jax.ShapeDtypeStruct((rows, columns), f32), jax.ShapeDtypeStruct((2, rows, columns), f32)]
    return pl.pallas_call(
        barotropic_kernel,
        name="barotropic",
        grid=(1,),
        in_specs=[whole(array) for array in arrays],
        out_specs=[whole(out) for out in outs],
        out_shape=outs,
        scratch_shapes=[pltpu.VMEM((9, rows + 2 * EDGE, columns + LANES), f32)],
        compiler_params=params(32),
        cost_estimate=pl.CostEstimate(flops=1 << 24, bytes_accessed=6 << 20, transcendentals=0),
    )(*arrays)


def to_next(array, axes):
    ends = lax.axis_size(axes) - 1
    return lax.ppermute(array, axes, [(i, i + 1) for i in range(ends)])


def to_previous(array, axes):
    ends = lax.axis_size(axes) - 1
    return lax.ppermute(array, axes, [(i + 1, i) for i in range(ends)])


def all_to_all(array):
    return lax.all_to_all(array, EVERY, split_axis=0, concat_axis=0, tiled=True)


def local(
    atm_flux,
    margin_source,
    margin_cell,
    margin_weight,
    margin_tile,
    land_mask,
    sea_depth,
    sea_height,
    transport,
    tracers,
):
    tiles = lax.axis_size(EVERY)
    count, levels, rows, columns = tracers.shape
    packed = pack(
        margin_tile.reshape(-1), atm_flux, margin_source, margin_cell, margin_weight, tiles, rows * columns
    )
    packed, land_mask, sea_depth, sea_height, transport, tracers = lax.optimization_barrier(
        (packed, land_mask, sea_depth, sea_height, transport, tracers)
    )
    arrived = all_to_all(packed)

    planes = tracers.reshape(count * levels, rows, columns)
    own_south, own_north, own_west, own_east = edges(planes, land_mask, sea_depth, sea_height, transport)
    from_west = to_next(own_east, "tx")
    from_east = to_previous(own_west, "tx")
    moved = move(land_mask, sea_depth, transport, planes)
    moved = moved.reshape(tracers.shape)
    own_south, own_north, moved = lax.optimization_barrier((own_south, own_north, moved))
    from_south = to_next(own_north, ROWS)
    from_north = to_previous(own_south, ROWS)
    arrived, moved = lax.optimization_barrier((arrived, moved))

    winds, heats, flux_low, flux_high = spread(arrived, rows, columns)
    flux_south = to_next(flux_high, ROWS)
    flux_north = to_previous(flux_low, ROWS)
    margins = (from_west, from_east, own_west, own_east)
    half = solve(heats, land_mask, sea_depth, transport, from_south, own_south, margins, moved, (), 0, 2)
    flux_south, flux_north, half = lax.optimization_barrier((flux_south, flux_north, half))
    side_west, side_east = sides(winds, flux_south, flux_north, from_south, from_north)
    flux_west = to_next(side_east, "tx")
    flux_east = to_previous(side_west, "tx")
    solved = solve(heats, land_mask, sea_depth, transport, from_north, own_north, margins, moved, (half,), 1, 2)
    flux_west, flux_east, solved = lax.optimization_barrier((flux_west, flux_east, solved))
    new_height, new_transport = barotropic(
        land_mask, sea_depth, sea_height, transport, from_south, from_north, from_west, from_east,
        winds, flux_south, flux_north, flux_west, flux_east,
    )
    return new_height, new_transport, solved


def solution(mesh):
    in_specs = (
        P(None, EVERY),
        P(EVERY, None),
        P(EVERY, None),
        P(EVERY, None),
        P(EVERY, None),
        P(ROWS, "tx"),
        P(ROWS, "tx"),
        P(ROWS, "tx"),
        P(None, ROWS, "tx"),
        P(None, None, ROWS, "tx"),
    )
    out_specs = (P(ROWS, "tx"), P(None, ROWS, "tx"), P(None, None, ROWS, "tx"))
    return jax.shard_map(local, mesh=mesh, in_specs=in_specs, out_specs=out_specs, check_vma=False)
```

```python
import functools

import jax
import jax.numpy as jnp
import numpy as np
from jax import lax
from jax.experimental import pallas as pl
from jax.experimental.pallas import tpu as pltpu
from jax.sharding import PartitionSpec as P

SUB = 3
EDGE = 8
LANES = 128
EVERY = ("comp", "ty", "tx")
ROWS = ("comp", "ty")
f32 = jnp.float32
i32 = jnp.int32
VM = pl.BlockSpec(memory_space=pltpu.VMEM)
SM = pl.BlockSpec(memory_space=pltpu.SMEM)


def params(mib):
    return pltpu.CompilerParams(vmem_limit_bytes=mib << 20)


def whole(array):
    return pl.BlockSpec(array.shape, lambda i: (0,) * array.ndim)


def pack_kernel(tile_ref, flux_ref, source_ref, cell_ref, weight_ref, out_ref, count_ref, *, beyond):
    blocks = source_ref.shape[0]
    tiles = out_ref.shape[0]
    group = 4
    nowhere = jnp.full((4, LANES), beyond, f32)

    def clear(t, carry):
        count_ref[t] = 0
        out_ref[t, 8] = nowhere
        return carry

    @pl.when(pl.program_id(0) == 0)
    def _():
        lax.fori_loop(0, tiles, clear, 0, unroll=True)

    begin = pl.program_id(0) * blocks
    sub = lax.broadcasted_iota(i32, (8, LANES), 0)

    def step(i, carry):
        for g in range(group):
            w = i * group + g
            x = flux_ref[:, pl.ds(pl.multiple_of(w * LANES, LANES), LANES)]
            after = pltpu.roll(x, 1, 0)
            six = pltpu.roll(x, 5, 0)
            five = pltpu.roll(x, 6, 0)
            y = jnp.where((sub == 4) | (sub == 5), after, x)
            y = jnp.where(sub == 6, 0.5 * after - 0.3 * x, y)
            y = jnp.where(sub == 3, 0.1 * (six - five), y)
            for half in range(2):
                b = 2 * w + half
                tile = tile_ref[begin + b]
                slot = count_ref[tile]
                count_ref[tile] = slot + 1
                index = jnp.broadcast_to(source_ref[pl.ds(b, 1), :], (8, LANES))
                picked = jnp.take_along_axis(y, index, axis=1)
                value = picked * jnp.broadcast_to(weight_ref[pl.ds(b, 1), :], (8, LANES))
                out_ref[tile, slot] = value[0:4]
                out_ref[tile, 4 + slot] = value[4:8]
                out_ref[tile, 8, pl.ds(slot, 1), :] = cell_ref[pl.ds(b, 1), :].astype(f32)
        return carry

    lax.fori_loop(0, blocks // (2 * group), step, 0)


def pack(tile, flux, source, cell, weight, tiles, beyond):
    blocks = source.shape[0]
    steps = 4 if blocks % 32 == 0 else 1
    line = pl.BlockSpec((blocks // steps, LANES), lambda i: (i, 0))
    return pl.pallas_call(
        functools.partial(pack_kernel, beyond=beyond),
        name="pack_margin",
        grid=(steps,),
        in_specs=[SM, pl.BlockSpec((8, flux.shape[1] // steps), lambda i: (0, i)), line, line, line],
        out_specs=pl.BlockSpec((tiles, 9, 4, LANES), lambda i: (0, 0, 0, 0)),
        out_shape=jax.ShapeDtypeStruct((tiles, 9, 4, LANES), f32),
        scratch_shapes=[pltpu.SMEM((tiles,), i32)],
        compiler_params=params(56),
        cost_estimate=pl.CostEstimate(flops=1 << 22, bytes_accessed=4 << 20, transcendentals=0),
    )(tile, flux, source, cell, weight)


def spread_kernel(cells_ref, load_ref, winds_ref, heats_ref, south_ref, north_ref, acc_ref, turned_ref, *, group):
    _, rows, columns = winds_ref.shape
    fields = 8
    high = columns // LANES
    depth = fields * high
    def clear(i, c):
        acc_ref[pl.ds(pl.multiple_of(i * 256, 256), 256),:] = jnp.zeros((256, LANES), f32)
        return c
    @pl.when(pl.program_id(0) == 0)
    def _():
        lax.fori_loop(0, rows * depth // 256, clear, 0)
        per = 4 * group
        chunk = min(cells_ref.shape[0], LANES // 4)
        for i in range(0, cells_ref.shape[0], chunk):
            cells = cells_ref[i : i + chunk, 0].reshape(4 * chunk, LANES)
            if chunk < LANES // 4:
                cells = jnp.concatenate([cells] * (LANES // (4 * chunk)), axis=0)
            columns_of = (cells.astype(i32) & (LANES - 1)).astype(f32).T
            for n in range(4 * chunk // per):
                part = columns_of if n == 0 else pltpu.roll(columns_of, LANES - n * per, 1)
                turned_ref[i // group + n] = part

    step = pl.program_id(0)
    low_iota = lax.broadcasted_iota(i32, (LANES, LANES), 1).astype(f32).astype(jnp.bfloat16)
    pattern = [
        (2 * i + (lax.broadcasted_iota(i32, (16, LANES), 0) >> 3)).astype(f32).astype(jnp.bfloat16) for i in range(high // 2)
    ]
    zero16 = jnp.zeros((16, LANES), jnp.bfloat16)
    one = jnp.ones((LANES, LANES), jnp.bfloat16)
    zero = jnp.zeros((LANES, LANES), jnp.bfloat16)

    for s in range(group):
        cells = load_ref[s, 8].astype(i32)
        highs = ((cells & (columns - 1)) >> 7).astype(f32)
        for k in range(4):
            value = jnp.concatenate([load_ref[s, k], load_ref[s, 4 + k]], axis=0)
            coarse = value.astype(jnp.bfloat16).astype(f32)
            fine = value - coarse
            coarse = jnp.concatenate([coarse, coarse], axis=0).astype(jnp.bfloat16)
            fine = jnp.concatenate([fine, fine], axis=0).astype(jnp.bfloat16)
            hk = jnp.broadcast_to(highs[k : k + 1], (16, LANES)).astype(jnp.bfloat16)
            c = 4 * s + k
            lk = jnp.broadcast_to(turned_ref[step, :, c : c + 1], (LANES, LANES)).astype(jnp.bfloat16)
            left = []
            right = []
            for p in pattern:
                hit = hk == p
                left.append(jnp.where(hit, coarse, zero16))
                right.append(jnp.where(hit, fine, zero16))
            lhs = jnp.concatenate([jnp.concatenate(left, axis=0), jnp.concatenate(right, axis=0)], axis=1)
            onehot = jnp.where(lk == low_iota, one, zero)
            rhs = jnp.concatenate([onehot, onehot], axis=0)
            both = lax.dot_general(lhs, rhs, (((1,), (0,)), ((), ())), preferred_element_type=f32)
            row = cells[k, 0] >> (columns.bit_length() - 1)
            place = pl.ds(pl.multiple_of(row * depth, depth), depth)
            acc_ref[place, :] += both

    def turn(i, carry):
        r = pl.multiple_of(i * 8, 8)
        block = acc_ref[pl.ds(pl.multiple_of(r * depth, 8 * depth), 8 * depth), :].reshape(8, depth, LANES)
        for h in range(high):
            piece = jnp.swapaxes(block[:, h * 8 : h * 8 + 8, :], 0, 1)
            for f in range(fields):
                ref = winds_ref if f < 4 else heats_ref
                ref[f % 4, pl.ds(r, 8), h * LANES : (h + 1) * LANES] = piece[f]
        return carry

    @pl.when(pl.program_id(0) == pl.num_programs(0) - 1)
    def _():
        lax.fori_loop(0, rows // 8, turn, 0)
        south_ref[...] = winds_ref[:, 0:EDGE, :]
        north_ref[...] = winds_ref[:, rows - EDGE : rows, :]


def spread(load, rows, columns):
    depth = 8 * columns // LANES
    sources = load.shape[0]
    group = 16 if sources % 16 == 0 else 1
    outs = [
        jax.ShapeDtypeStruct((4, rows, columns), f32),
        jax.ShapeDtypeStruct((4, rows, columns), f32),
        jax.ShapeDtypeStruct((4, EDGE, columns), f32),
        jax.ShapeDtypeStruct((4, EDGE, columns), f32),
    ]
    return pl.pallas_call(
        functools.partial(spread_kernel, group=group),
        name="spread_all",
        grid=(sources // group,),
        in_specs=[
            pl.BlockSpec((sources, 1, 4, LANES), lambda i: (0, 8, 0, 0)),
            pl.BlockSpec((group, *load.shape[1:]), lambda i: (i, 0, 0, 0)),
        ],
        out_specs=[whole(out) for out in outs],
        out_shape=outs,
        scratch_shapes=[
            pltpu.VMEM(((rows + 1) * depth, LANES), f32),
            pltpu.VMEM((sources // group, LANES, LANES), f32),
        ],
        compiler_params=params(24),
        cost_estimate=pl.CostEstimate(flops=1 << 30, bytes_accessed=4 << 20, transcendentals=0),
    )(load, load)


def edges_kernel(
    low_ref, high_ref, left_ref, right_ref, mask_ref, depth_ref, height_ref, flow_ref, south_ref, north_ref, west_ref, east_ref
):
    levels = low_ref.shape[0]
    rows, columns = mask_ref.shape
    lane = lax.broadcasted_iota(i32, (rows, LANES), 1)
    lasts = jnp.zeros((rows, LANES), f32)
    firsts = jnp.zeros((rows, LANES), f32)
    for p in range(levels):
        south_ref[p : p + 1, :] = low_ref[p, 0:1, :]
        north_ref[p : p + 1, :] = high_ref[p, EDGE - 1 : EDGE, :]
        firsts = jnp.where(lane == p, left_ref[p, :, 0:1], firsts)
        lasts = jnp.where(lane == p, right_ref[p, :, LANES - 1 : LANES], lasts)
    fields = [mask_ref, depth_ref, height_ref, flow_ref.at[0], flow_ref.at[1]]
    for f, ref in enumerate(fields):
        place = slice(levels + f * EDGE, levels + (f + 1) * EDGE)
        south_ref[place, :] = ref[0:EDGE, :].astype(f32)
        north_ref[place, :] = ref[rows - EDGE : rows, :].astype(f32)
        place = slice(f * rows, (f + 1) * rows)
        west_ref[place, :] = ref[:, 0:LANES].astype(f32)
        east_ref[place, :] = ref[:, columns - LANES : columns].astype(f32)
    west_ref[5 * rows : 6 * rows, :] = firsts
    east_ref[5 * rows : 6 * rows, :] = lasts


def edges(planes, mask, depth, height, flow):
    levels, rows, columns = planes.shape
    last_row = rows // EDGE - 1
    last_lane = columns // LANES - 1
    tall = jax.ShapeDtypeStruct((levels + 5 * EDGE, columns), f32)
    thin = jax.ShapeDtypeStruct((6 * rows, LANES), f32)
    return pl.pallas_call(
        edges_kernel,
        name="tile_edges",
        grid=(1,),
        in_specs=[
            pl.BlockSpec((levels, EDGE, columns), lambda i: (0, 0, 0)),
            pl.BlockSpec((levels, EDGE, columns), lambda i: (0, last_row, 0)),
            pl.BlockSpec((levels, rows, LANES), lambda i: (0, 0, 0)),
            pl.BlockSpec((levels, rows, LANES), lambda i: (0, 0, last_lane)),
            whole(mask),
            whole(depth),
            whole(height),
            whole(flow),
        ],
        out_specs=[whole(tall), whole(tall), whole(thin), whole(thin)],
        out_shape=[tall, tall, thin, thin],
        compiler_params=params(56),
        cost_estimate=pl.CostEstimate(flops=1 << 20, bytes_accessed=6 << 20, transcendentals=0),
    )(planes, planes, planes, planes, mask, depth, height, flow)


def beside(array, amount, axis):
    return pltpu.roll(array, amount % array.shape[axis], axis)


def drift(speed, toward):
    return 0.1 + 0.15 * jnp.maximum(-toward * speed, 0.0)


def move_kernel(mask_ref, depth_ref, flow_ref, planes_ref, out_ref, coef_ref, *, per):
    step = pl.program_id(0)
    rows = planes_ref.shape[1]
    columns = planes_ref.shape[2]

    @pl.when(step == 0)
    def _():
        mask = mask_ref[...].astype(f32)
        lane = lax.broadcasted_iota(i32, (rows, columns), 1)
        sub = lax.broadcasted_iota(i32, (rows, columns), 0)
        u = flow_ref[0] / depth_ref[...]
        v = flow_ref[1] / depth_ref[...]
        east = mask * jnp.where(lane == columns - 1, 0.0, beside(mask, -1, 1)) * drift(u, 1.0)
        west = mask * jnp.where(lane == 0, 0.0, beside(mask, 1, 1)) * drift(u, -1.0)
        north = mask * jnp.where(sub == rows - 1, 0.0, beside(mask, -1, 0)) * drift(v, 1.0)
        south = mask * jnp.where(sub == 0, 0.0, beside(mask, 1, 0)) * drift(v, -1.0)
        coef_ref[0] = 1.0 - (east + west + north + south)
        coef_ref[1] = east
        coef_ref[2] = west
        coef_ref[3] = north
        coef_ref[4] = south

    for n in range(per):
        for r in range(0, rows, 8):
            span = slice(r, r + 8)
            q = planes_ref[n, span, :]
            sub = lax.broadcasted_iota(i32, (8, columns), 0)
            east = beside(q, -1, 1)
            west = beside(q, 1, 1)
            below = planes_ref[n, max(r - 1, 0) : max(r - 1, 0) + 1, :]
            above = planes_ref[n, min(r + 8, rows - 1) : min(r + 8, rows - 1) + 1, :]
            north = jnp.where(sub == 7, above, beside(q, -1, 0))
            south = jnp.where(sub == 0, below, beside(q, 1, 0))
            out_ref[n, span, :] = (
                coef_ref[0, span, :] * q
                + coef_ref[1, span, :] * east
                + coef_ref[2, span, :] * west
                + coef_ref[3, span, :] * north
                + coef_ref[4, span, :] * south
            )


def move(mask, depth, flow, planes):
    levels, rows, columns = planes.shape
    per = 4
    return pl.pallas_call(
        functools.partial(move_kernel, per=per),
        name="tracer_move",
        grid=(levels // per,),
        in_specs=[
            whole(mask),
            whole(depth),
            whole(flow),
            pl.BlockSpec((per, rows, columns), lambda i: (i, 0, 0)),
        ],
        out_specs=pl.BlockSpec((per, rows, columns), lambda i: (i, 0, 0)),
        out_shape=jax.ShapeDtypeStruct(planes.shape, f32),
        scratch_shapes=[pltpu.VMEM((5, rows, columns), f32)],
        compiler_params=params(56),
        cost_estimate=pl.CostEstimate(flops=1 << 25, bytes_accessed=18 << 20, transcendentals=0),
    )(mask, depth, flow, planes)


def solve_kernel(
    flux_ref, mask_ref, depth_ref, flow_ref, near_ref, own_ref, west_ref, east_ref, own_west_ref, own_east_ref, *refs,
    part, parts, absorb, decay,
):
    moved_ref, out_ref, ratio_ref = refs[0], refs[-2], refs[-1]
    step = pl.program_id(0)
    levels = moved_ref.shape[1]
    rows = west_ref.shape[0] // 6
    columns = mask_ref.shape[1]
    start = (part * (rows // EDGE // parts) + step) * EDGE
    lane = lax.broadcasted_iota(i32, (EDGE, LANES), 1)
    sides = (
        (west_ref, own_west_ref, 0, -1.0, slice(0, LANES)),
        (east_ref, own_east_ref, LANES - 1, 1.0, slice(columns - LANES, columns)),
    )
    for beyond_ref, inside_ref, edge, toward, lanes in sides:

        def take(ref, field):
            return ref[pl.ds(pl.multiple_of(field * rows + start, EDGE), EDGE), :]

        there = LANES - 1 - edge
        land = take(inside_ref, 0)[:, edge : edge + 1] * take(beyond_ref, 0)[:, there : there + 1]
        speed = take(inside_ref, 3)[:, edge : edge + 1] / take(inside_ref, 1)[:, edge : edge + 1]
        extra = land * drift(speed, toward) * (take(beyond_ref, 5) - take(inside_ref, 5))
        for tracer in range(2):
            for k in range(levels):
                p = tracer * levels + k
                moved_ref[tracer, k, :, lanes] = moved_ref[tracer, k, :, lanes] + jnp.where(
                    lane == edge, extra[:, p : p + 1], 0.0
                )

    at_edge = step == (0 if part == 0 else pl.num_programs(0) - 1)
    run = functools.partial(
        solve_rows, flux_ref, mask_ref, depth_ref, flow_ref, near_ref, own_ref, moved_ref, out_ref, ratio_ref, absorb, decay
    )
    toward = -1.0 if part == 0 else 1.0

    @pl.when(at_edge)
    def _():
        run(toward)

    @pl.when(jnp.logical_not(at_edge))
    def _():
        run(None)


def solve_rows(
    flux_ref, mask_ref, depth_ref, flow_ref, near_ref, own_ref, moved_ref, out_ref, ratio_ref, absorb, decay, toward
):
    levels = moved_ref.shape[1]
    columns = mask_ref.shape[1]
    planes = 2 * levels
    mask = mask_ref[...].astype(f32)
    if toward is not None:
        row = 0 if toward < 0 else EDGE - 1
        other = planes + (EDGE - 1 if toward < 0 else 0)
        line = slice(row, row + 1)
        coef = mask[line] * near_ref[other : other + 1, :] * drift(flow_ref[0, line, :] / depth_ref[line, :], toward)
        hit = lax.broadcasted_iota(i32, (EDGE, columns), 0) == row

    def moved(tracer, k):
        value = moved_ref[tracer, k]
        if toward is not None:
            p = tracer * levels + k
            extra = coef * (near_ref[p : p + 1, :] - own_ref[p : p + 1, :])
            value = value + jnp.where(hit, extra, 0.0)
        return value

    heat_top = 0.5 * mask * flux_ref[0]
    sun = 0.5 * mask * flux_ref[1]
    salt_top = mask * flux_ref[2]
    stir = flux_ref[3]
    base = 0.2 * mask
    stir = 0.5 * mask * (stir * stir)
    above = jnp.zeros_like(mask)
    link = jnp.zeros_like(mask)
    heat_last = None
    salt_last = None
    for k in range(levels):
        heat = moved(0, k) + absorb[k] * sun
        salt = moved(1, k)
        if k == 0:
            heat = heat + heat_top
            salt = salt + salt_top
        below = base + decay[k] * stir if k < levels - 1 else jnp.zeros_like(mask)
        pivot = 1.0 + below + above
        if k > 0:
            pivot = pivot + above * link
            heat = heat + above * heat_last
            salt = salt + above * salt_last
        inverse = 1.0 / pivot
        link = -below * inverse
        heat_last = heat * inverse
        salt_last = salt * inverse
        above = below
        if k < levels - 1:
            ratio_ref[k] = link
        out_ref[0, k] = heat_last
        out_ref[1, k] = salt_last
    for k in range(levels - 2, -1, -1):
        link = ratio_ref[k]
        heat_last = out_ref[0, k] - link * heat_last
        salt_last = out_ref[1, k] - link * salt_last
        out_ref[0, k] = heat_last
        out_ref[1, k] = salt_last


def solve(flux, mask, depth, flow, near, own, margins, moved, done, part, parts):
    count, levels, rows, columns = moved.shape
    depths = np.arange(levels, dtype=np.float64)
    absorb = tuple(float(a) for a in np.exp(-depths / 3.0) - np.exp(-(depths + 1.0) / 3.0))
    decay = tuple(float(a) for a in np.exp(-depths / 2.0))
    steps = rows // EDGE // parts
    first = part * steps
    line = pl.BlockSpec((EDGE, columns), lambda i: (first + i, 0))
    block = pl.BlockSpec((count, levels, EDGE, columns), lambda i: (0, 0, first + i, 0))
    return pl.pallas_call(
        functools.partial(solve_kernel, part=part, parts=parts, absorb=absorb, decay=decay),
        name=f"column_solve_{part}",
        grid=(steps,),
        in_specs=[
            pl.BlockSpec((4, EDGE, columns), lambda i: (0, first + i, 0)),
            line,
            line,
            pl.BlockSpec((1, EDGE, columns), lambda i: (1, first + i, 0)),
            whole(near),
            whole(own),
            *[whole(margin) for margin in margins],
            block,
            *[pl.BlockSpec(memory_space=pl.ANY) for _ in done],
        ],
        out_specs=block,
        out_shape=jax.ShapeDtypeStruct(moved.shape, f32),
        scratch_shapes=[pltpu.VMEM((levels, EDGE, columns), f32)],
        input_output_aliases={11: 0} if done else {},
        compiler_params=params(48),
        cost_estimate=pl.CostEstimate(flops=1 << 24, bytes_accessed=9 << 20, transcendentals=0),
    )(flux, mask, depth, flow, near, own, *margins, moved, *done)


def sides_kernel(left_ref, right_ref, south_ref, north_ref, low_ref, high_ref, west_ref, east_ref):
    rows = left_ref.shape[1]
    columns = south_ref.shape[2]
    levels = low_ref.shape[0] - 5 * EDGE
    tall = rows + 2 * EDGE
    for ref, part_ref, lanes in (
        (west_ref, left_ref, slice(0, LANES)),
        (east_ref, right_ref, slice(columns - LANES, columns)),
    ):
        for f in range(4):
            start = f * tall
            ref[start : start + EDGE, :] = south_ref[f, :, lanes]
            ref[start + EDGE : start + EDGE + rows, :] = part_ref[f]
            ref[start + EDGE + rows : start + tall, :] = north_ref[f, :, lanes]
        for f in range(5):
            start = 4 * tall + 2 * EDGE * f
            place = slice(levels + f * EDGE, levels + (f + 1) * EDGE)
            ref[start : start + EDGE, :] = low_ref[place, lanes]
            ref[start + EDGE : start + 2 * EDGE, :] = high_ref[place, lanes]


def sides(winds, south, north, low, high):
    _, rows, columns = winds.shape
    last = columns // LANES - 1
    shape = jax.ShapeDtypeStruct((4 * (rows + 2 * EDGE) + 10 * EDGE, LANES), f32)
    return pl.pallas_call(
        sides_kernel,
        name="tile_sides",
        grid=(1,),
        in_specs=[
            pl.BlockSpec((4, rows, LANES), lambda i: (0, 0, 0)),
            pl.BlockSpec((4, rows, LANES), lambda i: (0, 0, last)),
            whole(south),
            whole(north),
            whole(low),
            whole(high),
        ],
        out_specs=[whole(shape), whole(shape)],
        out_shape=[shape, shape],
        compiler_params=params(16),
        cost_estimate=pl.CostEstimate(flops=1 << 16, bytes_accessed=2 << 20, transcendentals=0),
    )(winds, winds, south, north, low, high)


def barotropic_kernel(
    mask_ref, depth_ref, begin_ref, stream_ref, low_ref, high_ref, left_ref, right_ref,
    flux_ref, south_ref, north_ref, west_ref, east_ref, height_ref, flow_ref, wide_ref,
):
    rows, columns = begin_ref.shape
    levels = low_ref.shape[0] - 5 * EDGE
    tall = rows + 2 * EDGE
    middle = slice(EDGE, EDGE + rows)

    def merge(low, high):
        lane = lax.broadcasted_iota(i32, low.shape, 1)
        return jnp.where(lane < LANES // 2, high, low)

    for f, ref in enumerate([mask_ref, depth_ref, begin_ref, stream_ref.at[0], stream_ref.at[1]]):
        place = slice(levels + f * EDGE, levels + (f + 1) * EDGE)
        wide_ref[f, 0:EDGE, 0:columns] = low_ref[place, :]
        wide_ref[f, middle, 0:columns] = ref[...].astype(f32)
        wide_ref[f, EDGE + rows : tall, 0:columns] = high_ref[place, :]
        place = slice(f * rows, (f + 1) * rows)
        wide_ref[f, middle, columns : columns + LANES] = merge(left_ref[place, :], right_ref[place, :])
        start = 4 * tall + 2 * EDGE * f
        corner = merge(west_ref[start : start + 2 * EDGE, :], east_ref[start : start + 2 * EDGE, :])
        wide_ref[f, 0:EDGE, columns : columns + LANES] = corner[0:EDGE]
        wide_ref[f, EDGE + rows : tall, columns : columns + LANES] = corner[EDGE : 2 * EDGE]
    for f in range(4):
        wide_ref[5 + f, 0:EDGE, 0:columns] = south_ref[f]
        wide_ref[5 + f, middle, 0:columns] = flux_ref[f]
        wide_ref[5 + f, EDGE + rows : tall, 0:columns] = north_ref[f]
        place = slice(f * tall, (f + 1) * tall)
        wide_ref[5 + f, :, columns : columns + LANES] = merge(west_ref[place, :], east_ref[place, :])
    mask = wide_ref[0]
    drag = -0.5 * wide_ref[1]
    height = wide_ref[2]
    along = wide_ref[3]
    across = wide_ref[4]
    wind_x = 0.5 * wide_ref[5]
    wind_y = 0.5 * wide_ref[6]
    push = 0.5 * wide_ref[7]
    source = wide_ref[8]
    for k in range(SUB):
        level = mask * (height + push)
        along = mask * (0.95 * along + drag * (beside(level, -1, 1) - beside(level, 1, 1)) + wind_x)
        across = mask * (0.95 * across + drag * (beside(level, -1, 0) - beside(level, 1, 0)) + wind_y)
        spread_out = beside(along, -1, 1) - beside(along, 1, 1) + beside(across, -1, 0) - beside(across, 1, 0)
        height = mask * (height - 0.5 * spread_out + source)
    height_ref[...] = height[middle, :columns]
    flow_ref[0] = along[middle, :columns]
    flow_ref[1] = across[middle, :columns]


def barotropic(*arrays):
    rows, columns = arrays[2].shape
    outs = [jax.ShapeDtypeStruct((rows, columns), f32), jax.ShapeDtypeStruct((2, rows, columns), f32)]
    return pl.pallas_call(
        barotropic_kernel,
        name="barotropic",
        grid=(1,),
        in_specs=[whole(array) for array in arrays],
        out_specs=[whole(out) for out in outs],
        out_shape=outs,
        scratch_shapes=[pltpu.VMEM((9, rows + 2 * EDGE, columns + LANES), f32)],
        compiler_params=params(32),
        cost_estimate=pl.CostEstimate(flops=1 << 24, bytes_accessed=6 << 20, transcendentals=0),
    )(*arrays)


def to_next(array, axes):
    ends = lax.axis_size(axes) - 1
    return lax.ppermute(array, axes, [(i, i + 1) for i in range(ends)])


def to_previous(array, axes):
    ends = lax.axis_size(axes) - 1
    return lax.ppermute(array, axes, [(i + 1, i) for i in range(ends)])


def all_to_all(array):
    return lax.all_to_all(array, EVERY, split_axis=0, concat_axis=0, tiled=True)


def local(
    atm_flux,
    margin_source,
    margin_cell,
    margin_weight,
    margin_tile,
    land_mask,
    sea_depth,
    sea_height,
    transport,
    tracers,
):
    tiles = lax.axis_size(EVERY)
    count, levels, rows, columns = tracers.shape
    packed = pack(
        margin_tile.reshape(-1), atm_flux, margin_source, margin_cell, margin_weight, tiles, rows * columns
    )
    packed, land_mask, sea_depth, sea_height, transport, tracers = lax.optimization_barrier(
        (packed, land_mask, sea_depth, sea_height, transport, tracers)
    )
    arrived = all_to_all(packed)

    planes = tracers.reshape(count * levels, rows, columns)
    own_south, own_north, own_west, own_east = edges(planes, land_mask, sea_depth, sea_height, transport)
    from_west = to_next(own_east, "tx")
    from_east = to_previous(own_west, "tx")
    moved = move(land_mask, sea_depth, transport, planes)
    moved = moved.reshape(tracers.shape)
    own_south, own_north, moved = lax.optimization_barrier((own_south, own_north, moved))
    from_south = to_next(own_north, ROWS)
    from_north = to_previous(own_south, ROWS)
    arrived, moved = lax.optimization_barrier((arrived, moved))

    winds, heats, flux_low, flux_high = spread(arrived, rows, columns)
    flux_south = to_next(flux_high, ROWS)
    flux_north = to_previous(flux_low, ROWS)
    margins = (from_west, from_east, own_west, own_east)
    half = solve(heats, land_mask, sea_depth, transport, from_south, own_south, margins, moved, (), 0, 2)
    flux_south, flux_north, half = lax.optimization_barrier((flux_south, flux_north, half))
    side_west, side_east = sides(winds, flux_south, flux_north, from_south, from_north)
    flux_west = to_next(side_east, "tx")
    flux_east = to_previous(side_west, "tx")
    solved = solve(heats, land_mask, sea_depth, transport, from_north, own_north, margins, moved, (half,), 1, 2)
    flux_west, flux_east, solved = lax.optimization_barrier((flux_west, flux_east, solved))
    new_height, new_transport = barotropic(
        land_mask, sea_depth, sea_height, transport, from_south, from_north, from_west, from_east,
        winds, flux_south, flux_north, flux_west, flux_east,
    )
    return new_height, new_transport, solved


def solution(mesh):
    in_specs = (
        P(None, EVERY),
        P(EVERY, None),
        P(EVERY, None),
        P(EVERY, None),
        P(EVERY, None),
        P(ROWS, "tx"),
        P(ROWS, "tx"),
        P(ROWS, "tx"),
        P(None, ROWS, "tx"),
        P(None, None, ROWS, "tx"),
    )
    out_specs = (P(ROWS, "tx"), P(None, ROWS, "tx"), P(None, None, ROWS, "tx"))
    return jax.shard_map(local, mesh=mesh, in_specs=in_specs, out_specs=out_specs, check_vma=False)
```

```python
import functools

import jax
import jax.numpy as jnp
import numpy as np
from jax import lax
from jax.experimental import pallas as pl
from jax.experimental.pallas import tpu as pltpu
from jax.sharding import PartitionSpec as P

SUB = 3
EDGE = 8
LANES = 128
EVERY = ("comp", "ty", "tx")
ROWS = ("comp", "ty")
f32 = jnp.float32
i32 = jnp.int32
VM = pl.BlockSpec(memory_space=pltpu.VMEM)
SM = pl.BlockSpec(memory_space=pltpu.SMEM)


def params(mib):
    return pltpu.CompilerParams(vmem_limit_bytes=mib << 20)


def whole(array):
    return pl.BlockSpec(array.shape, lambda i: (0,) * array.ndim)


def pack_kernel(tile_ref, flux_ref, source_ref, cell_ref, weight_ref, out_ref, count_ref, *, beyond):
    blocks = source_ref.shape[0]
    tiles = out_ref.shape[0]
    group = 4
    nowhere = jnp.full((4, LANES), beyond, f32)

    def clear(t, carry):
        count_ref[t] = 0
        out_ref[t, 8] = nowhere
        return carry

    @pl.when(pl.program_id(0) == 0)
    def _():
        lax.fori_loop(0, tiles, clear, 0, unroll=True)

    begin = pl.program_id(0) * blocks
    sub = lax.broadcasted_iota(i32, (8, LANES), 0)

    def step(i, carry):
        for g in range(group):
            w = i * group + g
            x = flux_ref[:, pl.ds(pl.multiple_of(w * LANES, LANES), LANES)]
            after = pltpu.roll(x, 1, 0)
            six = pltpu.roll(x, 5, 0)
            five = pltpu.roll(x, 6, 0)
            y = jnp.where((sub == 4) | (sub == 5), after, x)
            y = jnp.where(sub == 6, 0.5 * after - 0.3 * x, y)
            y = jnp.where(sub == 3, 0.1 * (six - five), y)
            for half in range(2):
                b = 2 * w + half
                tile = tile_ref[begin + b]
                slot = count_ref[tile]
                count_ref[tile] = slot + 1
                index = jnp.broadcast_to(source_ref[pl.ds(b, 1), :], (8, LANES))
                picked = jnp.take_along_axis(y, index, axis=1)
                value = picked * jnp.broadcast_to(weight_ref[pl.ds(b, 1), :], (8, LANES))
                out_ref[tile, slot] = value[0:4]
                out_ref[tile, 4 + slot] = value[4:8]
                out_ref[tile, 8, pl.ds(slot, 1), :] = cell_ref[pl.ds(b, 1), :].astype(f32)
        return carry

    lax.fori_loop(0, blocks // (2 * group), step, 0)


def pack(tile, flux, source, cell, weight, tiles, beyond):
    blocks = source.shape[0]
    steps = 4 if blocks % 32 == 0 else 1
    line = pl.BlockSpec((blocks // steps, LANES), lambda i: (i, 0))
    return pl.pallas_call(
        functools.partial(pack_kernel, beyond=beyond),
        name="pack_margin",
        grid=(steps,),
        in_specs=[SM, pl.BlockSpec((8, flux.shape[1] // steps), lambda i: (0, i)), line, line, line],
        out_specs=pl.BlockSpec((tiles, 9, 4, LANES), lambda i: (0, 0, 0, 0)),
        out_shape=jax.ShapeDtypeStruct((tiles, 9, 4, LANES), f32),
        scratch_shapes=[pltpu.SMEM((tiles,), i32)],
        compiler_params=params(56),
        cost_estimate=pl.CostEstimate(flops=1 << 22, bytes_accessed=4 << 20, transcendentals=0),
    )(tile, flux, source, cell, weight)


def spread_kernel(cells_ref, load_ref, winds_ref, heats_ref, south_ref, north_ref, acc_ref, turned_ref, *, group):
    _, rows, columns = winds_ref.shape
    fields = 8
    high = columns // LANES
    depth = fields * high
    def clear(i, c):
        acc_ref[pl.ds(pl.multiple_of(i * 256, 256), 256),:] = jnp.zeros((256, LANES), f32)
        return c
    @pl.when(pl.program_id(0) == 0)
    def _():
        lax.fori_loop(0, rows * depth // 256, clear, 0)
        per = 4 * group
        chunk = min(cells_ref.shape[0], LANES // 4)
        for i in range(0, cells_ref.shape[0], chunk):
            cells = cells_ref[i : i + chunk, 0].reshape(4 * chunk, LANES)
            if chunk < LANES // 4:
                cells = jnp.concatenate([cells] * (LANES // (4 * chunk)), axis=0)
            columns_of = (cells.astype(i32) & (LANES - 1)).astype(f32).T
            for n in range(4 * chunk // per):
                part = columns_of if n == 0 else pltpu.roll(columns_of, LANES - n * per, 1)
                turned_ref[i // group + n] = part

    step = pl.program_id(0)
    low_iota = lax.broadcasted_iota(i32, (LANES, LANES), 1).astype(f32).astype(jnp.bfloat16)
    pattern = [
        (2 * i + (lax.broadcasted_iota(i32, (16, LANES), 0) >> 3)).astype(f32).astype(jnp.bfloat16) for i in range(high // 2)
    ]
    zero16 = jnp.zeros((16, LANES), jnp.bfloat16)
    one = jnp.ones((LANES, LANES), jnp.bfloat16)
    zero = jnp.zeros((LANES, LANES), jnp.bfloat16)

    for s in range(group):
        cells = load_ref[s, 8].astype(i32)
        highs = ((cells & (columns - 1)) >> 7).astype(f32)
        for k in range(4):
            value = jnp.concatenate([load_ref[s, k], load_ref[s, 4 + k]], axis=0)
            coarse = value.astype(jnp.bfloat16).astype(f32)
            fine = value - coarse
            coarse = jnp.concatenate([coarse, coarse], axis=0).astype(jnp.bfloat16)
            fine = jnp.concatenate([fine, fine], axis=0).astype(jnp.bfloat16)
            hk = jnp.broadcast_to(highs[k : k + 1], (16, LANES)).astype(jnp.bfloat16)
            c = 4 * s + k
            lk = jnp.broadcast_to(turned_ref[step, :, c : c + 1], (LANES, LANES)).astype(jnp.bfloat16)
            left = []
            right = []
            for p in pattern:
                hit = hk == p
                left.append(jnp.where(hit, coarse, zero16))
                right.append(jnp.where(hit, fine, zero16))
            lhs = jnp.concatenate([jnp.concatenate(left, axis=0), jnp.concatenate(right, axis=0)], axis=1)
            onehot = jnp.where(lk == low_iota, one, zero)
            rhs = jnp.concatenate([onehot, onehot], axis=0)
            both = lax.dot_general(lhs, rhs, (((1,), (0,)), ((), ())), preferred_element_type=f32)
            row = cells[k, 0] >> (columns.bit_length() - 1)
            place = pl.ds(pl.multiple_of(row * depth, depth), depth)
            acc_ref[place, :] += both

    def turn(i, carry):
        r = pl.multiple_of(i * 8, 8)
        block = acc_ref[pl.ds(pl.multiple_of(r * depth, 8 * depth), 8 * depth), :].reshape(8, depth, LANES)
        for h in range(high):
            piece = jnp.swapaxes(block[:, h * 8 : h * 8 + 8, :], 0, 1)
            for f in range(fields):
                ref = winds_ref if f < 4 else heats_ref
                ref[f % 4, pl.ds(r, 8), h * LANES : (h + 1) * LANES] = piece[f]
        return carry

    @pl.when(pl.program_id(0) == pl.num_programs(0) - 1)
    def _():
        lax.fori_loop(0, rows // 8, turn, 0)
        south_ref[...] = winds_ref[:, 0:EDGE, :]
        north_ref[...] = winds_ref[:, rows - EDGE : rows, :]


def spread(load, rows, columns):
    depth = 8 * columns // LANES
    sources = load.shape[0]
    group = 16 if sources % 16 == 0 else 1
    outs = [
        jax.ShapeDtypeStruct((4, rows, columns), f32),
        jax.ShapeDtypeStruct((4, rows, columns), f32),
        jax.ShapeDtypeStruct((4, EDGE, columns), f32),
        jax.ShapeDtypeStruct((4, EDGE, columns), f32),
    ]
    return pl.pallas_call(
        functools.partial(spread_kernel, group=group),
        name="spread_all",
        grid=(sources // group,),
        in_specs=[
            pl.BlockSpec((sources, 1, 4, LANES), lambda i: (0, 8, 0, 0)),
            pl.BlockSpec((group, *load.shape[1:]), lambda i: (i, 0, 0, 0)),
        ],
        out_specs=[whole(out) for out in outs],
        out_shape=outs,
        scratch_shapes=[
            pltpu.VMEM(((rows + 1) * depth, LANES), f32),
            pltpu.VMEM((sources // group, LANES, LANES), f32),
        ],
        compiler_params=params(24),
        cost_estimate=pl.CostEstimate(flops=1 << 30, bytes_accessed=4 << 20, transcendentals=0),
    )(load, load)


def edges_kernel(
    low_ref, high_ref, left_ref, right_ref, mask_ref, depth_ref, height_ref, flow_ref, south_ref, north_ref, west_ref, east_ref
):
    levels = low_ref.shape[0]
    rows, columns = mask_ref.shape
    lane = lax.broadcasted_iota(i32, (rows, LANES), 1)
    lasts = jnp.zeros((rows, LANES), f32)
    firsts = jnp.zeros((rows, LANES), f32)
    for p in range(levels):
        south_ref[p : p + 1, :] = low_ref[p, 0:1, :]
        north_ref[p : p + 1, :] = high_ref[p, EDGE - 1 : EDGE, :]
        firsts = jnp.where(lane == p, left_ref[p, :, 0:1], firsts)
        lasts = jnp.where(lane == p, right_ref[p, :, LANES - 1 : LANES], lasts)
    fields = [mask_ref, depth_ref, height_ref, flow_ref.at[0], flow_ref.at[1]]
    for f, ref in enumerate(fields):
        place = slice(levels + f * EDGE, levels + (f + 1) * EDGE)
        south_ref[place, :] = ref[0:EDGE, :].astype(f32)
        north_ref[place, :] = ref[rows - EDGE : rows, :].astype(f32)
        place = slice(f * rows, (f + 1) * rows)
        west_ref[place, :] = ref[:, 0:LANES].astype(f32)
        east_ref[place, :] = ref[:, columns - LANES : columns].astype(f32)
    west_ref[5 * rows : 6 * rows, :] = firsts
    east_ref[5 * rows : 6 * rows, :] = lasts


def edges(planes, mask, depth, height, flow):
    levels, rows, columns = planes.shape
    last_row = rows // EDGE - 1
    last_lane = columns // LANES - 1
    tall = jax.ShapeDtypeStruct((levels + 5 * EDGE, columns), f32)
    thin = jax.ShapeDtypeStruct((6 * rows, LANES), f32)
    return pl.pallas_call(
        edges_kernel,
        name="tile_edges",
        grid=(1,),
        in_specs=[
            pl.BlockSpec((levels, EDGE, columns), lambda i: (0, 0, 0)),
            pl.BlockSpec((levels, EDGE, columns), lambda i: (0, last_row, 0)),
            pl.BlockSpec((levels, rows, LANES), lambda i: (0, 0, 0)),
            pl.BlockSpec((levels, rows, LANES), lambda i: (0, 0, last_lane)),
            whole(mask),
            whole(depth),
            whole(height),
            whole(flow),
        ],
        out_specs=[whole(tall), whole(tall), whole(thin), whole(thin)],
        out_shape=[tall, tall, thin, thin],
        compiler_params=params(56),
        cost_estimate=pl.CostEstimate(flops=1 << 20, bytes_accessed=6 << 20, transcendentals=0),
    )(planes, planes, planes, planes, mask, depth, height, flow)


def beside(array, amount, axis):
    return pltpu.roll(array, amount % array.shape[axis], axis)


def drift(speed, toward):
    return 0.1 + 0.15 * jnp.maximum(-toward * speed, 0.0)


def move_kernel(mask_ref, depth_ref, flow_ref, planes_ref, out_ref, coef_ref, *, per):
    step = pl.program_id(0)
    rows = planes_ref.shape[1]
    columns = planes_ref.shape[2]

    @pl.when(step == 0)
    def _():
        mask = mask_ref[...].astype(f32)
        lane = lax.broadcasted_iota(i32, (rows, columns), 1)
        sub = lax.broadcasted_iota(i32, (rows, columns), 0)
        u = flow_ref[0] / depth_ref[...]
        v = flow_ref[1] / depth_ref[...]
        east = mask * jnp.where(lane == columns - 1, 0.0, beside(mask, -1, 1)) * drift(u, 1.0)
        west = mask * jnp.where(lane == 0, 0.0, beside(mask, 1, 1)) * drift(u, -1.0)
        north = mask * jnp.where(sub == rows - 1, 0.0, beside(mask, -1, 0)) * drift(v, 1.0)
        south = mask * jnp.where(sub == 0, 0.0, beside(mask, 1, 0)) * drift(v, -1.0)
        coef_ref[0] = 1.0 - (east + west + north + south)
        coef_ref[1] = east
        coef_ref[2] = west
        coef_ref[3] = north
        coef_ref[4] = south

    for n in range(per):
        for r in range(0, rows, 8):
            span = slice(r, r + 8)
            q = planes_ref[n, span, :]
            sub = lax.broadcasted_iota(i32, (8, columns), 0)
            east = beside(q, -1, 1)
            west = beside(q, 1, 1)
            below = planes_ref[n, max(r - 1, 0) : max(r - 1, 0) + 1, :]
            above = planes_ref[n, min(r + 8, rows - 1) : min(r + 8, rows - 1) + 1, :]
            north = jnp.where(sub == 7, above, beside(q, -1, 0))
            south = jnp.where(sub == 0, below, beside(q, 1, 0))
            out_ref[n, span, :] = (
                coef_ref[0, span, :] * q
                + coef_ref[1, span, :] * east
                + coef_ref[2, span, :] * west
                + coef_ref[3, span, :] * north
                + coef_ref[4, span, :] * south
            )


def move(mask, depth, flow, planes):
    levels, rows, columns = planes.shape
    per = 4
    return pl.pallas_call(
        functools.partial(move_kernel, per=per),
        name="tracer_move",
        grid=(levels // per,),
        in_specs=[
            whole(mask),
            whole(depth),
            whole(flow),
            pl.BlockSpec((per, rows, columns), lambda i: (i, 0, 0)),
        ],
        out_specs=pl.BlockSpec((per, rows, columns), lambda i: (i, 0, 0)),
        out_shape=jax.ShapeDtypeStruct(planes.shape, f32),
        scratch_shapes=[pltpu.VMEM((5, rows, columns), f32)],
        compiler_params=params(56),
        cost_estimate=pl.CostEstimate(flops=1 << 25, bytes_accessed=18 << 20, transcendentals=0),
    )(mask, depth, flow, planes)


def solve_kernel(
    flux_ref, mask_ref, depth_ref, flow_ref, near_ref, own_ref, west_ref, east_ref, own_west_ref, own_east_ref, *refs,
    part, parts, absorb, decay,
):
    moved_ref, out_ref, ratio_ref = refs[0], refs[-2], refs[-1]
    step = pl.program_id(0)
    levels = moved_ref.shape[1]
    rows = west_ref.shape[0] // 6
    columns = mask_ref.shape[1]
    start = (part * (rows // EDGE // parts) + step) * EDGE
    lane = lax.broadcasted_iota(i32, (EDGE, LANES), 1)
    sides = (
        (west_ref, own_west_ref, 0, -1.0, slice(0, LANES)),
        (east_ref, own_east_ref, LANES - 1, 1.0, slice(columns - LANES, columns)),
    )
    for beyond_ref, inside_ref, edge, toward, lanes in sides:

        def take(ref, field):
            return ref[pl.ds(pl.multiple_of(field * rows + start, EDGE), EDGE), :]

        there = LANES - 1 - edge
        land = take(inside_ref, 0)[:, edge : edge + 1] * take(beyond_ref, 0)[:, there : there + 1]
        speed = take(inside_ref, 3)[:, edge : edge + 1] / take(inside_ref, 1)[:, edge : edge + 1]
        extra = land * drift(speed, toward) * (take(beyond_ref, 5) - take(inside_ref, 5))
        for tracer in range(2):
            for k in range(levels):
                p = tracer * levels + k
                moved_ref[tracer, k, :, lanes] = moved_ref[tracer, k, :, lanes] + jnp.where(
                    lane == edge, extra[:, p : p + 1], 0.0
                )

    at_edge = step == (0 if part == 0 else pl.num_programs(0) - 1)
    run = functools.partial(
        solve_rows, flux_ref, mask_ref, depth_ref, flow_ref, near_ref, own_ref, moved_ref, out_ref, ratio_ref, absorb, decay
    )
    toward = -1.0 if part == 0 else 1.0

    @pl.when(at_edge)
    def _():
        run(toward)

    @pl.when(jnp.logical_not(at_edge))
    def _():
        run(None)


def solve_rows(
    flux_ref, mask_ref, depth_ref, flow_ref, near_ref, own_ref, moved_ref, out_ref, ratio_ref, absorb, decay, toward
):
    levels = moved_ref.shape[1]
    columns = mask_ref.shape[1]
    planes = 2 * levels
    mask = mask_ref[...].astype(f32)
    if toward is not None:
        row = 0 if toward < 0 else EDGE - 1
        other = planes + (EDGE - 1 if toward < 0 else 0)
        line = slice(row, row + 1)
        coef = mask[line] * near_ref[other : other + 1, :] * drift(flow_ref[0, line, :] / depth_ref[line, :], toward)
        hit = lax.broadcasted_iota(i32, (EDGE, columns), 0) == row

    def moved(tracer, k):
        value = moved_ref[tracer, k]
        if toward is not None:
            p = tracer * levels + k
            extra = coef * (near_ref[p : p + 1, :] - own_ref[p : p + 1, :])
            value = value + jnp.where(hit, extra, 0.0)
        return value

    heat_top = 0.5 * mask * flux_ref[0]
    sun = 0.5 * mask * flux_ref[1]
    salt_top = mask * flux_ref[2]
    stir = flux_ref[3]
    base = 0.2 * mask
    stir = 0.5 * mask * (stir * stir)
    above = jnp.zeros_like(mask)
    link = jnp.zeros_like(mask)
    heat_last = None
    salt_last = None
    for k in range(levels):
        heat = moved(0, k) + absorb[k] * sun
        salt = moved(1, k)
        if k == 0:
            heat = heat + heat_top
            salt = salt + salt_top
        below = base + decay[k] * stir if k < levels - 1 else jnp.zeros_like(mask)
        pivot = 1.0 + below + above
        if k > 0:
            pivot = pivot + above * link
            heat = heat + above * heat_last
            salt = salt + above * salt_last
        inverse = 1.0 / pivot
        link = -below * inverse
        heat_last = heat * inverse
        salt_last = salt * inverse
        above = below
        if k < levels - 1:
            ratio_ref[k] = link
        out_ref[0, k] = heat_last
        out_ref[1, k] = salt_last
    for k in range(levels - 2, -1, -1):
        link = ratio_ref[k]
        heat_last = out_ref[0, k] - link * heat_last
        salt_last = out_ref[1, k] - link * salt_last
        out_ref[0, k] = heat_last
        out_ref[1, k] = salt_last


def solve(flux, mask, depth, flow, near, own, margins, moved, done, part, parts):
    count, levels, rows, columns = moved.shape
    depths = np.arange(levels, dtype=np.float64)
    absorb = tuple(float(a) for a in np.exp(-depths / 3.0) - np.exp(-(depths + 1.0) / 3.0))
    decay = tuple(float(a) for a in np.exp(-depths / 2.0))
    steps = rows // EDGE // parts
    first = part * steps
    line = pl.BlockSpec((EDGE, columns), lambda i: (first + i, 0))
    block = pl.BlockSpec((count, levels, EDGE, columns), lambda i: (0, 0, first + i, 0))
    return pl.pallas_call(
        functools.partial(solve_kernel, part=part, parts=parts, absorb=absorb, decay=decay),
        name=f"column_solve_{part}",
        grid=(steps,),
        in_specs=[
            pl.BlockSpec((4, EDGE, columns), lambda i: (0, first + i, 0)),
            line,
            line,
            pl.BlockSpec((1, EDGE, columns), lambda i: (1, first + i, 0)),
            whole(near),
            whole(own),
            *[whole(margin) for margin in margins],
            block,
            *[pl.BlockSpec(memory_space=pl.ANY) for _ in done],
        ],
        out_specs=block,
        out_shape=jax.ShapeDtypeStruct(moved.shape, f32),
        scratch_shapes=[pltpu.VMEM((levels, EDGE, columns), f32)],
        input_output_aliases={11: 0} if done else {},
        compiler_params=params(24),
        cost_estimate=pl.CostEstimate(flops=1 << 24, bytes_accessed=9 << 20, transcendentals=0),
    )(flux, mask, depth, flow, near, own, *margins, moved, *done)


def sides_kernel(left_ref, right_ref, south_ref, north_ref, low_ref, high_ref, west_ref, east_ref):
    rows = left_ref.shape[1]
    columns = south_ref.shape[2]
    levels = low_ref.shape[0] - 5 * EDGE
    tall = rows + 2 * EDGE
    for ref, part_ref, lanes in (
        (west_ref, left_ref, slice(0, LANES)),
        (east_ref, right_ref, slice(columns - LANES, columns)),
    ):
        for f in range(4):
            start = f * tall
            ref[start : start + EDGE, :] = south_ref[f, :, lanes]
            ref[start + EDGE : start + EDGE + rows, :] = part_ref[f]
            ref[start + EDGE + rows : start + tall, :] = north_ref[f, :, lanes]
        for f in range(5):
            start = 4 * tall + 2 * EDGE * f
            place = slice(levels + f * EDGE, levels + (f + 1) * EDGE)
            ref[start : start + EDGE, :] = low_ref[place, lanes]
            ref[start + EDGE : start + 2 * EDGE, :] = high_ref[place, lanes]


def sides(winds, south, north, low, high):
    _, rows, columns = winds.shape
    last = columns // LANES - 1
    shape = jax.ShapeDtypeStruct((4 * (rows + 2 * EDGE) + 10 * EDGE, LANES), f32)
    return pl.pallas_call(
        sides_kernel,
        name="tile_sides",
        grid=(1,),
        in_specs=[
            pl.BlockSpec((4, rows, LANES), lambda i: (0, 0, 0)),
            pl.BlockSpec((4, rows, LANES), lambda i: (0, 0, last)),
            whole(south),
            whole(north),
            whole(low),
            whole(high),
        ],
        out_specs=[whole(shape), whole(shape)],
        out_shape=[shape, shape],
        compiler_params=params(16),
        cost_estimate=pl.CostEstimate(flops=1 << 16, bytes_accessed=2 << 20, transcendentals=0),
    )(winds, winds, south, north, low, high)


def barotropic_kernel(
    mask_ref, depth_ref, begin_ref, stream_ref, low_ref, high_ref, left_ref, right_ref,
    flux_ref, south_ref, north_ref, west_ref, east_ref, height_ref, flow_ref, wide_ref,
):
    rows, columns = begin_ref.shape
    levels = low_ref.shape[0] - 5 * EDGE
    tall = rows + 2 * EDGE
    middle = slice(EDGE, EDGE + rows)

    def merge(low, high):
        lane = lax.broadcasted_iota(i32, low.shape, 1)
        return jnp.where(lane < LANES // 2, high, low)

    for f, ref in enumerate([mask_ref, depth_ref, begin_ref, stream_ref.at[0], stream_ref.at[1]]):
        place = slice(levels + f * EDGE, levels + (f + 1) * EDGE)
        wide_ref[f, 0:EDGE, 0:columns] = low_ref[place, :]
        wide_ref[f, middle, 0:columns] = ref[...].astype(f32)
        wide_ref[f, EDGE + rows : tall, 0:columns] = high_ref[place, :]
        place = slice(f * rows, (f + 1) * rows)
        wide_ref[f, middle, columns : columns + LANES] = merge(left_ref[place, :], right_ref[place, :])
        start = 4 * tall + 2 * EDGE * f
        corner = merge(west_ref[start : start + 2 * EDGE, :], east_ref[start : start + 2 * EDGE, :])
        wide_ref[f, 0:EDGE, columns : columns + LANES] = corner[0:EDGE]
        wide_ref[f, EDGE + rows : tall, columns : columns + LANES] = corner[EDGE : 2 * EDGE]
    for f in range(4):
        wide_ref[5 + f, 0:EDGE, 0:columns] = south_ref[f]
        wide_ref[5 + f, middle, 0:columns] = flux_ref[f]
        wide_ref[5 + f, EDGE + rows : tall, 0:columns] = north_ref[f]
        place = slice(f * tall, (f + 1) * tall)
        wide_ref[5 + f, :, columns : columns + LANES] = merge(west_ref[place, :], east_ref[place, :])
    mask = wide_ref[0]
    drag = -0.5 * wide_ref[1]
    height = wide_ref[2]
    along = wide_ref[3]
    across = wide_ref[4]
    wind_x = 0.5 * wide_ref[5]
    wind_y = 0.5 * wide_ref[6]
    push = 0.5 * wide_ref[7]
    source = wide_ref[8]
    for k in range(SUB):
        level = mask * (height + push)
        along = mask * (0.95 * along + drag * (beside(level, -1, 1) - beside(level, 1, 1)) + wind_x)
        across = mask * (0.95 * across + drag * (beside(level, -1, 0) - beside(level, 1, 0)) + wind_y)
        spread_out = beside(along, -1, 1) - beside(along, 1, 1) + beside(across, -1, 0) - beside(across, 1, 0)
        height = mask * (height - 0.5 * spread_out + source)
    height_ref[...] = height[middle, :columns]
    flow_ref[0] = along[middle, :columns]
    flow_ref[1] = across[middle, :columns]


def barotropic(*arrays):
    rows, columns = arrays[2].shape
    outs = [jax.ShapeDtypeStruct((rows, columns), f32), jax.ShapeDtypeStruct((2, rows, columns), f32)]
    return pl.pallas_call(
        barotropic_kernel,
        name="barotropic",
        grid=(1,),
        in_specs=[whole(array) for array in arrays],
        out_specs=[whole(out) for out in outs],
        out_shape=outs,
        scratch_shapes=[pltpu.VMEM((9, rows + 2 * EDGE, columns + LANES), f32)],
        compiler_params=params(32),
        cost_estimate=pl.CostEstimate(flops=1 << 24, bytes_accessed=6 << 20, transcendentals=0),
    )(*arrays)


def to_next(array, axes):
    ends = lax.axis_size(axes) - 1
    return lax.ppermute(array, axes, [(i, i + 1) for i in range(ends)])


def to_previous(array, axes):
    ends = lax.axis_size(axes) - 1
    return lax.ppermute(array, axes, [(i + 1, i) for i in range(ends)])


def all_to_all(array):
    return lax.all_to_all(array, EVERY, split_axis=0, concat_axis=0, tiled=True)


def local(
    atm_flux,
    margin_source,
    margin_cell,
    margin_weight,
    margin_tile,
    land_mask,
    sea_depth,
    sea_height,
    transport,
    tracers,
):
    tiles = lax.axis_size(EVERY)
    count, levels, rows, columns = tracers.shape
    packed = pack(
        margin_tile.reshape(-1), atm_flux, margin_source, margin_cell, margin_weight, tiles, rows * columns
    )
    packed, land_mask, sea_depth, sea_height, transport, tracers = lax.optimization_barrier(
        (packed, land_mask, sea_depth, sea_height, transport, tracers)
    )
    arrived = all_to_all(packed)

    planes = tracers.reshape(count * levels, rows, columns)
    own_south, own_north, own_west, own_east = edges(planes, land_mask, sea_depth, sea_height, transport)
    from_west = to_next(own_east, "tx")
    from_east = to_previous(own_west, "tx")
    moved = move(land_mask, sea_depth, transport, planes)
    moved = moved.reshape(tracers.shape)
    own_south, own_north, moved = lax.optimization_barrier((own_south, own_north, moved))
    from_south = to_next(own_north, ROWS)
    from_north = to_previous(own_south, ROWS)
    arrived, moved = lax.optimization_barrier((arrived, moved))

    winds, heats, flux_low, flux_high = spread(arrived, rows, columns)
    flux_south = to_next(flux_high, ROWS)
    flux_north = to_previous(flux_low, ROWS)
    margins = (from_west, from_east, own_west, own_east)
    half = solve(heats, land_mask, sea_depth, transport, from_south, own_south, margins, moved, (), 0, 2)
    flux_south, flux_north, half = lax.optimization_barrier((flux_south, flux_north, half))
    side_west, side_east = sides(winds, flux_south, flux_north, from_south, from_north)
    flux_west = to_next(side_east, "tx")
    flux_east = to_previous(side_west, "tx")
    solved = solve(heats, land_mask, sea_depth, transport, from_north, own_north, margins, moved, (half,), 1, 2)
    flux_west, flux_east, solved = lax.optimization_barrier((flux_west, flux_east, solved))
    new_height, new_transport = barotropic(
        land_mask, sea_depth, sea_height, transport, from_south, from_north, from_west, from_east,
        winds, flux_south, flux_north, flux_west, flux_east,
    )
    return new_height, new_transport, solved


def solution(mesh):
    in_specs = (
        P(None, EVERY),
        P(EVERY, None),
        P(EVERY, None),
        P(EVERY, None),
        P(EVERY, None),
        P(ROWS, "tx"),
        P(ROWS, "tx"),
        P(ROWS, "tx"),
        P(None, ROWS, "tx"),
        P(None, None, ROWS, "tx"),
    )
    out_specs = (P(ROWS, "tx"), P(None, ROWS, "tx"), P(None, None, ROWS, "tx"))
    return jax.shard_map(local, mesh=mesh, in_specs=in_specs, out_specs=out_specs, check_vma=False)
```
